32 devices in a mesh: replica: 4 (over y, x), shard: 8 (over z, core).
Axes of the slice: x: 2, y: 2, z: 4, core: 2. Of those that a mesh axis runs over, the one named last changes fastest.
Arguments:
- hidden_in: bfloat16 [4096, 2048], P(('replica', 'shard')), may hold values from -6 to 6
- segment_ids: int32 [4096], P(('replica', 'shard')), may hold values from 0 to 4095, as said below
- routes: int32 [4096, 6], P(('replica', 'shard')), may hold values from 0 to 63, all different within a row; in each aligned block of 128 rows (0 to 127, 128 to 255, ...) at most 16 rows name the same one
- norm_gain: bfloat16 [2048], P('shard'), may hold values from 0.5 to 1.5
- query_weight: bfloat16 [2048, 3072], P('shard'), may hold values from -0.125 to 0.125
- kv_down: bfloat16 [2048, 576], P('shard'), may hold values from -0.125 to 0.125
- kv_gain: bfloat16 [512], P('shard'), may hold values from 0.5 to 1.5
- kv_up: bfloat16 [512, 4096], P(None, 'shard'), may hold values from -0.25 to 0.25
- out_weight: bfloat16 [2048, 2048], P('shard'), may hold values from -0.5 to 0.5
- mixer_gain: bfloat16 [2048], P('shard'), may hold values from 0.5 to 1.5
- router_weight: bfloat16 [2048, 64], P('shard'), may hold values from -0.375 to 0.375
- shared_gate: bfloat16 [2048, 2816], P('shard'), may hold values from -0.125 to 0.125
- shared_up: bfloat16 [2048, 2816], P('shard'), may hold values from -0.125 to 0.125
- shared_down: bfloat16 [2816, 2048], P(None, 'shard'), may hold values from -0.109375 to 0.109375
- expert_gate: bfloat16 [1, 2048, 1408], P(None, 'shard'), may hold values from -0.125 to 0.125
- expert_up: bfloat16 [1, 2048, 1408], P(None, 'shard'), may hold values from -0.125 to 0.125
- expert_down: bfloat16 [1, 1408, 2048], P(None, None, 'shard'), may hold values from -2.5 to 2.5
- cotangent: bfloat16 [4096, 2048], P(('replica', 'shard')), may hold values from -6 to 6
Outputs:
- output: bfloat16 [4096, 2048], P(('replica', 'shard'))
- grad_input: float32 [4096, 2048], P(('replica', 'shard'))
- grad_norm_gain: float32 [2048], P('shard')
- grad_query: float32 [2048, 3072], P('shard')
- grad_kv_down: float32 [2048, 576], P('shard')
- grad_kv_gain: float32 [512], P('shard')
- grad_kv_up: float32 [512, 4096], P(None, 'shard')
- grad_out_weight: float32 [2048, 2048], P('shard')
- grad_mixer_gain: float32 [2048], P('shard')
- grad_router: float32 [2048, 64], P('shard')
- grad_shared_gate: float32 [2048, 2816], P('shard')
- grad_shared_up: float32 [2048, 2816], P('shard')
- grad_shared_down: float32 [2816, 2048], P(None, 'shard')
- grad_expert_gate: float32 [1, 2048, 1408], P(None, 'shard')
- grad_expert_up: float32 [1, 2048, 1408], P(None, 'shard')
- grad_expert_down: float32 [1, 1408, 2048], P(None, None, 'shard')
The draws below stay inside these ranges and needn't reach their ends.
Inputs may be any that keep to these rules, and one draw needn't show every extreme that they name: `segment_ids`: segment numbers never fall, and every segment lies within one aligned block of 128 rows. `routes`: each row names 6 different experts; within the 128 rows of one device no expert is named by more than 16 rows.
All inputs are finite; a program needn't handle non-finite values.
Results may differ from the reference program's by a relative error of at most 0.034.
Values may be sent and summed in bfloat16 or wider, within the bound.
No kernel may reach another device: no remote copies, remote signals or barrier semaphores. Data moves between devices by JAX's collectives and lax.ppermute only.
A program may use at most 320 MiB of HBM per device.

```python
import math
import jax
import jax.numpy as jnp
import numpy as np
from jax import lax

D = 2048
H = 16
DN = 128
DR = 64
DV = 128
KVR = 512
NE = 64
TOPK = 6
FF = 1408
SH = 2816
EW = 1
TOK_DEV = 128
CAP = 16
TOKENS = 4096


def draw_segment_ids(key, part):
    block_count = TOKENS // TOK_DEV
    level_key, roll_key = jax.random.split(jax.random.fold_in(key, 17))
    level = jax.random.randint(level_key, (block_count, 1), 0, 4)
    threshold = jnp.where(level == 0, 0, jnp.where(level == 1, 1, jnp.where(level == 2, 8, 32)))
    rolled = jax.random.randint(roll_key, (block_count, TOK_DEV), 0, 256)
    column = jnp.arange(TOK_DEV, dtype=jnp.int32)[None, :]
    cut_flag = jnp.where((rolled < threshold) & (column > 0), 1, 0).astype(jnp.int32)
    local_ids = jnp.cumsum(cut_flag, axis=1)
    block_base = jnp.arange(block_count, dtype=jnp.int32)[:, None] * TOK_DEV
    return (local_ids + block_base).reshape(TOKENS).astype(jnp.int32)


def block_levels(own_key, shape, cuts, least, largest):
    loudness = 1.0
    for dim, blocks in cuts:
        steps = jax.random.uniform(jax.random.fold_in(jax.random.fold_in(own_key, 6), dim), (blocks,), jnp.float32, least / len(cuts), largest / len(cuts))
        loudness = loudness * jnp.repeat(jnp.exp(steps), shape[dim] // blocks).reshape((-1,) + (1,) * (len(shape) - 1 - dim))
    return loudness


def deal_out(stream_key, own, number, rows, count, top, reach, slope):
    sequence = jax.random.permutation(stream_key, count)
    heavy_load, common = load_shares(count, rows * top, reach, slope, True), load_shares(count, rows * top, reach, slope, False)
    places = jnp.arange(count)

    def named(tallies, offset_by):
        used = int((tallies > 0).sum())
        fixed = max(1, used // 4)
        passed = fixed + (places - fixed + offset_by * (used - fixed)) % max(1, count - fixed)
        return jnp.zeros((count,), jnp.int32).at[sequence[jnp.where(places < fixed, places, passed)]].set(jnp.asarray(tallies, jnp.int32))

    tallies = jnp.where(number % 4 == 0, named(heavy_load, number // 4), named(common, number - number // 4 - 1))
    mixed = jax.random.permutation(jax.random.fold_in(own, 3), count)
    source_of, sink = mixed[0:count // 2 * 2:2], mixed[1:count // 2 * 2:2]
    margin = jnp.minimum(tallies[source_of] - 1, reach - tallies[sink]) // 2
    margin = jnp.where((source_of == sequence[0]) | (sink == sequence[0]) | (tallies[sink] == 0), 0, jnp.maximum(margin, 0))
    passed = jax.random.randint(jax.random.fold_in(own, 4), (count // 2,), 0, 1 << 20) % (margin + 1)
    tallies = tallies.at[source_of].add(-passed).at[sink].add(passed)
    labels = jnp.searchsorted(jnp.cumsum(tallies), jnp.arange(rows * top), side="right").astype(jnp.int32)
    table = labels.reshape(top, rows).T
    table = table[jax.random.permutation(jax.random.fold_in(own, 1), rows)]
    offset_by = jax.random.randint(jax.random.fold_in(own, 2), (rows, 1), 0, top)
    return jnp.take_along_axis(table, (jnp.arange(top)[None, :] + offset_by) % top, axis=1)


def load_shares(amount, total, most, lean, full):
    portions = [(1 << 20) // math.isqrt(rank ** lean) + 1 for rank in range(1, amount + 1)]
    largest = most if full else min(most, max(-(-total // amount), total * portions[0] // sum(portions)))
    least = 1 if total - largest >= amount - 1 else 0
    given, rest = [largest] + [least] * (amount - 1), total - largest - least * (amount - 1)
    while rest > 0:
        movable = [i for i in range(1, amount) if given[i] < largest] or [i for i in range(1, amount) if given[i] < most]
        pool, left = sum([portions[i] for i in movable]), rest
        for i in movable:
            extra = min(most - given[i], max(1, left * portions[i] // pool), rest)
            given[i] = given[i] + extra
            rest = rest - extra
    return np.array(given)


def noise(key, dims, deviation, reach, shards=(), kind=jnp.bfloat16):
    entries = deviation * jax.random.normal(key, dims, jnp.float32)
    if shards:
        entries = entries * block_levels(key, dims, shards, -0.22, 0.18)
    return jnp.clip(entries, -reach, reach).astype(kind)


def setup_inputs(seed: int = 0) -> dict:
    key_list = jax.random.split(jax.random.key(seed), 19)
    hidden_in = noise(key_list[0], (TOKENS, D), 1.0, 6.0, ((0, 32),))
    segment_ids = draw_segment_ids(jax.random.fold_in(key_list[18], 71), 0)
    routes_keys = jax.random.split(jax.random.fold_in(key_list[2], 1), TOKENS // TOK_DEV)
    routes_turns = jax.random.permutation(jax.random.fold_in(key_list[2], 3), TOKENS // TOK_DEV)
    routes = jax.vmap(lambda own, number: deal_out(jax.random.fold_in(key_list[2], 2), own, number, TOK_DEV, NE, TOPK, CAP, 0))(routes_keys, routes_turns).reshape((TOKENS, TOPK))
    norm_gain = jnp.clip(1.0 + 0.1 * jax.random.normal(key_list[3], (D,), jnp.float32), 0.5, 1.5).astype(jnp.bfloat16)
    query_weight = noise(key_list[4], (D, H * (DN + DR)), D ** -0.5, 0.125, ((0, 8),))
    kv_down = noise(key_list[5], (D, KVR + DR), D ** -0.5, 0.125, ((0, 8),))
    kv_gain = jnp.clip(1.0 + 0.1 * jax.random.normal(key_list[6], (KVR,), jnp.float32), 0.5, 1.5).astype(jnp.bfloat16)
    kv_up = noise(key_list[7], (KVR, H * (DN + DV)), KVR ** -0.5, 0.25, ((1, 8),))
    out_weight = noise(key_list[8], (H * DV, D), (H * DV // 16) ** -0.5, 0.5, ((0, 8),))
    mixer_gain = jnp.clip(1.0 + 0.1 * jax.random.normal(key_list[9], (D,), jnp.float32), 0.5, 1.5).astype(jnp.bfloat16)
    router_weight = noise(key_list[10], (D, NE), (D // 9) ** -0.5, 0.375, ((0, 8),))
    shared_gate = noise(key_list[11], (D, SH), D ** -0.5, 0.125, ((0, 8),))
    shared_up = noise(key_list[12], (D, SH), D ** -0.5, 0.125, ((0, 8),))
    shared_down = noise(key_list[13], (SH, D), SH ** -0.5, 0.109375, ((1, 8),))
    expert_gate = noise(key_list[14], (EW, D, FF), D ** -0.5, 0.125, ((1, 8),))
    expert_up = noise(key_list[15], (EW, D, FF), D ** -0.5, 0.125, ((1, 8),))
    expert_down = noise(key_list[16], (EW, FF, D), (max(FF // 256, 1)) ** -0.5, 2.5, ((2, 8),))
    cotangent = noise(key_list[17], (TOKENS, D), 1.0, 6.0, ((0, 32),))
    return {"hidden_in": hidden_in, "segment_ids": segment_ids, "routes": routes, "norm_gain": norm_gain, "query_weight": query_weight, "kv_down": kv_down, "kv_gain": kv_gain, "kv_up": kv_up, "out_weight": out_weight, "mixer_gain": mixer_gain, "router_weight": router_weight, "shared_gate": shared_gate, "shared_up": shared_up, "shared_down": shared_down, "expert_gate": expert_gate, "expert_up": expert_up, "expert_down": expert_down, "cotangent": cotangent}


EPSILON = 1e-06
NEGATIVE = -1e+30

def inv_rms(values):
    return lax.rsqrt(lax.optimization_barrier(jnp.mean(values * values, axis=-1, keepdims=True)) + EPSILON)

def mixed_einsum(form, left, right):
    return jnp.einsum(form, left.astype(jnp.float32), right.astype(jnp.float32), precision=lax.Precision.HIGHEST)

def rope_tables(seg_block):
    count = seg_block.shape[0]
    index = jnp.arange(count, dtype=jnp.int32)
    same_seg = seg_block[:, None] == seg_block[None, :]
    start = lax.optimization_barrier(jnp.min(jnp.where(same_seg, index[None, :], count), axis=1)).astype(jnp.int32)
    position = (index - start).astype(jnp.float32)
    half_rope = DR // 2
    freq_table = 10000.0 ** (-jnp.arange(half_rope, dtype=jnp.float32) / half_rope)
    angles = position[:, None] * freq_table[None, :]
    allowed = same_seg & (index[None, :] <= index[:, None])
    return (jnp.cos(angles), jnp.sin(angles), allowed)

def rotate(values, cosine, sine):
    half_rope = values.shape[-1] // 2
    first_half = values[..., :half_rope]
    second_half = values[..., half_rope:]
    return jnp.concatenate([first_half * cosine - second_half * sine, second_half * cosine + first_half * sine], axis=-1)

def unrotate(grads, cosine, sine):
    half_rope = grads.shape[-1] // 2
    first_half = grads[..., :half_rope]
    second_half = grads[..., half_rope:]
    return jnp.concatenate([first_half * cosine + second_half * sine, second_half * cosine - first_half * sine], axis=-1)

def silu_parts(pre_act):
    sigmoid_val = jax.nn.sigmoid(pre_act)
    return (pre_act * sigmoid_val, sigmoid_val * (1.0 + pre_act * (1.0 - sigmoid_val)))

def attention_forward(x_float, seg_block, attn_weights):
    norm_gain, query_weight, kv_down, kv_gain, kv_up, out_weight = attn_weights
    count = x_float.shape[0]
    scale_one = inv_rms(x_float)
    normed_one = (x_float * scale_one * norm_gain.astype(jnp.float32)).astype(jnp.bfloat16)
    query_all = jnp.dot(normed_one, query_weight, preferred_element_type=jnp.float32).reshape(count, H, DN + DR)
    latent_all = jnp.dot(normed_one, kv_down, preferred_element_type=jnp.float32)
    latent = latent_all[:, :KVR]
    key_rope = latent_all[:, KVR:]
    scale_kv = inv_rms(latent)
    latent_normed = (latent * scale_kv * kv_gain.astype(jnp.float32)).astype(jnp.bfloat16)
    kv_heads = jnp.dot(latent_normed, kv_up, preferred_element_type=jnp.float32).reshape(count, H, DN + DV)
    cosine, sine, allowed = rope_tables(seg_block)
    query_rot = rotate(query_all[..., DN:], cosine[:, None, :], sine[:, None, :])
    key_rot = rotate(key_rope, cosine, sine)
    score_scale = (DN + DR) ** (-0.5)
    query_b = (jnp.concatenate([query_all[..., :DN], query_rot], axis=-1) * score_scale).astype(jnp.bfloat16)
    key_b = jnp.concatenate([kv_heads[..., :DN], jnp.broadcast_to(key_rot[:, None, :], (count, H, DR))], axis=-1).astype(jnp.bfloat16)
    value_b = kv_heads[..., DN:].astype(jnp.bfloat16)
    scores = mixed_einsum('thd,shd->hts', query_b, key_b)
    scores = jnp.where(allowed[None], scores, NEGATIVE)
    top_score = lax.optimization_barrier(jnp.max(scores, axis=-1, keepdims=True))
    expd = jnp.exp(scores - top_score)
    row_total = lax.optimization_barrier(jnp.sum(expd, axis=-1, keepdims=True))
    log_sum = top_score + jnp.log(row_total)
    weights_b = (expd / row_total).astype(jnp.bfloat16)
    attended = mixed_einsum('hts,shd->thd', weights_b, value_b).astype(jnp.bfloat16).reshape(count, H * DV)
    hidden = x_float + jnp.dot(attended, out_weight, preferred_element_type=jnp.float32)
    saved = (normed_one, latent, scale_kv, latent_normed, cosine, sine, allowed, query_b, key_b, value_b, log_sum, attended)
    return (hidden, saved)

def moe_forward(hidden, route_block, moe_weights):
    mixer_gain, router_weight, shared_gate, shared_up, shared_down, expert_gate, expert_up, expert_down = moe_weights
    scale_two = inv_rms(hidden)
    normed_two = (hidden * scale_two * mixer_gain.astype(jnp.float32)).astype(jnp.bfloat16)
    logits = jnp.dot(normed_two, router_weight, preferred_element_type=jnp.float32)
    router_probs = jax.nn.softmax(logits, axis=-1)
    selected = jnp.any(route_block[:, :, None] == jnp.arange(EW, dtype=jnp.int32)[None, None, :], axis=1).astype(jnp.float32)
    combine = router_probs[:, :EW] * selected
    shared_gpre = jnp.dot(normed_two, shared_gate, preferred_element_type=jnp.float32)
    shared_upre = jnp.dot(normed_two, shared_up, preferred_element_type=jnp.float32)
    shared_hidden = (silu_parts(shared_gpre)[0] * shared_upre).astype(jnp.bfloat16)
    shared_out = jnp.dot(shared_hidden, shared_down, preferred_element_type=jnp.float32)
    expert_gpre = mixed_einsum('td,edf->etf', normed_two, expert_gate)
    expert_upre = mixed_einsum('td,edf->etf', normed_two, expert_up)
    expert_hidden = (silu_parts(expert_gpre)[0] * expert_upre).astype(jnp.bfloat16)
    expert_out = mixed_einsum('etf,efd->etd', expert_hidden, expert_down)
    total = hidden + shared_out + lax.optimization_barrier(jnp.sum(combine.T[:, :, None] * expert_out, axis=0))
    saved = (normed_two, scale_two, router_probs, selected, combine, shared_gpre, shared_upre, shared_hidden, expert_gpre, expert_upre, expert_hidden, expert_out)
    return (total.astype(jnp.bfloat16), saved)

def moe_backward(grad_out, hidden, saved, moe_weights):
    mixer_gain, router_weight, shared_gate, shared_up, shared_down, expert_gate, expert_up, expert_down = moe_weights
    normed_two, scale_two, router_probs, selected, combine, shared_gpre, shared_upre, shared_hidden, expert_gpre, expert_upre, expert_hidden, expert_out = saved
    count = hidden.shape[0]
    grad_float = grad_out.astype(jnp.float32)
    grad_combine = lax.optimization_barrier(jnp.sum(grad_float[None] * expert_out, axis=-1)).T
    grad_probs = jnp.concatenate([grad_combine * selected, jnp.zeros((count, NE - EW), jnp.float32)], axis=-1)
    grad_logits = router_probs * (grad_probs - lax.optimization_barrier(jnp.sum(router_probs * grad_probs, axis=-1, keepdims=True)))
    logit_b = grad_logits.astype(jnp.bfloat16)
    grad_router = jnp.dot(normed_two.T, logit_b, preferred_element_type=jnp.float32)
    grad_normed = jnp.dot(logit_b, router_weight.T, preferred_element_type=jnp.float32)
    grad_shared_down = jnp.dot(shared_hidden.T, grad_out, preferred_element_type=jnp.float32)
    grad_sh = jnp.dot(grad_out, shared_down.T, preferred_element_type=jnp.float32)
    shared_act, shared_slope = silu_parts(shared_gpre)
    grad_sg = (grad_sh * shared_upre * shared_slope).astype(jnp.bfloat16)
    grad_su = (grad_sh * shared_act).astype(jnp.bfloat16)
    grad_shared_gate = jnp.dot(normed_two.T, grad_sg, preferred_element_type=jnp.float32)
    grad_shared_up = jnp.dot(normed_two.T, grad_su, preferred_element_type=jnp.float32)
    grad_normed = grad_normed + jnp.dot(grad_sg, shared_gate.T, preferred_element_type=jnp.float32)
    grad_normed = grad_normed + jnp.dot(grad_su, shared_up.T, preferred_element_type=jnp.float32)
    grad_eo = (combine.T[:, :, None] * grad_float[None]).astype(jnp.bfloat16)
    grad_expert_down = mixed_einsum('etf,etd->efd', expert_hidden, grad_eo)
    grad_eh = mixed_einsum('etd,efd->etf', grad_eo, expert_down)
    expert_act, expert_slope = silu_parts(expert_gpre)
    grad_eg = (grad_eh * expert_upre * expert_slope).astype(jnp.bfloat16)
    grad_eu = (grad_eh * expert_act).astype(jnp.bfloat16)
    grad_expert_gate = mixed_einsum('td,etf->edf', normed_two, grad_eg)
    grad_expert_up = mixed_einsum('td,etf->edf', normed_two, grad_eu)
    grad_normed = grad_normed + mixed_einsum('etf,edf->td', grad_eg, expert_gate)
    grad_normed = grad_normed + mixed_einsum('etf,edf->td', grad_eu, expert_up)
    grad_mixer_gain = lax.optimization_barrier(jnp.sum(grad_normed * hidden * scale_two, axis=0))
    scaled = grad_normed * mixer_gain.astype(jnp.float32)
    grad_hidden = grad_float + scale_two * scaled - hidden * scale_two ** 3 * lax.optimization_barrier(jnp.mean(scaled * hidden, axis=-1, keepdims=True))
    return (grad_hidden, (grad_mixer_gain, grad_router, grad_shared_gate, grad_shared_up, grad_shared_down, grad_expert_gate, grad_expert_up, grad_expert_down))

def attention_backward(grad_hidden, x_float, saved, attn_weights):
    norm_gain, query_weight, kv_down, kv_gain, kv_up, out_weight = attn_weights
    normed_one, latent, scale_kv, latent_normed, cosine, sine, allowed, query_b, key_b, value_b, log_sum, attended = saved
    count = x_float.shape[0]
    grad_hb = grad_hidden.astype(jnp.bfloat16)
    grad_out_weight = jnp.dot(attended.T, grad_hb, preferred_element_type=jnp.float32)
    grad_att = jnp.dot(grad_hb, out_weight.T, preferred_element_type=jnp.float32).astype(jnp.bfloat16).reshape(count, H, DV)
    scores = mixed_einsum('thd,shd->hts', query_b, key_b)
    scores = jnp.where(allowed[None], scores, NEGATIVE)
    probs_f = jnp.exp(scores - log_sum)
    probs_b = probs_f.astype(jnp.bfloat16)
    grad_values = mixed_einsum('hts,thd->shd', probs_b, grad_att)
    grad_probs = mixed_einsum('thd,shd->hts', grad_att, value_b)
    delta = lax.optimization_barrier(jnp.sum(grad_att.astype(jnp.float32) * attended.astype(jnp.float32).reshape(count, H, DV), axis=-1)).T
    grad_scores = (probs_f * (grad_probs - delta[:, :, None])).astype(jnp.bfloat16)
    grad_q = mixed_einsum('hts,shd->thd', grad_scores, key_b) * (DN + DR) ** (-0.5)
    grad_k = mixed_einsum('hts,thd->shd', grad_scores, query_b)
    grad_qrot = unrotate(grad_q[..., DN:], cosine[:, None, :], sine[:, None, :])
    grad_qb = jnp.concatenate([grad_q[..., :DN], grad_qrot], axis=-1).reshape(count, H * (DN + DR)).astype(jnp.bfloat16)
    grad_query = jnp.dot(normed_one.T, grad_qb, preferred_element_type=jnp.float32)
    grad_normed = jnp.dot(grad_qb, query_weight.T, preferred_element_type=jnp.float32)
    grad_krope = unrotate(lax.optimization_barrier(jnp.sum(grad_k[..., DN:], axis=1)), cosine, sine)
    grad_kvb = jnp.concatenate([grad_k[..., :DN], grad_values], axis=-1).reshape(count, H * (DN + DV)).astype(jnp.bfloat16)
    grad_kv_up = jnp.dot(latent_normed.T, grad_kvb, preferred_element_type=jnp.float32)
    grad_latent_normed = jnp.dot(grad_kvb, kv_up.T, preferred_element_type=jnp.float32)
    grad_kv_gain = lax.optimization_barrier(jnp.sum(grad_latent_normed * latent * scale_kv, axis=0))
    latent_scaled = grad_latent_normed * kv_gain.astype(jnp.float32)
    grad_latent = scale_kv * latent_scaled - latent * scale_kv ** 3 * lax.optimization_barrier(jnp.mean(latent_scaled * latent, axis=-1, keepdims=True))
    grad_downb = jnp.concatenate([grad_latent, grad_krope], axis=-1).astype(jnp.bfloat16)
    grad_kv_down = jnp.dot(normed_one.T, grad_downb, preferred_element_type=jnp.float32)
    grad_normed = grad_normed + jnp.dot(grad_downb, kv_down.T, preferred_element_type=jnp.float32)
    scale_one = inv_rms(x_float)
    grad_norm_gain = lax.optimization_barrier(jnp.sum(grad_normed * x_float * scale_one, axis=0))
    input_scaled = grad_normed * norm_gain.astype(jnp.float32)
    grad_input = grad_hidden + scale_one * input_scaled - x_float * scale_one ** 3 * lax.optimization_barrier(jnp.mean(input_scaled * x_float, axis=-1, keepdims=True))
    return (grad_input, (grad_norm_gain, grad_query, grad_kv_down, grad_kv_gain, grad_kv_up, grad_out_weight))

def reference(hidden_in, segment_ids, routes, norm_gain, query_weight, kv_down, kv_gain, kv_up, out_weight, mixer_gain, router_weight, shared_gate, shared_up, shared_down, expert_gate, expert_up, expert_down, cotangent):
    attn_weights = (norm_gain, query_weight, kv_down, kv_gain, kv_up, out_weight)
    moe_weights = (mixer_gain, router_weight, shared_gate, shared_up, shared_down, expert_gate, expert_up, expert_down)
    blocks = hidden_in.shape[0] // TOK_DEV

    def one_block(carry, inputs):
        x_block, seg_block, route_block, grad_block = inputs
        x_float = x_block.astype(jnp.float32)
        hidden, attn_saved = attention_forward(x_float, seg_block, attn_weights)
        result, moe_saved = moe_forward(hidden, route_block, moe_weights)
        grad_hidden, moe_partials = moe_backward(grad_block, hidden, moe_saved, moe_weights)
        grad_input, attn_partials = attention_backward(grad_hidden, x_float, attn_saved, attn_weights)
        partials = attn_partials + moe_partials
        new_carry = tuple((total + lax.optimization_barrier(part.astype(jnp.bfloat16)).astype(jnp.float32) for total, part in zip(carry, partials)))
        return (new_carry, (result, grad_input))
    init = tuple((jnp.zeros(weight.shape, jnp.float32) for weight in attn_weights + moe_weights))
    inputs = (hidden_in.reshape(blocks, TOK_DEV, D), segment_ids.reshape(blocks, TOK_DEV), routes.reshape(blocks, TOK_DEV, TOPK), cotangent.reshape(blocks, TOK_DEV, D))
    totals, (results, grads_in) = lax.scan(one_block, init, inputs)
    return (results.reshape(blocks * TOK_DEV, D), grads_in.reshape(blocks * TOK_DEV, D), totals[0], totals[1], totals[2], totals[3], totals[4], totals[5], totals[6], totals[7], totals[8], totals[9], totals[10], totals[11], totals[12], totals[13])
```

```python
import jax
import jax.numpy as jnp
from jax import lax
from jax.experimental import pallas as pl
from jax.experimental.layout import Layout, with_layout_constraint
from jax.experimental.pallas import tpu as pltpu
from jax.sharding import PartitionSpec as P

D = 2048
H = 16
DN = 128
DR = 64
DV = 128
KVR = 512
NE = 64
CAP = 16
FF = 1408
SH = 2816
TOK = 128

EPSILON = 1e-06
NEGATIVE = -1e30
BF = jnp.bfloat16
F32 = jnp.float32
SCALE = (DN + DR) ** (-0.5)


def dot(left, right):
    return jnp.dot(left, right, preferred_element_type=F32)


def dot_t(left, right):
    return lax.dot_general(left, right, (((1,), (1,)), ((), ())), preferred_element_type=F32)


def t_dot(left, right):
    return lax.dot_general(left, right, (((0,), (0,)), ((), ())), preferred_element_type=F32)


def ein(form, left, right):
    return jnp.einsum(form, left, right, preferred_element_type=F32)


def inv_rms(values):
    return lax.rsqrt(jnp.mean(values * values, axis=-1, keepdims=True) + EPSILON)


def silu_parts(pre_act):
    sigmoid_val = jax.nn.sigmoid(pre_act)
    return (pre_act * sigmoid_val, sigmoid_val * (1.0 + pre_act * (1.0 - sigmoid_val)))


def by_rows(values):
    return with_layout_constraint(values, Layout(major_to_minor=(0, 1)))


def fold(values, rows):
    n, c = values.shape
    f = rows // n
    if f <= 1:
        return values
    return values.reshape(n, f, c // f).transpose(1, 0, 2).reshape(rows, c // f)


def unfold(values, rows):
    n, c = values.shape
    f = n // rows
    if f <= 1:
        return values
    return values.reshape(f, rows, c).transpose(1, 0, 2).reshape(rows, f * c)


def roll_sum(values):
    values = values + pltpu.roll(values, 64, 1)
    return values + pltpu.roll(values, 32, 1)


def lane_index():
    return lax.broadcasted_iota(jnp.int32, (TOK, 128), 1)


def attention_kernel(R, HR, q_ref, rope_ref, kv_ref, cos_ref, sin_ref, bias_ref, out_w_ref,
                     att_ref, probs_ref, qb_ref, krb_ref, *part_refs):
    HN = HR * DN
    lane = lane_index()
    cos, sin = cos_ref[...], sin_ref[...]
    rope = rope_ref[...]
    k_1 = roll_sum(jnp.where(lane < 32, rope, 0.0))
    k_2 = roll_sum(jnp.where((lane >= 32) & (lane < 64), rope, 0.0))
    kr_1 = (k_1 * cos - k_2 * sin).astype(BF)
    kr_2 = (k_2 * cos + k_1 * sin).astype(BF)
    krb_ref[:, :128] = kr_1
    krb_ref[:, 128:] = kr_2
    q_1, q_2 = q_ref[:, HN : HN + 128], q_ref[:, HN + 128 :]
    qr_1 = (q_1 * cos - q_2 * sin) * SCALE
    qr_2 = (q_2 * cos + q_1 * sin) * SCALE
    q_n = (q_ref[:, :HN] * SCALE).astype(BF)
    qb_ref[:, :HN] = q_n
    qb_ref[:, HN : HN + 128] = qr_1.astype(BF)
    qb_ref[:, HN + 128 :] = qr_2.astype(BF)
    bias = bias_ref[0]
    for h in range(HR):
        head = (lane >= 32 * h) & (lane < 32 * h + 32)
        scores = (
            dot_t(q_n[:, h * DN : (h + 1) * DN], kv_ref[:, h * DN : (h + 1) * DN])
            + dot_t(jnp.where(head, qr_1, 0.0).astype(BF), kr_1)
            + dot_t(jnp.where(head, qr_2, 0.0).astype(BF), kr_2)
            + bias
        )
        expd = jnp.exp(scores - jnp.max(scores, axis=-1, keepdims=True))
        probs = expd / jnp.sum(expd, axis=-1, keepdims=True)
        probs_ref[h] = probs
        value = kv_ref[:, HN + h * DV : HN + (h + 1) * DV]
        att_ref[:, h * DV : (h + 1) * DV] = dot(probs.astype(BF), value).astype(BF)
    part = dot(att_ref[...], out_w_ref[...]).astype(BF)
    for k in range(R):

        @pl.when(pl.program_id(0) == k)
        def _():
            part_refs[k][...] = part


def attention_grad_kernel(R, HR, *refs):
    grad_refs = refs[:R]
    (att_ref, probs_ref, kv_ref, qb_ref, krb_ref, cos_ref, sin_ref, out_w_ref, kvu_ref,
     gq_ref, gkv_ref) = refs[R : R + 11]
    glat_refs = refs[R + 11 : 2 * R + 11]
    ghb_ref = refs[2 * R + 11]
    HN = HR * DN
    step = pl.program_id(0)
    for k in range(R):

        @pl.when(step == k)
        def _():
            ghb_ref[...] = grad_refs[k][...]

    ghb = ghb_ref[...]
    g_att = dot_t(ghb, out_w_ref[...]).astype(BF)
    lane = lane_index()
    cos, sin = cos_ref[...], sin_ref[...]
    kr_1, kr_2 = krb_ref[:, :128], krb_ref[:, 128:]
    qr_1 = qb_ref[:, HN : HN + 128].astype(F32)
    qr_2 = qb_ref[:, HN + 128 :].astype(F32)
    zero = jnp.zeros((TOK, 128), F32)
    gq_1, gq_2, gk_1, gk_2 = zero, zero, zero, zero
    for h in range(HR):
        cut = slice(h * DN, (h + 1) * DN)
        cut_v = slice(HN + h * DV, HN + (h + 1) * DV)
        head = (lane >= 32 * h) & (lane < 32 * h + 32)
        ga = g_att[:, cut]
        probs = probs_ref[h]
        gkv_ref[:, cut_v] = t_dot(probs.astype(BF), ga).astype(BF)
        delta = jnp.sum(ga.astype(F32) * att_ref[:, cut].astype(F32), axis=-1, keepdims=True)
        gs = (probs * (dot_t(ga, kv_ref[:, cut_v]) - delta)).astype(BF)
        gq_ref[:, cut] = (dot(gs, kv_ref[:, cut]) * SCALE).astype(BF)
        gq_1 = gq_1 + jnp.where(head, dot(gs, kr_1), 0.0)
        gq_2 = gq_2 + jnp.where(head, dot(gs, kr_2), 0.0)
        gkv_ref[:, cut] = t_dot(gs, qb_ref[:, cut]).astype(BF)
        gk_1 = gk_1 + t_dot(gs, jnp.where(head, qr_1, 0.0).astype(BF))
        gk_2 = gk_2 + t_dot(gs, jnp.where(head, qr_2, 0.0).astype(BF))
    gq_ref[:, HN : HN + 128] = ((gq_1 * cos + gq_2 * sin) * SCALE).astype(BF)
    gq_ref[:, HN + 128 :] = ((gq_2 * cos - gq_1 * sin) * SCALE).astype(BF)
    u_1, u_2 = roll_sum(gk_1), roll_sum(gk_2)
    r_1, r_2 = u_1 * cos + u_2 * sin, u_2 * cos - u_1 * sin
    g_rope = jnp.where(lane < 32, r_1, jnp.where(lane < 64, r_2, 0.0)).astype(BF)
    g_lat = dot_t(gkv_ref[...], kvu_ref[...]).astype(BF)
    for k in range(R):

        @pl.when(step == k)
        def _():
            glat_refs[k][:, :KVR] = g_lat
            glat_refs[k][:, KVR:] = g_rope


def exact_dot(left, right):
    return jnp.dot(left, right, precision=lax.Precision.HIGHEST, preferred_element_type=F32)


REP, SHD = "replica", "shard"


STEPS = 4
CHUNK = D // STEPS


def ffn_grad_kernel(R, SR, FR, cot_ref, rest_ref, in_ref, act_ref, slope_ref, e_hid_ref, e_act_ref,
                    e_slope_ref, rows_geo_ref, rows_g_ref, spread_ref, probs_ref, chosen_ref,
                    router_ref, geg_ref, e_geg_ref, rows_out_ref, gc_ref, *refs):
    part_refs = refs[:R]
    acc_ref, e_acc_ref, gc_acc_ref, lg_ref = refs[R:]
    step = pl.program_id(0)

    @pl.when(step < STEPS)
    def _():
        w_edt = rest_ref[:, SR:]
        s_gh = dot(cot_ref[...], rest_ref[:, :SR])
        e_gh = dot(rows_geo_ref[...], w_edt)
        rows_out = dot_t(e_hid_ref[...], w_edt)
        rows_out_ref[...] = rows_out
        gc_rows = jnp.sum(rows_g_ref[...] * rows_out, axis=-1, keepdims=True)
        gc_rows = jnp.broadcast_to(gc_rows, gc_acc_ref.shape)

        @pl.when(step == 0)
        def _():
            acc_ref[...] = s_gh
            e_acc_ref[...] = e_gh
            gc_acc_ref[...] = gc_rows

        @pl.when(step > 0)
        def _():
            acc_ref[...] += s_gh
            e_acc_ref[...] += e_gh
            gc_acc_ref[...] += gc_rows

    @pl.when(step == STEPS - 1)
    def _():
        s_gh = acc_ref[...]
        geg_ref[:, :SR] = (s_gh * slope_ref[...]).astype(BF)
        geg_ref[:, SR:] = (s_gh * act_ref[...]).astype(BF)
        e_gh = e_acc_ref[...]
        e_geg_ref[:, :FR] = (e_gh * e_slope_ref[...]).astype(BF)
        e_geg_ref[:, FR:] = (e_gh * e_act_ref[...]).astype(BF)
        for k in range(R):
            tok, row = slice(k * TOK, (k + 1) * TOK), slice(k * CAP, (k + 1) * CAP)
            gc = exact_dot(spread_ref[tok, :], gc_acc_ref[row, :])
            gc_ref[tok, :] = gc
            p = (gc * chosen_ref[tok, :])[:, :NE]
            probs = probs_ref[tok, :]
            first = lax.broadcasted_iota(jnp.int32, (TOK, NE), 1) == 0
            lg = probs * (jnp.where(first, p, 0.0) - probs[:, :1] * p)
            lg_ref[tok, :] = lg.astype(BF)

    @pl.when(step >= STEPS)
    def _():
        g_n2 = dot_t(geg_ref[...], in_ref[:, : 2 * SR]) + dot_t(lg_ref[...], router_ref[...])
        rows_back = dot_t(e_geg_ref[...], in_ref[:, 2 * SR :])
        for k in range(R):
            tok, row = slice(k * TOK, (k + 1) * TOK), slice(k * CAP, (k + 1) * CAP)
            part = g_n2[tok] + exact_dot(spread_ref[tok, :], rows_back[row])
            part_refs[k][...] = part.astype(BF)


def ffn_out_kernel(R, SR, s_hid_ref, rest_ref, spread_ref, rows_w_ref, rows_out_ref, *part_refs):
    w_sdt = rest_ref[:, :SR]
    for k in range(R):
        tok, row = slice(k * TOK, (k + 1) * TOK), slice(k * CAP, (k + 1) * CAP)
        part = dot_t(s_hid_ref[tok, :], w_sdt) + exact_dot(
            spread_ref[tok, :], rows_w_ref[row, :] * rows_out_ref[row, :]
        )
        part_refs[k][...] = part.astype(BF)


def add_kernel(hidden_ref, *refs):
    total = hidden_ref[...]
    for ref in refs[:-1]:
        total = total + ref[...].astype(F32)
    refs[-1][...] = total.astype(BF)


def ffn_weight_kernel(SR, FR, n2_ref, geg_ref, rows_in_ref, e_geg_ref, rows_geo_ref, e_hid_ref, out_ref):
    cut = 2 * SR + 2 * FR
    out_ref[:, : 2 * SR] = t_dot(n2_ref[...], geg_ref[...]).astype(BF)
    out_ref[:, 2 * SR : cut] = t_dot(rows_in_ref[...], e_geg_ref[...]).astype(BF)
    out_ref[:, cut:] = t_dot(rows_geo_ref[...], e_hid_ref[...]).astype(BF)


def product_kernel(left_ref, right_ref, out_ref):
    out_ref[...] = t_dot(left_ref[...], right_ref[...]).astype(BF)


def attention_weight_kernel(R, QW, r_ref, n1_ref, gq_ref, *refs):
    grad_refs, att_refs = refs[:R], refs[R : 2 * R]
    out_ref, ghb_ref, att_ref = refs[2 * R :]
    step = pl.program_id(0)

    @pl.when(step == 0)
    def _():
        for k in range(R):
            ghb_ref[k * TOK : (k + 1) * TOK, :] = grad_refs[k][...]

    for k in range(R):

        @pl.when((r_ref[0] ^ step) == k)
        def _():
            for i in range(R):
                att_ref[i * TOK : (i + 1) * TOK, :] = att_refs[k][
                    (i ^ k) * TOK : ((i ^ k) + 1) * TOK, :
                ]

    out_ref[:, :QW] = t_dot(n1_ref[...], gq_ref[...]).astype(BF)
    out_ref[:, QW:] = t_dot(att_ref[...], ghb_ref[...]).astype(BF)


def whole_block(shape):
    return pl.BlockSpec(shape, lambda *_: (0,) * len(shape))


def join_ffn_kernel(R, SR, FR, blocks, gate_ref, up_ref, e_gate_ref, e_up_ref, e_down_ref):
    cut = 2 * SR
    for j in range(R):
        gate_ref[:, j * SR : (j + 1) * SR] = blocks[j, :, :SR].astype(F32)
        up_ref[:, j * SR : (j + 1) * SR] = blocks[j, :, SR:cut].astype(F32)
        e_gate_ref[:, j * FR : (j + 1) * FR] = blocks[j, :, cut : cut + FR].astype(F32)
        e_up_ref[:, j * FR : (j + 1) * FR] = blocks[j, :, cut + FR : cut + 2 * FR].astype(F32)
        e_down_ref[j * FR : (j + 1) * FR, :] = blocks[j, :, cut + 2 * FR :].astype(F32).T


def join_down_kernel(R, SR, blocks, down_ref):
    for j in range(R):
        down_ref[j * SR : (j + 1) * SR, :] = blocks[j].astype(F32).T


def join_attention_kernel(R, HR, blocks, query_ref, out_ref):
    HN, W, half = HR * DN, DN + DR, DR // 2
    DC = D // R
    for j in range(R):
        for h in range(HR):
            at = (j * HR + h) * W
            one, two = HN + h * half, HN + 128 + h * half
            query_ref[:, at : at + DN] = blocks[j, :, h * DN : (h + 1) * DN].astype(F32)
            query_ref[:, at + DN : at + DN + half] = blocks[j, :, one : one + half].astype(F32)
            query_ref[:, at + DN + half : at + W] = blocks[j, :, two : two + half].astype(F32)
        out_ref[:, j * DC : (j + 1) * DC] = blocks[j, :, HN + 256 :].astype(F32)


def join_tail_kernel(R, HS, KR, LR, blocks, up_ref, down_ref, router_ref):
    W, NR = DN + DV, NE // R
    for j in range(R):
        for h in range(HS):
            up_ref[j * KR : (j + 1) * KR, h * W : (h + 1) * W] = blocks[
                j, h * KR : (h + 1) * KR, :W
            ].astype(F32)
        down_ref[j * LR : (j + 1) * LR, :] = blocks[j, :, W : W + LR].astype(F32).T
        router_ref[j * NR : (j + 1) * NR, :] = blocks[j, :, W + LR :].astype(F32).T


def join_blocks(kernel, R, r, pieces, outs):
    rows, width = pieces[0][2].shape

    def body(r_ref, *refs):
        block_ref = refs[-1]
        for (k, row, values), ref in zip(pieces, refs):
            block_ref[r_ref[0] ^ k, row : row + values.shape[0], :] = ref[...]
        kernel(block_ref, *refs[len(pieces) : -1])

    return pl.pallas_call(
        body,
        in_specs=[pl.BlockSpec(memory_space=pltpu.SMEM)]
        + [whole_block(values.shape) for _, _, values in pieces],
        out_specs=[whole_block(s) for s in outs],
        out_shape=[jax.ShapeDtypeStruct(s, F32) for s in outs],
        scratch_shapes=[pltpu.VMEM((R, rows, width), BF)],
    )(r.reshape(1), *[values for _, _, values in pieces])


def make_local(R, S):
    DL = D // S
    HR = H // R
    HS = H // S
    KR = KVR // R
    DC = D // R
    FR = FF // R
    SR = SH // R
    LR = (KVR + DR) // R
    NR = NE // R
    T = R * TOK
    QW = HR * DN + 256
    half = DR // 2
    HL = HR * half
    GR = DL // 64
    links = [[(i, i ^ k) for i in range(R)] for k in range(R)]

    def send(values, k):
        return lax.ppermute(values, REP, links[k])

    def gather(values):
        return [values] + [send(values, k) for k in range(1, R)]

    def local(
        hidden_in,
        segment_ids,
        routes,
        norm_gain,
        query_weight,
        kv_down,
        kv_gain,
        kv_up,
        out_weight,
        mixer_gain,
        router_weight,
        shared_gate,
        shared_up,
        shared_down,
        expert_gate,
        expert_up,
        expert_down,
        cotangent,
    ):
        r = lax.axis_index(REP)

        def part(values, width, axis=1):
            return lax.dynamic_slice_in_dim(values, r * width, width, axis)

        def natural(blocks):
            stacked = jnp.stack(blocks)
            return [
                lax.dynamic_index_in_dim(stacked, r ^ j, 0, keepdims=False) for j in range(R)
            ]

        def reduce_parts(parts):
            own = parts[0].astype(F32)
            received = [send(parts[k].astype(BF), k) for k in range(1, R)]
            for part_sum in received:
                own = own + part_sum.astype(F32)
            return own

        def reduce_blocks(total):
            return reduce_parts([total[k * TOK : (k + 1) * TOK] for k in range(R)])

        def gather_pieces(values):
            if R != 4:
                return [(k, 0, block) for k, block in enumerate(gather(values))]
            mid = values.shape[0] // 2
            values = by_rows(values)
            side, other = by_rows(send(values, 1)), by_rows(send(values, 2))
            top, low = by_rows(send(other[:mid], 1)), by_rows(send(side[mid:], 2))
            return [(0, 0, values), (1, 0, side), (2, 0, other), (3, 0, top), (3, mid, low)]

        def shard_gather(values):
            return lax.all_gather(values, SHD, axis=0, tiled=True)

        def shard_reduce(values):
            return lax.psum_scatter(values, SHD, scatter_dimension=0, tiled=True)

        index = jnp.arange(TOK, dtype=jnp.int32)
        same_own = segment_ids[:, None] == segment_ids[None, :]
        start_own = jnp.min(jnp.where(same_own, index[None, :], TOK), axis=1)
        chosen_own = jnp.any(routes == 0, axis=1)
        meta_own = jnp.concatenate(
            [
                start_own.astype(BF)[None],
                chosen_own.astype(BF)[None],
                jnp.zeros((6, TOK), BF),
            ]
        )
        meta = jnp.stack(gather(meta_own))
        x_all = jnp.concatenate(gather(hidden_in))
        cot_all = jnp.concatenate(gather(cotangent))

        kv_piece = (
            part(kv_up, KR, 0).reshape(KR, HS, DN + DV).transpose(1, 0, 2).reshape(HS * KR, DN + DV)
        )
        head_own = jnp.concatenate([part(out_weight, DC), fold(kv_piece, DL)], axis=1)
        head_all = shard_gather(head_own)
        kvu_all = unfold_all(head_all[:, DC:], S, DL, HS * KR).reshape(H, KR, DN + DV)
        out_all = head_all[:, :DC]
        head_blocks = []
        for k in range(R):
            rk = r ^ k
            piece = jnp.concatenate(
                [
                    lax.dynamic_slice_in_dim(out_all, rk * HR * DV, HR * DV, 0),
                    fold(
                        lax.dynamic_slice_in_dim(kvu_all, rk * HR, HR, 0).reshape(
                            HR * KR, DN + DV
                        ),
                        HR * DV,
                    ),
                ],
                axis=1,
            )
            head_blocks.append(send(piece, k) if k else piece)
        head_nat = natural(head_blocks)
        out_w = jnp.concatenate([b[:, :DC] for b in head_nat], axis=1)
        kvu = jnp.concatenate(
            [unfold(b[:, DC:], HR * KR).reshape(HR, KR, DN + DV) for b in head_nat], axis=1
        )
        kvu2 = jnp.concatenate(
            [
                kvu[:, :, :DN].transpose(1, 0, 2).reshape(KVR, HR * DN),
                kvu[:, :, DN:].transpose(1, 0, 2).reshape(KVR, HR * DV),
            ],
            axis=1,
        )

        def gain_rows(one, two, kv):
            lead = one.shape[:-1]
            pads = [(0, 0)] * len(lead)
            rows = jnp.concatenate(
                [
                    one.reshape(lead + (GR, 64)),
                    two.reshape(lead + (GR, 64)),
                    jnp.pad(kv, pads + [(0, 64 - KVR // S)]).reshape(lead + (1, 64)),
                ],
                axis=-2,
            )
            return jnp.pad(rows, pads + [(0, DL - 2 * GR - 1), (0, 0)])

        q_own = part(query_weight, HR * (DN + DR)).reshape(DL, HR, DN + DR)
        rope_pad = ((0, 0), (0, 128 - HL))
        attn_own = jnp.concatenate(
            [
                q_own[..., :DN].reshape(DL, HR * DN),
                jnp.pad(q_own[..., DN : DN + half].reshape(DL, HL), rope_pad),
                jnp.pad(q_own[..., DN + half :].reshape(DL, HL), rope_pad),
                kv_down,
                router_weight,
                gain_rows(norm_gain, mixer_gain, kv_gain),
            ],
            axis=1,
        )
        attn_all = shard_gather(attn_own)
        CD, CR, CG = QW, QW + KVR + DR, QW + KVR + DR + NE
        w_q = attn_all[:, :QW]
        w_down = attn_all[:, CD:CR]
        w_router = attn_all[:, CR:CG]
        gain_all = attn_all[:, CG:].reshape(S, DL, 64).astype(F32)
        gain_one = gain_all[:, :GR].reshape(D)
        gain_two = gain_all[:, GR : 2 * GR].reshape(D)
        gain_kv = gain_all[:, 2 * GR, : KVR // S].reshape(KVR)

        in_all = shard_gather(
            jnp.concatenate(
                [
                    part(shared_gate, SR),
                    part(shared_up, SR),
                    part(expert_gate[0], FR),
                    part(expert_up[0], FR),
                ],
                axis=1,
            ),
        )
        w_gu, w_egu = in_all[:, : 2 * SR], in_all[:, 2 * SR :]
        rest_all = shard_gather(
            jnp.concatenate([part(shared_down, SR, 0).T, part(expert_down[0], FR, 0).T], axis=1),
        )

        xf = x_all.astype(F32)
        scale_one = inv_rms(xf)
        n1 = (xf * scale_one * gain_one).astype(BF)
        qlat = dot(n1, attn_all)
        latent = qlat[:, CD : CD + KVR]
        scale_kv = inv_rms(latent)
        lat_n = (latent * scale_kv * gain_kv).astype(BF)
        kv = dot(lat_n, kvu2).astype(BF)

        start = meta[:, 0].astype(F32)
        position = index.astype(F32)[None] - start
        freq = 10000.0 ** (-jnp.arange(half, dtype=F32) / half)
        angles = position.reshape(T, 1) * jnp.tile(freq, 4)[None]
        cosine, sine = jnp.cos(angles), jnp.sin(angles)
        allowed = (start[:, :, None] == start[:, None, :]) & (index[None, :] <= index[:, None])[None]
        bias = jnp.where(allowed, 0.0, NEGATIVE).astype(F32)

        def rows(width, column=0):
            return pl.BlockSpec((TOK, width), lambda i: (i, column))

        def whole(*shape):
            return pl.BlockSpec(shape, lambda i: (0,) * len(shape))

        HN = HR * DN
        forward = pl.pallas_call(
            lambda *refs: attention_kernel(R, HR, *refs),
            grid=(R,),
            in_specs=[
                rows(QW),
                rows(128, (CD + KVR) // 128),
                rows(2 * HN),
                rows(128),
                rows(128),
                pl.BlockSpec((1, TOK, TOK), lambda i: (i, 0, 0)),
                whole(HN, D),
            ],
            out_specs=[
                rows(HN),
                pl.BlockSpec((HR, TOK, TOK), lambda i: (i, 0, 0)),
                rows(QW),
                rows(256),
            ]
            + [whole(TOK, D)] * R,
            out_shape=[
                jax.ShapeDtypeStruct((T, HN), BF),
                jax.ShapeDtypeStruct((R * HR, TOK, TOK), F32),
                jax.ShapeDtypeStruct((T, QW), BF),
                jax.ShapeDtypeStruct((T, 256), BF),
            ]
            + [jax.ShapeDtypeStruct((TOK, D), BF)] * R,
        )
        att, probs, q_b, kr_b, *out_parts = forward(
            qlat, qlat, kv, cosine, sine, bias, out_w
        )
        x_own = hidden_in.astype(F32)
        hidden = x_own + reduce_parts(out_parts)

        scale_two = inv_rms(hidden)
        n2_own = (hidden * scale_two * gain_two).astype(BF)
        n2 = jnp.concatenate(gather(n2_own))
        att_all = gather(att)
        probs_r = jax.nn.softmax(dot(n2, w_router), axis=-1)
        chosen = meta[:, 1].astype(F32)
        combine = probs_r[:, 0].reshape(R, TOK) * chosen
        place = jnp.cumsum(chosen.astype(jnp.int32), axis=1) - 1
        slots = jnp.arange(CAP, dtype=jnp.int32)
        dispatch = (
            (place[:, None, :] == slots[None, :, None]) & (chosen[:, None, :] > 0.5)
        ).astype(F32)
        dispatch_b = dispatch.astype(BF)
        n2_b = n2.reshape(R, TOK, D)
        cot_b = cot_all.reshape(R, TOK, D)
        rows_in = ein("bct,btd->bcd", dispatch_b, n2_b).astype(BF).reshape(R * CAP, D)
        rows_g = ein("bct,btd->bcd", dispatch_b, cot_b).reshape(R * CAP, D)
        rows_w = jnp.sum(dispatch * combine[:, None, :], axis=-1).reshape(R * CAP, 1)

        pre = dot(n2, w_gu)
        g_pre, u_pre = pre[:, :SR], pre[:, SR:]
        act, slope = silu_parts(g_pre)
        s_hid = (act * u_pre).astype(BF)
        down_part = pl.pallas_call(
            product_kernel,
            grid=(STEPS,),
            in_specs=[pl.BlockSpec((T, CHUNK), lambda i: (0, i)), whole_block((T, SR))],
            out_specs=pl.BlockSpec((CHUNK, SR), lambda i: (i, 0)),
            out_shape=jax.ShapeDtypeStruct((D, SR), BF),
        )(cot_all, s_hid)
        down_red = shard_reduce(down_part)
        e_pre = dot(rows_in, w_egu)
        e_g, e_u = e_pre[:, :FR], e_pre[:, FR:]
        e_act, e_slope = silu_parts(e_g)
        e_hid = (e_act * e_u).astype(BF)
        rows_geo = (rows_w * rows_g).astype(BF)
        spread = dispatch.transpose(0, 2, 1).reshape(T, CAP)
        chosen_wide = jnp.broadcast_to(chosen.reshape(T, 1), (T, 128))
        operands = (
            cot_all,
            rest_all,
            in_all,
            act,
            u_pre * slope,
            e_hid,
            e_act,
            e_u * e_slope,
            rows_geo,
            rows_g,
            spread,
            probs_r,
            chosen_wide,
            w_router,
        )
        RC = R * CAP

        def early(i):
            return jnp.minimum(i, STEPS - 1)

        def late(i):
            return jnp.maximum(i - STEPS, 0)

        specs = {
            0: pl.BlockSpec((T, CHUNK), lambda i: (0, early(i))),
            1: pl.BlockSpec((CHUNK, SR + FR), lambda i: (early(i), 0)),
            2: pl.BlockSpec((CHUNK, 2 * SR + 2 * FR), lambda i: (late(i), 0)),
            8: pl.BlockSpec((RC, CHUNK), lambda i: (0, early(i))),
            9: pl.BlockSpec((RC, CHUNK), lambda i: (0, early(i))),
            13: pl.BlockSpec((CHUNK, NE), lambda i: (late(i), 0)),
        }
        shapes = [
            ((T, 2 * SR), BF),
            ((RC, 2 * FR), BF),
            ((RC, D), F32),
            ((T, 128), F32),
        ] + [((TOK, D), BF)] * R
        s_geg, e_geg, rows_out, gc_wide, *gn2_parts = pl.pallas_call(
            lambda *refs: ffn_grad_kernel(R, SR, FR, *refs),
            grid=(2 * STEPS,),
            in_specs=[specs.get(n, whole_block(v.shape)) for n, v in enumerate(operands)],
            out_specs=[
                whole_block(shapes[0][0]),
                whole_block(shapes[1][0]),
                pl.BlockSpec((RC, CHUNK), lambda i: (0, early(i))),
                whole_block(shapes[3][0]),
            ]
            + [pl.BlockSpec((TOK, CHUNK), lambda i: (0, late(i)))] * R,
            out_shape=[jax.ShapeDtypeStruct(s, t) for s, t in shapes],
            scratch_shapes=[
                pltpu.VMEM((T, SR), F32),
                pltpu.VMEM((RC, FR), F32),
                pltpu.VMEM((RC, 128), F32),
                pltpu.VMEM((T, NE), BF),
            ],
        )(*operands)
        gc_part = gc_wide[:, 0].reshape(R, TOK)

        def logits_grad(gc):
            p = (gc * chosen).reshape(T, 1)
            first = (jnp.arange(NE) == 0).astype(F32)[None]
            return (probs_r * (p * first - probs_r[:, :1] * p)).astype(BF)

        gn2 = reduce_parts(gn2_parts)

        def columns(values):
            return pl.BlockSpec((values.shape[0], CHUNK), lambda i: (0, i))

        GW = 2 * SR + 3 * FR
        gu_part = pl.pallas_call(
            lambda *refs: ffn_weight_kernel(SR, FR, *refs),
            grid=(STEPS,),
            in_specs=[
                columns(n2),
                whole_block(s_geg.shape),
                columns(rows_in),
                whole_block(e_geg.shape),
                columns(rows_geo),
                whole_block(e_hid.shape),
            ],
            out_specs=pl.BlockSpec((CHUNK, GW), lambda i: (i, 0)),
            out_shape=jax.ShapeDtypeStruct((D, GW), BF),
        )(n2, s_geg, rows_in, e_geg, rows_geo, e_hid)
        gu_red = shard_reduce(gu_part)
        operands = (s_hid, rest_all, spread, rows_w, rows_out)
        out_ffn = pl.pallas_call(
            lambda *refs: ffn_out_kernel(R, SR, *refs),
            in_specs=[whole_block(v.shape) for v in operands],
            out_specs=[whole_block((TOK, D))] * R,
            out_shape=[jax.ShapeDtypeStruct((TOK, D), BF)] * R,
        )(*operands)
        out_ffn = [out_ffn[0]] + [send(out_ffn[k], k) for k in range(1, R)]
        result = pl.pallas_call(
            add_kernel, out_shape=jax.ShapeDtypeStruct((TOK, D), BF)
        )(hidden, *out_ffn)
        gc_all = gather(gc_part)
        gc_total = gc_all[0]
        for j in range(1, R):
            gc_total = gc_total + jnp.stack([gc_all[j][k ^ j] for k in range(R)])

        g_mixer = jnp.sum(gn2 * hidden * scale_two, axis=0)
        scaled = gn2 * gain_two
        grad_hidden = (
            cotangent.astype(F32)
            + scale_two * scaled
            - hidden * scale_two**3 * jnp.mean(scaled * hidden, axis=-1, keepdims=True)
        )

        backward = pl.pallas_call(
            lambda *refs: attention_grad_kernel(R, HR, *refs),
            grid=(R,),
            in_specs=[whole(TOK, D)] * R
            + [
                rows(HN),
                pl.BlockSpec((HR, TOK, TOK), lambda i: (i, 0, 0)),
                rows(2 * HN),
                rows(QW),
                rows(256),
                rows(128),
                rows(128),
                whole(HN, D),
                whole(KVR, 2 * HN),
            ],
            out_specs=[rows(QW), rows(2 * HN)] + [whole(TOK, KVR + 128)] * R,
            out_shape=[
                jax.ShapeDtypeStruct((T, QW), BF),
                jax.ShapeDtypeStruct((T, 2 * HN), BF),
            ]
            + [jax.ShapeDtypeStruct((TOK, KVR + 128), BF)] * R,
            scratch_shapes=[pltpu.VMEM((TOK, D), BF)],
        )
        ghb = gather(grad_hidden.astype(BF))
        gq, g_kv, *glat_parts = backward(
            *ghb, att, probs, kv, q_b, kr_b, cosine, sine, out_w, kvu2
        )
        attn_part = pl.pallas_call(
            lambda *refs: attention_weight_kernel(R, QW, *refs),
            grid_spec=pltpu.PrefetchScalarGridSpec(
                num_scalar_prefetch=1,
                grid=(R,),
                in_specs=[
                    pl.BlockSpec((T, DC), lambda i, r_ref: (0, i)),
                    whole_block((T, QW)),
                ]
                + [pl.BlockSpec((TOK, DC), lambda i, r_ref: (0, r_ref[0]))] * R
                + [whole_block((T, HN))] * R,
                out_specs=pl.BlockSpec((DC, QW + DC), lambda i, r_ref: (i, 0)),
                scratch_shapes=[pltpu.VMEM((T, DC), BF), pltpu.VMEM((T, HN), BF)],
            ),
            out_shape=jax.ShapeDtypeStruct((D, QW + DC), BF),
        )(r.reshape(1), n1, gq, *ghb, *att_all)
        glat = reduce_parts(glat_parts)
        latent_own, scale_kv_own = latent[:TOK], scale_kv[:TOK]
        gl_n = glat[:, :KVR]
        g_kvgain = jnp.sum(gl_n * latent_own * scale_kv_own, axis=0)
        lat_scaled = gl_n * gain_kv
        g_latent = scale_kv_own * lat_scaled - latent_own * scale_kv_own**3 * jnp.mean(
            lat_scaled * latent_own, axis=-1, keepdims=True
        )
        gd_own = jnp.concatenate([g_latent, glat[:, KVR : KVR + DR]], axis=1).astype(BF)
        gd = part(jnp.concatenate(gather(gd_own)), LR)
        gn1_part = dot_t(gq, w_q) + dot_t(gd, part(w_down, LR))
        gn1 = reduce_blocks(gn1_part)
        scale_own = scale_one[:TOK]
        scaled_one = gn1 * gain_one
        grad_input = (
            grad_hidden
            + scale_own * scaled_one
            - x_own * scale_own**3 * jnp.mean(scaled_one * x_own, axis=-1, keepdims=True)
        )
        g_norm = jnp.sum(gn1_part * xf * scale_one, axis=0)

        g_kvu2 = t_dot(lat_n, g_kv).astype(BF)
        g_kvu = jnp.concatenate(
            [
                g_kvu2[:, :HN].reshape(KVR, HR, DN),
                g_kvu2[:, HN:].reshape(KVR, HR, DV),
            ],
            axis=2,
        ).transpose(1, 0, 2)
        kvu_blocks = []
        for k in range(R):
            b = lax.dynamic_slice_in_dim(g_kvu, (r ^ k) * KR, KR, 1)
            kvu_blocks.append(send(b, k) if k else b)
        g_kvu_all = jnp.concatenate(natural(kvu_blocks))
        g_kvu_all = fold_all(g_kvu_all.reshape(H * KR, DN + DV), S, DL)

        g_router = t_dot(n2, part(logits_grad(gc_total), NR))
        g_down = t_dot(n1, gd)
        vectors = jnp.concatenate([g_norm, g_mixer, g_kvgain])
        summed = sum(gather(vectors))
        g_gains = gain_rows(
            summed[:D].reshape(S, DL),
            summed[D : 2 * D].reshape(S, DL),
            summed[2 * D :].reshape(S, KVR // S),
        ).reshape(D, 64)
        attn_red = shard_reduce(attn_part)
        pad = (-(LR + NR + 64)) % 128
        tail_red = shard_reduce(
            jnp.concatenate(
                [
                    g_kvu_all,
                    g_down.astype(BF),
                    g_router.astype(BF),
                    g_gains.astype(BF),
                    jnp.zeros((D, pad), BF),
                ],
                axis=1,
            ),
        )

        KW = HS * KR * (DN + DV) // DL
        (own_sd,) = join_blocks(
            lambda *refs: join_down_kernel(R, SR, *refs), R, r, gather_pieces(down_red), [(SH, DL)]
        )
        own_sg, own_su, own_eg, own_eu, own_ed = join_blocks(
            lambda *refs: join_ffn_kernel(R, SR, FR, *refs),
            R,
            r,
            gather_pieces(gu_red),
            [(DL, SH), (DL, SH), (DL, FF), (DL, FF), (FF, DL)],
        )
        own_qw, own_ow = join_blocks(
            lambda *refs: join_attention_kernel(R, HR, *refs),
            R,
            r,
            gather_pieces(attn_red),
            [(DL, H * (DN + DR)), (DL, D)],
        )
        tail_pieces = gather(tail_red[:, : KW + LR + NR])
        gains_red = tail_red[:, KW + LR + NR : KW + LR + NR + 64].astype(F32)
        if KW == DN + DV:
            own_ku, own_kd, own_rw = join_blocks(
                lambda *refs: join_tail_kernel(R, HS, KR, LR, *refs),
                R,
                r,
                [(k, 0, block) for k, block in enumerate(tail_pieces)],
                [(KVR, HS * (DN + DV)), (KVR + DR, DL), (NE, DL)],
            )
            own_kd, own_rw = own_kd.T, own_rw.T
        else:
            tail_nat = natural(tail_pieces)
            own_ku = jnp.concatenate(
                [
                    unfold(b[:, :KW], HS * KR)
                    .reshape(HS, KR, DN + DV)
                    .transpose(1, 0, 2)
                    .reshape(KR, HS * (DN + DV))
                    for b in tail_nat
                ]
            ).astype(F32)
            own_kd = jnp.concatenate([b[:, KW : KW + LR] for b in tail_nat], axis=1).astype(F32)
            own_rw = jnp.concatenate([b[:, KW + LR :] for b in tail_nat], axis=1).astype(F32)
        return (
            result,
            grad_input,
            gains_red[:GR].reshape(DL),
            own_qw,
            own_kd,
            gains_red[2 * GR, : KVR // S],
            own_ku,
            own_ow,
            gains_red[GR : 2 * GR].reshape(DL),
            own_rw,
            own_sg,
            own_su,
            own_sd,
            own_eg[None],
            own_eu[None],
            own_ed[None],
        )

    return local


def unfold_all(values, S, DL, rows):
    _, c = values.shape
    f = DL // rows
    if f <= 1:
        return values
    return values.reshape(S, f, rows, c).transpose(0, 2, 1, 3).reshape(S * rows, f * c)


def fold_all(values, S, DL):
    n, c = values.shape
    f = S * DL // n
    if f <= 1:
        return values
    return values.reshape(S, n // S, f, c // f).transpose(0, 2, 1, 3).reshape(S * DL, c // f)


def solution(mesh):
    tokens = P((REP, SHD), None)
    rows, cols = P(SHD, None), P(None, SHD)
    placed = (
        tokens,
        P((REP, SHD)),
        tokens,
        P(SHD),
        rows,
        rows,
        P(SHD),
        cols,
        rows,
        P(SHD),
        rows,
        rows,
        rows,
        cols,
        P(None, SHD, None),
        P(None, SHD, None),
        P(None, None, SHD),
        tokens,
    )
    outs = (tokens, tokens) + placed[3:17]
    body = make_local(mesh.shape[REP], mesh.shape[SHD])

    return jax.shard_map(
        body,
        mesh=mesh,
        in_specs=placed,
        out_specs=outs,
        check_vma=False,
    )
```

```python
import jax
import jax.numpy as jnp
from jax import lax
from jax.experimental import pallas as pl
from jax.experimental.pallas import tpu as pltpu
from jax.sharding import PartitionSpec as P

D = 2048
H = 16
DN = 128
DR = 64
DV = 128
KVR = 512
NE = 64
CAP = 16
FF = 1408
SH = 2816
TOK = 128

EPSILON = 1e-06
NEGATIVE = -1e30
BF = jnp.bfloat16
F32 = jnp.float32
SCALE = (DN + DR) ** (-0.5)


def dot(left, right):
    return jnp.dot(left, right, preferred_element_type=F32)


def dot_t(left, right):
    return lax.dot_general(left, right, (((1,), (1,)), ((), ())), preferred_element_type=F32)


def t_dot(left, right):
    return lax.dot_general(left, right, (((0,), (0,)), ((), ())), preferred_element_type=F32)


def ein(form, left, right):
    return jnp.einsum(form, left, right, preferred_element_type=F32)


def inv_rms(values):
    return lax.rsqrt(jnp.mean(values * values, axis=-1, keepdims=True) + EPSILON)


def silu_parts(pre_act):
    sigmoid_val = jax.nn.sigmoid(pre_act)
    return (pre_act * sigmoid_val, sigmoid_val * (1.0 + pre_act * (1.0 - sigmoid_val)))


def fold(values, rows):
    n, c = values.shape
    f = rows // n
    if f <= 1:
        return values
    return values.reshape(n, f, c // f).transpose(1, 0, 2).reshape(rows, c // f)


def unfold(values, rows):
    n, c = values.shape
    f = n // rows
    if f <= 1:
        return values
    return values.reshape(f, rows, c).transpose(1, 0, 2).reshape(rows, f * c)


def roll_sum(values):
    values = values + pltpu.roll(values, 64, 1)
    return values + pltpu.roll(values, 32, 1)


def lane_index():
    return lax.broadcasted_iota(jnp.int32, (TOK, 128), 1)


def block_at(R, r_ref, k, width):
    if R != 4:
        return slice(k * width, (k + 1) * width)
    return pl.ds(pl.multiple_of((r_ref[0] ^ k) * width, width), width)


def attention_kernel(R, HR, r_ref, q_ref, rope_ref, lat_ref, cos_ref, sin_ref, bias_ref, *refs):
    out_w_refs, kvu_refs = refs[:R], refs[R : 2 * R]
    att_ref, probs_ref, qb_ref, krb_ref, kv_ref = refs[2 * R : 2 * R + 5]
    part_refs, sum_ref = refs[2 * R + 5 : 3 * R + 5], refs[-1]
    HN, KR, W = HR * DN, KVR // R, DN + DV
    lats = [lat_ref[:, block_at(R, r_ref, k, KR)] for k in range(R)]
    for h in range(HR):
        total = dot(lats[0], kvu_refs[0][h * KR : (h + 1) * KR, :])
        for k in range(1, R):
            total = total + dot(lats[k], kvu_refs[k][h * KR : (h + 1) * KR, :])
        kv_ref[:, h * W : (h + 1) * W] = total.astype(BF)
    lane = lane_index()
    cos, sin = cos_ref[...], sin_ref[...]
    rope = rope_ref[...]
    k_1 = roll_sum(jnp.where(lane < 32, rope, 0.0))
    k_2 = roll_sum(jnp.where((lane >= 32) & (lane < 64), rope, 0.0))
    kr_1 = (k_1 * cos - k_2 * sin).astype(BF)
    kr_2 = (k_2 * cos + k_1 * sin).astype(BF)
    krb_ref[:, :128] = kr_1
    krb_ref[:, 128:] = kr_2
    q_1, q_2 = q_ref[:, HN : HN + 128], q_ref[:, HN + 128 :]
    qr_1 = (q_1 * cos - q_2 * sin) * SCALE
    qr_2 = (q_2 * cos + q_1 * sin) * SCALE
    q_n = (q_ref[:, :HN] * SCALE).astype(BF)
    qb_ref[:, :HN] = q_n
    qb_ref[:, HN : HN + 128] = qr_1.astype(BF)
    qb_ref[:, HN + 128 :] = qr_2.astype(BF)
    bias = bias_ref[0]
    for h in range(HR):
        head = (lane >= 32 * h) & (lane < 32 * h + 32)
        scores = (
            dot_t(q_n[:, h * DN : (h + 1) * DN], kv_ref[:, h * W : h * W + DN])
            + dot_t(jnp.where(head, qr_1, 0.0).astype(BF), kr_1)
            + dot_t(jnp.where(head, qr_2, 0.0).astype(BF), kr_2)
            + bias
        )
        expd = jnp.exp(scores - jnp.max(scores, axis=-1, keepdims=True))
        probs = expd / jnp.sum(expd, axis=-1, keepdims=True)
        probs_ref[h] = probs
        value = kv_ref[:, h * W + DN : (h + 1) * W]
        att_ref[:, h * DV : (h + 1) * DV] = dot(probs.astype(BF), value).astype(BF)
    att = att_ref[...]
    for k in range(R):
        sum_ref[:, block_at(R, r_ref, k, D // R)] = dot(att, out_w_refs[k][...]).astype(BF)
    for k in range(R):

        @pl.when(pl.program_id(0) == k)
        def _():
            part_refs[k][...] = sum_ref[...]


def attention_grad_kernel(R, HR, r_ref, *refs):
    grad_refs, out_w_refs, kvu_refs = refs[:R], refs[R : 2 * R], refs[2 * R : 3 * R]
    (att_ref, probs_ref, kv_ref, qb_ref, krb_ref, cos_ref, sin_ref,
     gq_ref, gkv_ref) = refs[3 * R : 3 * R + 9]
    glat_refs = refs[3 * R + 9 : 4 * R + 9]
    ghb_ref, lat_ref = refs[4 * R + 9 :]
    HN, KR, W = HR * DN, KVR // R, DN + DV
    step = pl.program_id(0)
    for k in range(R):

        @pl.when(step == k)
        def _():
            ghb_ref[...] = grad_refs[k][...]

    g_att = dot_t(ghb_ref[:, block_at(R, r_ref, 0, D // R)], out_w_refs[0][...])
    for k in range(1, R):
        g_att = g_att + dot_t(ghb_ref[:, block_at(R, r_ref, k, D // R)], out_w_refs[k][...])
    g_att = g_att.astype(BF)
    lane = lane_index()
    cos, sin = cos_ref[...], sin_ref[...]
    kr_1, kr_2 = krb_ref[:, :128], krb_ref[:, 128:]
    qr_1 = qb_ref[:, HN : HN + 128].astype(F32)
    qr_2 = qb_ref[:, HN + 128 :].astype(F32)
    zero = jnp.zeros((TOK, 128), F32)
    gq_1, gq_2, gk_1, gk_2 = zero, zero, zero, zero
    for h in range(HR):
        cut = slice(h * DN, (h + 1) * DN)
        key, value = slice(h * W, h * W + DN), slice(h * W + DN, (h + 1) * W)
        head = (lane >= 32 * h) & (lane < 32 * h + 32)
        ga = g_att[:, cut]
        probs = probs_ref[h]
        gkv_ref[:, value] = t_dot(probs.astype(BF), ga).astype(BF)
        delta = jnp.sum(ga.astype(F32) * att_ref[:, cut].astype(F32), axis=-1, keepdims=True)
        gs = (probs * (dot_t(ga, kv_ref[:, value]) - delta)).astype(BF)
        gq_ref[:, cut] = (dot(gs, kv_ref[:, key]) * SCALE).astype(BF)
        gq_1 = gq_1 + jnp.where(head, dot(gs, kr_1), 0.0)
        gq_2 = gq_2 + jnp.where(head, dot(gs, kr_2), 0.0)
        gkv_ref[:, key] = t_dot(gs, qb_ref[:, cut]).astype(BF)
        gk_1 = gk_1 + t_dot(gs, jnp.where(head, qr_1, 0.0).astype(BF))
        gk_2 = gk_2 + t_dot(gs, jnp.where(head, qr_2, 0.0).astype(BF))
    gq_ref[:, HN : HN + 128] = ((gq_1 * cos + gq_2 * sin) * SCALE).astype(BF)
    gq_ref[:, HN + 128 :] = ((gq_2 * cos - gq_1 * sin) * SCALE).astype(BF)
    u_1, u_2 = roll_sum(gk_1), roll_sum(gk_2)
    r_1, r_2 = u_1 * cos + u_2 * sin, u_2 * cos - u_1 * sin
    g_rope = jnp.where(lane < 32, r_1, jnp.where(lane < 64, r_2, 0.0)).astype(BF)
    lat_ref[:, KVR:] = g_rope
    for k in range(R):
        total = dot_t(gkv_ref[:, :W], kvu_refs[k][:KR, :])
        for h in range(1, HR):
            total = total + dot_t(
                gkv_ref[:, h * W : (h + 1) * W], kvu_refs[k][h * KR : (h + 1) * KR, :]
            )
        lat_ref[:, block_at(R, r_ref, k, KR)] = total.astype(BF)
    for k in range(R):

        @pl.when(step == k)
        def _():
            glat_refs[k][...] = lat_ref[...]


def scatter_rows(spread, rows):
    high = rows.astype(BF)
    low = (rows - high.astype(F32)).astype(BF)
    return dot(spread, jnp.concatenate([high, low], axis=0))


REP, SHD = "replica", "shard"


STEPS = 4
CHUNK = D // STEPS


def ffn_grad_kernel(R, SR, FR, cot_ref, rest_ref, in_ref, act_ref, slope_ref, e_hid_ref, e_act_ref,
                    e_slope_ref, rows_geo_ref, rows_g_ref, spread_ref, probs_ref, chosen_ref,
                    router_ref, geg_ref, e_geg_ref, rows_out_ref, gc_ref, *refs):
    part_refs = refs[:R]
    acc_ref, e_acc_ref, gc_acc_ref, lg_ref = refs[R:]
    step = pl.program_id(0)

    @pl.when(step < STEPS)
    def _():
        w_edt = rest_ref[:, SR:]
        s_gh = dot(cot_ref[...], rest_ref[:, :SR])
        e_gh = dot(rows_geo_ref[...], w_edt)
        rows_out = dot_t(e_hid_ref[...], w_edt)
        rows_out_ref[...] = rows_out
        gc_rows = jnp.sum(rows_g_ref[...] * rows_out, axis=-1, keepdims=True)
        gc_rows = jnp.broadcast_to(gc_rows, gc_acc_ref.shape)

        @pl.when(step == 0)
        def _():
            acc_ref[...] = s_gh
            e_acc_ref[...] = e_gh
            gc_acc_ref[...] = gc_rows

        @pl.when(step > 0)
        def _():
            acc_ref[...] += s_gh
            e_acc_ref[...] += e_gh
            gc_acc_ref[...] += gc_rows

    @pl.when(step == STEPS - 1)
    def _():
        s_gh = acc_ref[...]
        geg_ref[:, :SR] = (s_gh * slope_ref[...]).astype(BF)
        geg_ref[:, SR:] = (s_gh * act_ref[...]).astype(BF)
        e_gh = e_acc_ref[...]
        e_geg_ref[:, :FR] = (e_gh * e_slope_ref[...]).astype(BF)
        e_geg_ref[:, FR:] = (e_gh * e_act_ref[...]).astype(BF)
        gc = scatter_rows(spread_ref[...], gc_acc_ref[...])
        gc_ref[...] = gc
        p = (gc * chosen_ref[...])[:, :NE]
        probs = probs_ref[...]
        first = lax.broadcasted_iota(jnp.int32, probs.shape, 1) == 0
        lg = probs * (jnp.where(first, p, 0.0) - probs[:, :1] * p)
        lg_ref[...] = lg.astype(BF)

    @pl.when(step >= STEPS)
    def _():
        g_n2 = dot_t(geg_ref[...], in_ref[:, : 2 * SR]) + dot_t(lg_ref[...], router_ref[...])
        rows_back = dot_t(e_geg_ref[...], in_ref[:, 2 * SR :])
        total = g_n2 + scatter_rows(spread_ref[...], rows_back)
        for k in range(R):
            part_refs[k][...] = total[k * TOK : (k + 1) * TOK].astype(BF)


def ffn_out_kernel(R, SR, s_hid_ref, rest_ref, spread_ref, rows_w_ref, rows_out_ref, *part_refs):
    total = dot_t(s_hid_ref[...], rest_ref[:, :SR]) + scatter_rows(
        spread_ref[...], rows_w_ref[...] * rows_out_ref[...]
    )
    for k in range(R):
        part_refs[k][...] = total[k * TOK : (k + 1) * TOK].astype(BF)


def add_kernel(hidden_ref, *refs):
    total = hidden_ref[...]
    for ref in refs[:-1]:
        total = total + ref[...].astype(F32)
    refs[-1][...] = total.astype(BF)


def ffn_weight_kernel(SR, FR, n2_ref, geg_ref, rows_in_ref, e_geg_ref, rows_geo_ref, e_hid_ref, out_ref):
    cut = 2 * SR + 2 * FR
    out_ref[:, : 2 * SR] = t_dot(n2_ref[...], geg_ref[...]).astype(BF)
    out_ref[:, 2 * SR : cut] = t_dot(rows_in_ref[...], e_geg_ref[...]).astype(BF)
    out_ref[:, cut : cut + FR] = t_dot(rows_geo_ref[...], e_hid_ref[...]).astype(BF)
    if out_ref.shape[1] > cut + FR:
        out_ref[:, cut + FR :] = jnp.zeros((CHUNK, out_ref.shape[1] - cut - FR), BF)


def product_kernel(left_ref, right_ref, out_ref):
    out_ref[...] = t_dot(left_ref[...], right_ref[...]).astype(BF)


def attention_weight_kernel(R, QW, r_ref, n1_ref, gq_ref, *refs):
    grad_refs, att_refs = refs[:R], refs[R : 2 * R]
    out_ref, ghb_ref, att_ref = refs[2 * R :]
    step = pl.program_id(0)

    @pl.when(step == 0)
    def _():
        for k in range(R):
            ghb_ref[k * TOK : (k + 1) * TOK, :] = grad_refs[k][...]

    for k in range(R):

        @pl.when((r_ref[0] ^ step) == k)
        def _():
            for i in range(R):
                att_ref[i * TOK : (i + 1) * TOK, :] = att_refs[k][
                    (i ^ k) * TOK : ((i ^ k) + 1) * TOK, :
                ]

    out_ref[:, :QW] = t_dot(n1_ref[...], gq_ref[...]).astype(BF)
    out_ref[:, QW:] = t_dot(att_ref[...], ghb_ref[...]).astype(BF)


def tail_kernel(R, HS, HR, KR, LR, NR, r_ref, n1_ref, n2_ref, gd_ref, lg_ref, gains_ref, *refs):
    out_ref = refs[R]
    W, n = DN + DV, HR // HS
    step = pl.program_id(0)
    out_ref[...] = jnp.zeros(out_ref.shape, BF)
    for k in range(R):

        @pl.when((r_ref[0] ^ (step // n)) == k)
        def _():
            for h in range(HS):
                out_ref[h * KR : (h + 1) * KR, :W] = refs[k][(step % n) * HS + h]

    out_ref[:, W : W + LR] = t_dot(n1_ref[...], gd_ref[...]).astype(BF)
    out_ref[:, W + LR : W + LR + NR] = t_dot(n2_ref[...], lg_ref[...]).astype(BF)
    cut = W + LR + NR
    out_ref[: gains_ref.shape[1], cut : cut + 64] = gains_ref[0].astype(BF)


def whole_block(shape):
    return pl.BlockSpec(shape, lambda *_: (0,) * len(shape))


def join_ffn_kernel(R, SR, FR, blocks, gate_ref, up_ref, e_gate_ref, e_up_ref, e_down_ref):
    cut = 2 * SR
    for j in range(R):
        gate_ref[:, j * SR : (j + 1) * SR] = blocks[j, :, :SR].astype(F32)
        up_ref[:, j * SR : (j + 1) * SR] = blocks[j, :, SR:cut].astype(F32)
        e_gate_ref[:, j * FR : (j + 1) * FR] = blocks[j, :, cut : cut + FR].astype(F32)
        e_up_ref[:, j * FR : (j + 1) * FR] = blocks[j, :, cut + FR : cut + 2 * FR].astype(F32)
        e_down = blocks[j, :, cut + 2 * FR : cut + 3 * FR].astype(F32)
        e_down_ref[j * FR : (j + 1) * FR, :] = e_down.T


def join_down_kernel(R, SR, blocks, down_ref):
    for j in range(R):
        down_ref[j * SR : (j + 1) * SR, :] = blocks[j].astype(F32).T


def join_attention_kernel(R, HR, blocks, query_ref, out_ref):
    HN, W, half = HR * DN, DN + DR, DR // 2
    DC = D // R
    for j in range(R):
        for h in range(HR):
            at = (j * HR + h) * W
            one, two = HN + h * half, HN + 128 + h * half
            query_ref[:, at : at + DN] = blocks[j, :, h * DN : (h + 1) * DN].astype(F32)
            query_ref[:, at + DN : at + DN + half] = blocks[j, :, one : one + half].astype(F32)
            query_ref[:, at + DN + half : at + W] = blocks[j, :, two : two + half].astype(F32)
        out_ref[:, j * DC : (j + 1) * DC] = blocks[j, :, HN + 256 :].astype(F32)


def join_tail_kernel(R, HS, KR, LR, blocks, up_ref, down_ref, router_ref):
    W, NR = DN + DV, NE // R
    for j in range(R):
        for h in range(HS):
            up_ref[j * KR : (j + 1) * KR, h * W : (h + 1) * W] = blocks[
                j, h * KR : (h + 1) * KR, :W
            ].astype(F32)
        down_ref[j * LR : (j + 1) * LR, :] = blocks[j, :, W : W + LR].astype(F32).T
        router_ref[j * NR : (j + 1) * NR, :] = blocks[j, :, W + LR : W + LR + NR].astype(F32).T


def join_blocks(kernel, R, r, pieces, outs):
    rows, width = pieces[0][2].shape

    def body(r_ref, *refs):
        block_ref = refs[-1]
        for (k, row, values), ref in zip(pieces, refs):
            block_ref[r_ref[0] ^ k, row : row + values.shape[0], :] = ref[...]
        kernel(block_ref, *refs[len(pieces) : -1])

    return pl.pallas_call(
        body,
        in_specs=[pl.BlockSpec(memory_space=pltpu.SMEM)]
        + [whole_block(values.shape) for _, _, values in pieces],
        out_specs=[whole_block(s) for s in outs],
        out_shape=[jax.ShapeDtypeStruct(s, F32) for s in outs],
        scratch_shapes=[pltpu.VMEM((R, rows, width), BF)],
    )(r.reshape(1), *[values for _, _, values in pieces])


def make_local(R, S):
    DL = D // S
    HR = H // R
    HS = H // S
    KR = KVR // R
    DC = D // R
    FR = FF // R
    SR = SH // R
    LR = (KVR + DR) // R
    NR = NE // R
    T = R * TOK
    QW = HR * DN + 256
    half = DR // 2
    HL = HR * half
    GR = DL // 64
    links = [[(i, i ^ k) for i in range(R)] for k in range(R)]

    def send(values, k):
        return lax.ppermute(values, REP, links[k])

    def gather(values):
        return [values] + [send(values, k) for k in range(1, R)]

    def local(
        hidden_in,
        segment_ids,
        routes,
        norm_gain,
        query_weight,
        kv_down,
        kv_gain,
        kv_up,
        out_weight,
        mixer_gain,
        router_weight,
        shared_gate,
        shared_up,
        shared_down,
        expert_gate,
        expert_up,
        expert_down,
        cotangent,
    ):
        r = lax.axis_index(REP)

        def part(values, width, axis=1):
            return lax.dynamic_slice_in_dim(values, r * width, width, axis)

        def natural(blocks):
            stacked = jnp.stack(blocks)
            return [
                lax.dynamic_index_in_dim(stacked, r ^ j, 0, keepdims=False) for j in range(R)
            ]

        def reduce_parts(parts):
            own = parts[0].astype(F32)
            received = [send(parts[k].astype(BF), k) for k in range(1, R)]
            for part_sum in received:
                own = own + part_sum.astype(F32)
            return own

        def reduce_blocks(total):
            return reduce_parts([total[k * TOK : (k + 1) * TOK] for k in range(R)])

        def gather_pieces(values):
            if R != 4:
                return [(k, 0, block) for k, block in enumerate(gather(values))]
            mid = values.shape[0] // 2
            side, other = send(values, 1), send(values, 2)
            top, low = send(other[:mid], 1), send(side[mid:], 2)
            return [(0, 0, values), (1, 0, side), (2, 0, other), (3, 0, top), (3, mid, low)]

        def shard_gather(values):
            return lax.all_gather(values, SHD, axis=0, tiled=True)

        def shard_reduce(values):
            return lax.psum_scatter(values, SHD, scatter_dimension=0, tiled=True)

        index = jnp.arange(TOK, dtype=jnp.int32)
        same_own = segment_ids[:, None] == segment_ids[None, :]
        start_own = jnp.min(jnp.where(same_own, index[None, :], TOK), axis=1)
        chosen_own = jnp.any(routes == 0, axis=1)
        meta_own = jnp.concatenate(
            [
                start_own.astype(BF)[None],
                chosen_own.astype(BF)[None],
                jnp.zeros((6, TOK), BF),
            ]
        )
        meta = jnp.stack(gather(meta_own))
        x_all = jnp.concatenate(gather(hidden_in))
        cot_all = jnp.concatenate(gather(cotangent))

        CD, CR, CG = QW, QW + KVR + DR, QW + KVR + DR + NE
        CH = -(-(CG + 64) // 128) * 128
        KW = HS * KR * (DN + DV) // DL
        kv_piece = (
            part(kv_up, KR, 0).reshape(KR, HS, DN + DV).transpose(1, 0, 2).reshape(HS * KR, DN + DV)
        )

        def gain_rows(one, two, kv):
            lead = one.shape[:-1]
            pads = [(0, 0)] * len(lead)
            rows = jnp.concatenate(
                [
                    one.reshape(lead + (GR, 64)),
                    two.reshape(lead + (GR, 64)),
                    jnp.pad(kv, pads + [(0, 64 - KVR // S)]).reshape(lead + (1, 64)),
                ],
                axis=-2,
            )
            return jnp.pad(rows, pads + [(0, DL - 2 * GR - 1), (0, 0)])

        q_own = part(query_weight, HR * (DN + DR)).reshape(DL, HR, DN + DR)
        rope_pad = ((0, 0), (0, 128 - HL))
        attn_own = jnp.concatenate(
            [
                q_own[..., :DN].reshape(DL, HR * DN),
                jnp.pad(q_own[..., DN : DN + half].reshape(DL, HL), rope_pad),
                jnp.pad(q_own[..., DN + half :].reshape(DL, HL), rope_pad),
                kv_down,
                router_weight,
                gain_rows(norm_gain, mixer_gain, kv_gain),
                jnp.zeros((DL, CH - CG - 64), BF),
                part(out_weight, DC),
                fold(kv_piece, DL),
            ],
            axis=1,
        )
        attn_all = shard_gather(attn_own)
        head_blocks = []
        for k in range(R):
            piece = lax.dynamic_slice_in_dim(attn_all, (r ^ k) * HR * DV, HR * DV, 0)[:, CH:]
            head_blocks.append(send(piece, k) if k else piece)
        if R == 4:
            out_ws = kvus = head_blocks
            kvu_spec = pl.BlockSpec((HR * KR, DN + DV), lambda i, r_ref: (0, DC // KW))
        else:
            head_nat = natural(head_blocks)
            out_ws = [b[:, :DC] for b in head_nat]
            kvus = [unfold_all(b[:, DC:], S // R, DL, HS * KR) for b in head_nat]
            kvu_spec = whole_block((HR * KR, DN + DV))
        out_w_spec = pl.BlockSpec((HR * DV, DC), lambda i, r_ref: (0, 0))
        r_one = r.reshape(1)
        w_q = attn_all[:, :QW]
        w_down = attn_all[:, CD:CR]
        w_router = attn_all[:, CR:CG]
        gain_all = attn_all[:, CG : CG + 64].reshape(S, DL, 64).astype(F32)
        gain_one = gain_all[:, :GR].reshape(D)
        gain_two = gain_all[:, GR : 2 * GR].reshape(D)
        gain_kv = gain_all[:, 2 * GR, : KVR // S].reshape(KVR)

        in_all = shard_gather(
            jnp.concatenate(
                [
                    part(shared_gate, SR),
                    part(shared_up, SR),
                    part(expert_gate[0], FR),
                    part(expert_up[0], FR),
                ],
                axis=1,
            ),
        )
        w_gu, w_egu = in_all[:, : 2 * SR], in_all[:, 2 * SR :]
        rest_all = shard_gather(
            jnp.concatenate([part(shared_down, SR, 0).T, part(expert_down[0], FR, 0).T], axis=1),
        )

        xf = x_all.astype(F32)
        scale_one = inv_rms(xf)
        n1 = (xf * scale_one * gain_one).astype(BF)
        qlat = dot(n1, attn_all[:, :CH])
        latent = qlat[:, CD : CD + KVR]
        scale_kv = inv_rms(latent)
        lat_n = (latent * scale_kv * gain_kv).astype(BF)

        start = meta[:, 0].astype(F32)
        position = index.astype(F32)[None] - start
        freq = 10000.0 ** (-jnp.arange(half, dtype=F32) / half)
        angles = position.reshape(T, 1) * jnp.tile(freq, 4)[None]
        cosine, sine = jnp.cos(angles), jnp.sin(angles)
        allowed = (start[:, :, None] == start[:, None, :]) & (index[None, :] <= index[:, None])[None]
        bias = jnp.where(allowed, 0.0, NEGATIVE).astype(F32)

        def rows(width, column=0):
            return pl.BlockSpec((TOK, width), lambda i, r_ref: (i, column))

        HN = HR * DN
        probs_spec = pl.BlockSpec((HR, TOK, TOK), lambda i, r_ref: (i, 0, 0))
        forward = pl.pallas_call(
            lambda *refs: attention_kernel(R, HR, *refs),
            grid_spec=pltpu.PrefetchScalarGridSpec(
                num_scalar_prefetch=1,
                grid=(R,),
                in_specs=[
                    rows(QW),
                    rows(128, (CD + KVR) // 128),
                    rows(KVR),
                    rows(128),
                    rows(128),
                    pl.BlockSpec((1, TOK, TOK), lambda i, r_ref: (i, 0, 0)),
                ]
                + [out_w_spec] * R
                + [kvu_spec] * R,
                out_specs=[rows(HN), probs_spec, rows(QW), rows(256), rows(2 * HN)]
                + [whole_block((TOK, D))] * R,
                scratch_shapes=[pltpu.VMEM((TOK, D), BF)],
            ),
            out_shape=[
                jax.ShapeDtypeStruct((T, HN), BF),
                jax.ShapeDtypeStruct((R * HR, TOK, TOK), F32),
                jax.ShapeDtypeStruct((T, QW), BF),
                jax.ShapeDtypeStruct((T, 256), BF),
                jax.ShapeDtypeStruct((T, 2 * HN), BF),
            ]
            + [jax.ShapeDtypeStruct((TOK, D), BF)] * R,
        )
        att, probs, q_b, kr_b, kv, *out_parts = forward(
            r_one, qlat, qlat, lat_n, cosine, sine, bias, *out_ws, *kvus
        )
        x_own = hidden_in.astype(F32)
        hidden = x_own + reduce_parts(out_parts)

        scale_two = inv_rms(hidden)
        n2_own = (hidden * scale_two * gain_two).astype(BF)
        n2 = jnp.concatenate(gather(n2_own))
        att_all = gather(att)
        probs_r = jax.nn.softmax(dot(n2, w_router), axis=-1)
        chosen = meta[:, 1].astype(F32)
        combine = probs_r[:, 0].reshape(R, TOK) * chosen
        place = jnp.cumsum(chosen.astype(jnp.int32), axis=1) - 1
        slots = jnp.arange(CAP, dtype=jnp.int32)
        dispatch = (
            (place[:, None, :] == slots[None, :, None]) & (chosen[:, None, :] > 0.5)
        ).astype(F32)
        dispatch_b = dispatch.astype(BF)
        n2_b = n2.reshape(R, TOK, D)
        cot_b = cot_all.reshape(R, TOK, D)
        rows_in = ein("bct,btd->bcd", dispatch_b, n2_b).astype(BF).reshape(R * CAP, D)
        rows_g = ein("bct,btd->bcd", dispatch_b, cot_b).reshape(R * CAP, D)
        rows_w = jnp.sum(dispatch * combine[:, None, :], axis=-1).reshape(R * CAP, 1)

        pre = dot(n2, w_gu)
        g_pre, u_pre = pre[:, :SR], pre[:, SR:]
        act, slope = silu_parts(g_pre)
        s_hid = (act * u_pre).astype(BF)
        down_part = pl.pallas_call(
            product_kernel,
            grid=(STEPS,),
            in_specs=[pl.BlockSpec((T, CHUNK), lambda i: (0, i)), whole_block((T, SR))],
            out_specs=pl.BlockSpec((CHUNK, SR), lambda i: (i, 0)),
            out_shape=jax.ShapeDtypeStruct((D, SR), BF),
        )(cot_all, s_hid)
        down_red = shard_reduce(down_part)
        e_pre = dot(rows_in, w_egu)
        e_g, e_u = e_pre[:, :FR], e_pre[:, FR:]
        e_act, e_slope = silu_parts(e_g)
        e_hid = (e_act * e_u).astype(BF)
        rows_geo = (rows_w * rows_g).astype(BF)
        slot = (place + CAP * jnp.arange(R)[:, None]).reshape(T, 1)
        spread = (slot == jnp.arange(2 * R * CAP)[None] % (R * CAP)) & (chosen.reshape(T, 1) > 0.5)
        spread = (spread & (place.reshape(T, 1) < CAP)).astype(BF)
        chosen_wide = jnp.broadcast_to(chosen.reshape(T, 1), (T, 128))
        operands = (
            cot_all,
            rest_all,
            in_all,
            act,
            u_pre * slope,
            e_hid,
            e_act,
            e_u * e_slope,
            rows_geo,
            rows_g,
            spread,
            probs_r,
            chosen_wide,
            w_router,
        )
        RC = R * CAP

        def early(i):
            return jnp.minimum(i, STEPS - 1)

        def late(i):
            return jnp.maximum(i - STEPS, 0)

        specs = {
            0: pl.BlockSpec((T, CHUNK), lambda i: (0, early(i))),
            1: pl.BlockSpec((CHUNK, SR + FR), lambda i: (early(i), 0)),
            2: pl.BlockSpec((CHUNK, 2 * SR + 2 * FR), lambda i: (late(i), 0)),
            8: pl.BlockSpec((RC, CHUNK), lambda i: (0, early(i))),
            9: pl.BlockSpec((RC, CHUNK), lambda i: (0, early(i))),
            13: pl.BlockSpec((CHUNK, NE), lambda i: (late(i), 0)),
        }
        shapes = [
            ((T, 2 * SR), BF),
            ((RC, 2 * FR), BF),
            ((RC, D), F32),
            ((T, 128), F32),
        ] + [((TOK, D), BF)] * R
        s_geg, e_geg, rows_out, gc_wide, *gn2_parts = pl.pallas_call(
            lambda *refs: ffn_grad_kernel(R, SR, FR, *refs),
            grid=(2 * STEPS,),
            in_specs=[specs.get(n, whole_block(v.shape)) for n, v in enumerate(operands)],
            out_specs=[
                whole_block(shapes[0][0]),
                whole_block(shapes[1][0]),
                pl.BlockSpec((RC, CHUNK), lambda i: (0, early(i))),
                whole_block(shapes[3][0]),
            ]
            + [pl.BlockSpec((TOK, CHUNK), lambda i: (0, late(i)))] * R,
            out_shape=[jax.ShapeDtypeStruct(s, t) for s, t in shapes],
            scratch_shapes=[
                pltpu.VMEM((T, SR), F32),
                pltpu.VMEM((RC, FR), F32),
                pltpu.VMEM((RC, 128), F32),
                pltpu.VMEM((T, NE), BF),
            ],
        )(*operands)
        gc_part = gc_wide[:, 0].reshape(R, TOK)

        def logits_grad(gc):
            p = (gc * chosen).reshape(T, 1)
            first = (jnp.arange(NE) == 0).astype(F32)[None]
            return (probs_r * (p * first - probs_r[:, :1] * p)).astype(BF)

        gn2 = reduce_parts(gn2_parts)

        def columns(values):
            return pl.BlockSpec((values.shape[0], CHUNK), lambda i: (0, i))

        GW = -(-(2 * SR + 3 * FR) // 128) * 128
        gu_part = pl.pallas_call(
            lambda *refs: ffn_weight_kernel(SR, FR, *refs),
            grid=(STEPS,),
            in_specs=[
                columns(n2),
                whole_block(s_geg.shape),
                columns(rows_in),
                whole_block(e_geg.shape),
                columns(rows_geo),
                whole_block(e_hid.shape),
            ],
            out_specs=pl.BlockSpec((CHUNK, GW), lambda i: (i, 0)),
            out_shape=jax.ShapeDtypeStruct((D, GW), BF),
        )(n2, s_geg, rows_in, e_geg, rows_geo, e_hid)
        gu_red = shard_reduce(gu_part)
        operands = (s_hid, rest_all, spread, rows_w, rows_out)
        specs = {
            1: pl.BlockSpec((CHUNK, SR + FR), lambda i: (i, 0)),
            4: pl.BlockSpec((RC, CHUNK), lambda i: (0, i)),
        }
        out_ffn = pl.pallas_call(
            lambda *refs: ffn_out_kernel(R, SR, *refs),
            grid=(STEPS,),
            in_specs=[specs.get(n, whole_block(v.shape)) for n, v in enumerate(operands)],
            out_specs=[pl.BlockSpec((TOK, CHUNK), lambda i: (0, i))] * R,
            out_shape=[jax.ShapeDtypeStruct((TOK, D), BF)] * R,
        )(*operands)
        out_ffn = [out_ffn[0]] + [send(out_ffn[k], k) for k in range(1, R)]
        result = pl.pallas_call(
            add_kernel, out_shape=jax.ShapeDtypeStruct((TOK, D), BF)
        )(hidden, *out_ffn)
        gc_all = gather(gc_part)
        gc_total = gc_all[0]
        for j in range(1, R):
            gc_total = gc_total + jnp.stack([gc_all[j][k ^ j] for k in range(R)])

        g_mixer = jnp.sum(gn2 * hidden * scale_two, axis=0)
        scaled = gn2 * gain_two
        grad_hidden = (
            cotangent.astype(F32)
            + scale_two * scaled
            - hidden * scale_two**3 * jnp.mean(scaled * hidden, axis=-1, keepdims=True)
        )

        backward = pl.pallas_call(
            lambda *refs: attention_grad_kernel(R, HR, *refs),
            grid_spec=pltpu.PrefetchScalarGridSpec(
                num_scalar_prefetch=1,
                grid=(R,),
                in_specs=[whole_block((TOK, D))] * R
                + [out_w_spec] * R
                + [kvu_spec] * R
                + [
                    rows(HN),
                    probs_spec,
                    rows(2 * HN),
                    rows(QW),
                    rows(256),
                    rows(128),
                    rows(128),
                ],
                out_specs=[rows(QW), rows(2 * HN)] + [whole_block((TOK, KVR + 128))] * R,
                scratch_shapes=[pltpu.VMEM((TOK, D), BF), pltpu.VMEM((TOK, KVR + 128), BF)],
            ),
            out_shape=[
                jax.ShapeDtypeStruct((T, QW), BF),
                jax.ShapeDtypeStruct((T, 2 * HN), BF),
            ]
            + [jax.ShapeDtypeStruct((TOK, KVR + 128), BF)] * R,
        )
        ghb = gather(grad_hidden.astype(BF))
        gq, g_kv, *glat_parts = backward(
            r_one, *ghb, *out_ws, *kvus, att, probs, kv, q_b, kr_b, cosine, sine
        )
        attn_part = pl.pallas_call(
            lambda *refs: attention_weight_kernel(R, QW, *refs),
            grid_spec=pltpu.PrefetchScalarGridSpec(
                num_scalar_prefetch=1,
                grid=(R,),
                in_specs=[
                    pl.BlockSpec((T, DC), lambda i, r_ref: (0, i)),
                    whole_block((T, QW)),
                ]
                + [pl.BlockSpec((TOK, DC), lambda i, r_ref: (0, r_ref[0]))] * R
                + [whole_block((T, HN))] * R,
                out_specs=pl.BlockSpec((DC, QW + DC), lambda i, r_ref: (i, 0)),
                scratch_shapes=[pltpu.VMEM((T, DC), BF), pltpu.VMEM((T, HN), BF)],
            ),
            out_shape=jax.ShapeDtypeStruct((D, QW + DC), BF),
        )(r.reshape(1), n1, gq, *ghb, *att_all)
        glat = reduce_parts(glat_parts)
        latent_own, scale_kv_own = latent[:TOK], scale_kv[:TOK]
        gl_n = glat[:, :KVR]
        g_kvgain = jnp.sum(gl_n * latent_own * scale_kv_own, axis=0)
        lat_scaled = gl_n * gain_kv
        g_latent = scale_kv_own * lat_scaled - latent_own * scale_kv_own**3 * jnp.mean(
            lat_scaled * latent_own, axis=-1, keepdims=True
        )
        gd_own = jnp.concatenate([g_latent, glat[:, KVR : KVR + DR]], axis=1).astype(BF)
        gd = part(jnp.concatenate(gather(gd_own)), LR)
        gn1_part = dot_t(gq, w_q) + dot_t(gd, part(w_down, LR))
        gn1 = reduce_blocks(gn1_part)
        scale_own = scale_one[:TOK]
        scaled_one = gn1 * gain_one
        grad_input = (
            grad_hidden
            + scale_own * scaled_one
            - x_own * scale_own**3 * jnp.mean(scaled_one * x_own, axis=-1, keepdims=True)
        )
        g_norm = jnp.sum(gn1_part * xf * scale_one, axis=0)

        g_kvu = t_dot(lat_n, g_kv).astype(BF).reshape(KVR, HR, DN + DV).transpose(1, 0, 2)
        kvu_blocks = []
        for k in range(R):
            b = lax.dynamic_slice_in_dim(g_kvu, (r ^ k) * KR, KR, 1)
            kvu_blocks.append(send(b, k) if k else b)
        lg = part(logits_grad(gc_total), NR)
        vectors = jnp.concatenate([g_norm, g_mixer, g_kvgain])
        summed = sum(gather(vectors))
        g_gains = gain_rows(
            summed[:D].reshape(S, DL),
            summed[D : 2 * D].reshape(S, DL),
            summed[2 * D :].reshape(S, KVR // S),
        )
        attn_red = shard_reduce(attn_part)
        TW = -(-(KW + LR + NR + 64) // 128) * 128
        if KW == DN + DV:
            tail_part = pl.pallas_call(
                lambda *refs: tail_kernel(R, HS, HR, KR, LR, NR, *refs),
                grid_spec=pltpu.PrefetchScalarGridSpec(
                    num_scalar_prefetch=1,
                    grid=(S,),
                    in_specs=[
                        pl.BlockSpec((T, DL), lambda i, r_ref: (0, i)),
                        pl.BlockSpec((T, DL), lambda i, r_ref: (0, i)),
                        whole_block(gd.shape),
                        whole_block(lg.shape),
                        pl.BlockSpec((1, 16, 64), lambda i, r_ref: (i, 0, 0)),
                    ]
                    + [whole_block((HR, KR, DN + DV))] * R,
                    out_specs=pl.BlockSpec((DL, TW), lambda i, r_ref: (i, 0)),
                ),
                out_shape=jax.ShapeDtypeStruct((D, TW), BF),
            )(r_one, n1, n2, gd, lg, g_gains[:, :16], *kvu_blocks)
        else:
            g_kvu_all = jnp.concatenate(natural(kvu_blocks))
            tail_part = jnp.concatenate(
                [
                    fold_all(g_kvu_all.reshape(H * KR, DN + DV), S, DL),
                    t_dot(n1, gd).astype(BF),
                    t_dot(n2, lg).astype(BF),
                    g_gains.reshape(D, 64).astype(BF),
                    jnp.zeros((D, TW - KW - LR - NR - 64), BF),
                ],
                axis=1,
            )
        tail_red = shard_reduce(tail_part)

        (own_sd,) = join_blocks(
            lambda *refs: join_down_kernel(R, SR, *refs), R, r, gather_pieces(down_red), [(SH, DL)]
        )
        own_sg, own_su, own_eg, own_eu, own_ed = join_blocks(
            lambda *refs: join_ffn_kernel(R, SR, FR, *refs),
            R,
            r,
            gather_pieces(gu_red),
            [(DL, SH), (DL, SH), (DL, FF), (DL, FF), (FF, DL)],
        )
        own_qw, own_ow = join_blocks(
            lambda *refs: join_attention_kernel(R, HR, *refs),
            R,
            r,
            gather_pieces(attn_red),
            [(DL, H * (DN + DR)), (DL, D)],
        )
        tail_pieces = gather(tail_red)
        gains_red = tail_red[:, KW + LR + NR : KW + LR + NR + 64].astype(F32)
        if KW == DN + DV:
            own_ku, own_kd, own_rw = join_blocks(
                lambda *refs: join_tail_kernel(R, HS, KR, LR, *refs),
                R,
                r,
                [(k, 0, block) for k, block in enumerate(tail_pieces)],
                [(KVR, HS * (DN + DV)), (KVR + DR, DL), (NE, DL)],
            )
            own_kd, own_rw = own_kd.T, own_rw.T
        else:
            tail_nat = natural(tail_pieces)
            own_ku = jnp.concatenate(
                [
                    unfold(b[:, :KW], HS * KR)
                    .reshape(HS, KR, DN + DV)
                    .transpose(1, 0, 2)
                    .reshape(KR, HS * (DN + DV))
                    for b in tail_nat
                ]
            ).astype(F32)
            own_kd = jnp.concatenate([b[:, KW : KW + LR] for b in tail_nat], axis=1).astype(F32)
            own_rw = jnp.concatenate([b[:, KW + LR : KW + LR + NR] for b in tail_nat], axis=1).astype(F32)
        return (
            result,
            grad_input,
            gains_red[:GR].reshape(DL),
            own_qw,
            own_kd,
            gains_red[2 * GR, : KVR // S],
            own_ku,
            own_ow,
            gains_red[GR : 2 * GR].reshape(DL),
            own_rw,
            own_sg,
            own_su,
            own_sd,
            own_eg[None],
            own_eu[None],
            own_ed[None],
        )

    return local


def unfold_all(values, S, DL, rows):
    _, c = values.shape
    f = DL // rows
    if f <= 1:
        return values
    return values.reshape(S, f, rows, c).transpose(0, 2, 1, 3).reshape(S * rows, f * c)


def fold_all(values, S, DL):
    n, c = values.shape
    f = S * DL // n
    if f <= 1:
        return values
    return values.reshape(S, n // S, f, c // f).transpose(0, 2, 1, 3).reshape(S * DL, c // f)


def solution(mesh):
    tokens = P((REP, SHD), None)
    rows, cols = P(SHD, None), P(None, SHD)
    placed = (
        tokens,
        P((REP, SHD)),
        tokens,
        P(SHD),
        rows,
        rows,
        P(SHD),
        cols,
        rows,
        P(SHD),
        rows,
        rows,
        rows,
        cols,
        P(None, SHD, None),
        P(None, SHD, None),
        P(None, None, SHD),
        tokens,
    )
    outs = (tokens, tokens) + placed[3:17]
    body = make_local(mesh.shape[REP], mesh.shape[SHD])

    return jax.shard_map(
        body,
        mesh=mesh,
        in_specs=placed,
        out_specs=outs,
        check_vma=False,
    )
```

```python
import jax
import jax.numpy as jnp
from jax import lax
from jax.experimental import pallas as pl
from jax.experimental.pallas import tpu as pltpu
from jax.sharding import PartitionSpec as P

D = 2048
H = 16
DN = 128
DR = 64
DV = 128
KVR = 512
NE = 64
CAP = 16
FF = 1408
SH = 2816
TOK = 128

EPSILON = 1e-06
NEGATIVE = -1e30
BF = jnp.bfloat16
F32 = jnp.float32
SCALE = (DN + DR) ** (-0.5)


def dot(left, right):
    return jnp.dot(left, right, preferred_element_type=F32)


def dot_t(left, right):
    return lax.dot_general(left, right, (((1,), (1,)), ((), ())), preferred_element_type=F32)


def t_dot(left, right):
    return lax.dot_general(left, right, (((0,), (0,)), ((), ())), preferred_element_type=F32)


def inv_rms(values):
    return lax.rsqrt(jnp.mean(values * values, axis=-1, keepdims=True) + EPSILON)


def silu_parts(pre_act):
    sigmoid_val = jax.nn.sigmoid(pre_act)
    return (pre_act * sigmoid_val, sigmoid_val * (1.0 + pre_act * (1.0 - sigmoid_val)))


def fold(values, rows):
    n, c = values.shape
    f = rows // n
    if f <= 1:
        return values
    return values.reshape(n, f, c // f).transpose(1, 0, 2).reshape(rows, c // f)


def unfold(values, rows):
    n, c = values.shape
    f = n // rows
    if f <= 1:
        return values
    return values.reshape(f, rows, c).transpose(1, 0, 2).reshape(rows, f * c)


def roll_sum(values):
    values = values + pltpu.roll(values, 64, 1)
    return values + pltpu.roll(values, 32, 1)


def lane_index():
    return lax.broadcasted_iota(jnp.int32, (TOK, 128), 1)


def block_at(R, r_ref, k, width):
    if R != 4:
        return slice(k * width, (k + 1) * width)
    return pl.ds(pl.multiple_of((r_ref[0] ^ k) * width, width), width)


def attention_kernel(R, HR, r_ref, q_ref, rope_ref, lat_ref, cos_ref, sin_ref, bias_ref, *refs):
    out_w_refs, kvu_refs = refs[:R], refs[R : 2 * R]
    att_ref, probs_ref, qb_ref, krb_ref, kv_ref = refs[2 * R : 2 * R + 5]
    part_refs, sum_ref = refs[2 * R + 5 : 3 * R + 5], refs[-1]
    HN, KR, W = HR * DN, KVR // R, DN + DV
    lats = [lat_ref[:, block_at(R, r_ref, k, KR)] for k in range(R)]
    for h in range(HR):
        total = dot(lats[0], kvu_refs[0][h * KR : (h + 1) * KR, :])
        for k in range(1, R):
            total = total + dot(lats[k], kvu_refs[k][h * KR : (h + 1) * KR, :])
        kv_ref[:, h * W : (h + 1) * W] = total.astype(BF)
    lane = lane_index()
    cos, sin = cos_ref[...], sin_ref[...]
    rope = rope_ref[...]
    k_1 = roll_sum(jnp.where(lane < 32, rope, 0.0))
    k_2 = roll_sum(jnp.where((lane >= 32) & (lane < 64), rope, 0.0))
    kr_1 = (k_1 * cos - k_2 * sin).astype(BF)
    kr_2 = (k_2 * cos + k_1 * sin).astype(BF)
    krb_ref[:, :128] = kr_1
    krb_ref[:, 128:] = kr_2
    q_1, q_2 = q_ref[:, HN : HN + 128], q_ref[:, HN + 128 :]
    qr_1 = (q_1 * cos - q_2 * sin) * SCALE
    qr_2 = (q_2 * cos + q_1 * sin) * SCALE
    q_n = (q_ref[:, :HN] * SCALE).astype(BF)
    qb_ref[:, :HN] = q_n
    qb_ref[:, HN : HN + 128] = qr_1.astype(BF)
    qb_ref[:, HN + 128 :] = qr_2.astype(BF)
    bias = bias_ref[0]
    for h in range(HR):
        head = (lane >= 32 * h) & (lane < 32 * h + 32)
        scores = (
            dot_t(q_n[:, h * DN : (h + 1) * DN], kv_ref[:, h * W : h * W + DN])
            + dot_t(jnp.where(head, qr_1, 0.0).astype(BF), kr_1)
            + dot_t(jnp.where(head, qr_2, 0.0).astype(BF), kr_2)
            + bias
        )
        expd = jnp.exp(scores - jnp.max(scores, axis=-1, keepdims=True))
        probs = expd / jnp.sum(expd, axis=-1, keepdims=True)
        probs_ref[h] = probs
        value = kv_ref[:, h * W + DN : (h + 1) * W]
        att_ref[:, h * DV : (h + 1) * DV] = dot(probs.astype(BF), value).astype(BF)
    att = att_ref[...]
    for k in range(R):
        sum_ref[:, block_at(R, r_ref, k, D // R)] = dot(att, out_w_refs[k][...]).astype(BF)
    for k in range(R):

        @pl.when(pl.program_id(0) == k)
        def _():
            part_refs[k][...] = sum_ref[...]


def attention_grad_kernel(R, HR, r_ref, *refs):
    grad_refs, out_w_refs, kvu_refs = refs[:R], refs[R : 2 * R], refs[2 * R : 3 * R]
    (att_ref, probs_ref, kv_ref, qb_ref, krb_ref, cos_ref, sin_ref,
     gq_ref, gkv_ref) = refs[3 * R : 3 * R + 9]
    glat_refs = refs[3 * R + 9 : 4 * R + 9]
    ghb_ref, lat_ref = refs[4 * R + 9 :]
    HN, KR, W = HR * DN, KVR // R, DN + DV
    step = pl.program_id(0)
    for k in range(R):

        @pl.when(step == k)
        def _():
            ghb_ref[...] = grad_refs[k][...]

    g_att = dot_t(ghb_ref[:, block_at(R, r_ref, 0, D // R)], out_w_refs[0][...])
    for k in range(1, R):
        g_att = g_att + dot_t(ghb_ref[:, block_at(R, r_ref, k, D // R)], out_w_refs[k][...])
    g_att = g_att.astype(BF)
    lane = lane_index()
    cos, sin = cos_ref[...], sin_ref[...]
    kr_1, kr_2 = krb_ref[:, :128], krb_ref[:, 128:]
    qr_1 = qb_ref[:, HN : HN + 128].astype(F32)
    qr_2 = qb_ref[:, HN + 128 :].astype(F32)
    zero = jnp.zeros((TOK, 128), F32)
    gq_1, gq_2, gk_1, gk_2 = zero, zero, zero, zero
    for h in range(HR):
        cut = slice(h * DN, (h + 1) * DN)
        key, value = slice(h * W, h * W + DN), slice(h * W + DN, (h + 1) * W)
        head = (lane >= 32 * h) & (lane < 32 * h + 32)
        ga = g_att[:, cut]
        probs = probs_ref[h]
        gkv_ref[:, value] = t_dot(probs.astype(BF), ga).astype(BF)
        delta = jnp.sum(ga.astype(F32) * att_ref[:, cut].astype(F32), axis=-1, keepdims=True)
        gs = (probs * (dot_t(ga, kv_ref[:, value]) - delta)).astype(BF)
        gq_ref[:, cut] = (dot(gs, kv_ref[:, key]) * SCALE).astype(BF)
        gq_1 = gq_1 + jnp.where(head, dot(gs, kr_1), 0.0)
        gq_2 = gq_2 + jnp.where(head, dot(gs, kr_2), 0.0)
        gkv_ref[:, key] = t_dot(gs, qb_ref[:, cut]).astype(BF)
        gk_1 = gk_1 + t_dot(gs, jnp.where(head, qr_1, 0.0).astype(BF))
        gk_2 = gk_2 + t_dot(gs, jnp.where(head, qr_2, 0.0).astype(BF))
    gq_ref[:, HN : HN + 128] = ((gq_1 * cos + gq_2 * sin) * SCALE).astype(BF)
    gq_ref[:, HN + 128 :] = ((gq_2 * cos - gq_1 * sin) * SCALE).astype(BF)
    u_1, u_2 = roll_sum(gk_1), roll_sum(gk_2)
    r_1, r_2 = u_1 * cos + u_2 * sin, u_2 * cos - u_1 * sin
    g_rope = jnp.where(lane < 32, r_1, jnp.where(lane < 64, r_2, 0.0)).astype(BF)
    lat_ref[:, KVR:] = g_rope
    for k in range(R):
        total = dot_t(gkv_ref[:, :W], kvu_refs[k][:KR, :])
        for h in range(1, HR):
            total = total + dot_t(
                gkv_ref[:, h * W : (h + 1) * W], kvu_refs[k][h * KR : (h + 1) * KR, :]
            )
        lat_ref[:, block_at(R, r_ref, k, KR)] = total.astype(BF)
    for k in range(R):

        @pl.when(step == k)
        def _():
            glat_refs[k][...] = lat_ref[...]


def scatter_rows(spread, rows):
    high = rows.astype(BF)
    low = (rows - high.astype(F32)).astype(BF)
    return dot(spread, jnp.concatenate([high, low], axis=0))


REP, SHD = "replica", "shard"


STEPS = 4
CHUNK = D // STEPS


def add_step(step, ref, value):
    @pl.when(step == 0)
    def _():
        ref[...] = value

    @pl.when(step > 0)
    def _():
        ref[...] += value


def ffn_in_kernel(R, SR, FR, *refs):
    (in_ref, router_ref, pick_ref, chosen_ref, rows_g_ref, n2_ref, rows_in_ref, act_ref, slope_ref,
     s_hid_ref, e_act_ref, e_slope_ref, e_hid_ref, probs_ref, rows_w_ref, rows_geo_ref, acc_ref,
     e_acc_ref, logits_ref) = refs[R:]
    step = pl.program_id(0)
    for k in range(R):
        n2_ref[k * TOK : (k + 1) * TOK, :] = refs[k][...]
    n2 = n2_ref[...]
    rows_in = dot(pick_ref[...], n2).astype(BF)
    rows_in_ref[...] = rows_in
    add_step(step, acc_ref, dot(n2, in_ref[:, : 2 * SR]))
    add_step(step, e_acc_ref, dot(rows_in, in_ref[:, 2 * SR : 2 * SR + 2 * FR]))
    add_step(step, logits_ref, dot(n2, router_ref[:, 128 - NE :]))

    @pl.when(step == STEPS - 1)
    def _():
        up = acc_ref[:, SR:]
        act, slope = silu_parts(acc_ref[:, :SR])
        act_ref[...] = act
        slope_ref[...] = slope * up
        s_hid_ref[...] = (act * up).astype(BF)
        e_up = e_acc_ref[:, FR:]
        e_act, e_slope = silu_parts(e_acc_ref[:, :FR])
        e_act_ref[...] = e_act
        e_slope_ref[...] = e_slope * e_up
        e_hid_ref[...] = (e_act * e_up).astype(BF)
        logits = logits_ref[...]
        expd = jnp.exp(logits - jnp.max(logits, axis=-1, keepdims=True))
        probs = expd / jnp.sum(expd, axis=-1, keepdims=True)
        probs_ref[...] = probs
        combine = probs[:, :1] * chosen_ref[...]
        high = combine.astype(BF)
        low = (combine - high.astype(F32)).astype(BF)
        rows_w = dot(pick_ref[...], high) + dot(pick_ref[...], low)
        rows_w_ref[...] = rows_w
        rows_geo_ref[...] = (rows_w[:, :1] * rows_g_ref[...]).astype(BF)


def ffn_grad_kernel(SR, FR, EX, cot_ref, rest_ref, more_ref, act_ref, slope_ref, e_hid_ref, e_act_ref,
                    e_slope_ref, rows_geo_ref, rows_g_ref, spread_ref, probs_ref, chosen_ref,
                    geg_ref, e_geg_ref, rows_out_ref, gc_ref, lg_ref, acc_ref, e_acc_ref,
                    gc_acc_ref):
    step = pl.program_id(0)
    FM, at = FR - EX, (2 * SR + 2 * FR) % 128
    w_edt, w_more = rest_ref[:, SR:], more_ref[:, at : at + EX]
    geo = rows_geo_ref[...]
    add_step(step, acc_ref, dot(cot_ref[...], rest_ref[:, :SR]))
    add_step(step, e_acc_ref.at[:, :FM], dot(geo, w_edt))
    add_step(step, e_acc_ref.at[:, FM:], dot(geo, w_more))
    rows_out = dot_t(e_hid_ref[:, :FM], w_edt) + dot_t(e_hid_ref[:, FM:], w_more)
    rows_out_ref[...] = rows_out
    gc_rows = jnp.sum(rows_g_ref[...] * rows_out, axis=-1, keepdims=True)
    add_step(step, gc_acc_ref, jnp.broadcast_to(gc_rows, gc_acc_ref.shape))

    @pl.when(step == STEPS - 1)
    def _():
        s_gh = acc_ref[...]
        geg_ref[:, :SR] = (s_gh * slope_ref[...]).astype(BF)
        geg_ref[:, SR:] = (s_gh * act_ref[...]).astype(BF)
        e_gh = e_acc_ref[...]
        e_geg_ref[:, :FR] = (e_gh * e_slope_ref[...]).astype(BF)
        e_geg_ref[:, FR:] = (e_gh * e_act_ref[...]).astype(BF)
        gc = scatter_rows(spread_ref[...], gc_acc_ref[...])
        gc_ref[...] = gc
        p = (gc * chosen_ref[...])[:, :NE]
        probs = probs_ref[...]
        first = lax.broadcasted_iota(jnp.int32, probs.shape, 1) == 0
        lg = probs * (jnp.where(first, p, 0.0) - probs[:, :1] * p)
        lg_ref[...] = lg.astype(BF)


def ffn_n2_kernel(R, SR, geg_ref, e_geg_ref, lg_ref, spread_ref, in_ref, router_ref, *part_refs):
    total = dot_t(geg_ref[...], in_ref[:, : 2 * SR]) + dot_t(lg_ref[...], router_ref[:, 128 - NE :])
    rows_back = dot_t(e_geg_ref[...], in_ref[:, 2 * SR : 2 * SR + e_geg_ref.shape[1]])
    total = total + scatter_rows(spread_ref[...], rows_back)
    for k in range(R):
        part_refs[k][...] = total[k * TOK : (k + 1) * TOK].astype(BF)


def ffn_out_kernel(R, SR, s_hid_ref, rest_ref, spread_ref, rows_w_ref, rows_out_ref, *part_refs):
    total = dot_t(s_hid_ref[...], rest_ref[:, :SR]) + scatter_rows(
        spread_ref[...], rows_w_ref[:, :1] * rows_out_ref[...]
    )
    for k in range(R):
        part_refs[k][...] = total[k * TOK : (k + 1) * TOK].astype(BF)


def add_kernel(hidden_ref, *refs):
    total = hidden_ref[...]
    for ref in refs[:-1]:
        total = total + ref[...].astype(F32)
    refs[-1][...] = total.astype(BF)


def ffn_weight_kernel(SR, FR, n2_ref, geg_ref, rows_in_ref, e_geg_ref, rows_geo_ref, e_hid_ref, out_ref):
    cut = 2 * SR + 2 * FR
    out_ref[:, : 2 * SR] = t_dot(n2_ref[...], geg_ref[...]).astype(BF)
    out_ref[:, 2 * SR : cut] = t_dot(rows_in_ref[...], e_geg_ref[...]).astype(BF)
    out_ref[:, cut : cut + FR] = t_dot(rows_geo_ref[...], e_hid_ref[...]).astype(BF)
    if out_ref.shape[1] > cut + FR:
        out_ref[:, cut + FR :] = jnp.zeros((CHUNK, out_ref.shape[1] - cut - FR), BF)


def product_kernel(left_ref, right_ref, out_ref):
    out_ref[...] = t_dot(left_ref[...], right_ref[...]).astype(BF)


def attention_weight_kernel(R, QW, r_ref, n1_ref, gq_ref, *refs):
    grad_refs, att_refs = refs[:R], refs[R : 2 * R]
    out_ref, ghb_ref, att_ref = refs[2 * R :]
    step = pl.program_id(0)

    @pl.when(step == 0)
    def _():
        for k in range(R):
            ghb_ref[k * TOK : (k + 1) * TOK, :] = grad_refs[k][...]

    for k in range(R):

        @pl.when((r_ref[0] ^ step) == k)
        def _():
            for i in range(R):
                att_ref[i * TOK : (i + 1) * TOK, :] = att_refs[k][
                    (i ^ k) * TOK : ((i ^ k) + 1) * TOK, :
                ]

    out_ref[:, :QW] = t_dot(n1_ref[...], gq_ref[...]).astype(BF)
    out_ref[:, QW:] = t_dot(att_ref[...], ghb_ref[...]).astype(BF)


def tail_kernel(R, HS, HR, KR, LR, NR, r_ref, n1_ref, n2_ref, gd_ref, lg_ref, gains_ref, *refs):
    out_ref = refs[R]
    W, n = DN + DV, HR // HS
    step = pl.program_id(0)
    out_ref[...] = jnp.zeros(out_ref.shape, BF)
    for k in range(R):

        @pl.when((r_ref[0] ^ (step // n)) == k)
        def _():
            for h in range(HS):
                out_ref[h * KR : (h + 1) * KR, :W] = refs[k][(step % n) * HS + h]

    out_ref[:, W : W + LR] = t_dot(n1_ref[...], gd_ref[...]).astype(BF)
    out_ref[:, W + LR : W + LR + NR] = t_dot(n2_ref[...], lg_ref[...]).astype(BF)
    cut = W + LR + NR
    out_ref[: gains_ref.shape[1], cut : cut + 64] = gains_ref[0].astype(BF)


def whole_block(shape):
    return pl.BlockSpec(shape, lambda *_: (0,) * len(shape))


def join_ffn_kernel(R, SR, FR, blocks, gate_ref, up_ref, e_gate_ref, e_up_ref, e_down_ref):
    cut = 2 * SR
    for j in range(R):
        gate_ref[:, j * SR : (j + 1) * SR] = blocks[j, :, :SR].astype(F32)
        up_ref[:, j * SR : (j + 1) * SR] = blocks[j, :, SR:cut].astype(F32)
        e_gate_ref[:, j * FR : (j + 1) * FR] = blocks[j, :, cut : cut + FR].astype(F32)
        e_up_ref[:, j * FR : (j + 1) * FR] = blocks[j, :, cut + FR : cut + 2 * FR].astype(F32)
        e_down = blocks[j, :, cut + 2 * FR : cut + 3 * FR].astype(F32)
        e_down_ref[j * FR : (j + 1) * FR, :] = e_down.T


def join_down_kernel(R, SR, blocks, down_ref):
    for j in range(R):
        down_ref[j * SR : (j + 1) * SR, :] = blocks[j].astype(F32).T


def join_attention_kernel(R, HR, blocks, query_ref, out_ref):
    HN, W, half = HR * DN, DN + DR, DR // 2
    DC = D // R
    for j in range(R):
        for h in range(HR):
            at = (j * HR + h) * W
            one, two = HN + h * half, HN + 128 + h * half
            query_ref[:, at : at + DN] = blocks[j, :, h * DN : (h + 1) * DN].astype(F32)
            query_ref[:, at + DN : at + DN + half] = blocks[j, :, one : one + half].astype(F32)
            query_ref[:, at + DN + half : at + W] = blocks[j, :, two : two + half].astype(F32)
        out_ref[:, j * DC : (j + 1) * DC] = blocks[j, :, HN + 256 :].astype(F32)


def join_tail_kernel(R, HS, KR, LR, blocks, up_ref, down_ref, router_ref):
    W, NR = DN + DV, NE // R
    for j in range(R):
        for h in range(HS):
            up_ref[j * KR : (j + 1) * KR, h * W : (h + 1) * W] = blocks[
                j, h * KR : (h + 1) * KR, :W
            ].astype(F32)
        down_ref[j * LR : (j + 1) * LR, :] = blocks[j, :, W : W + LR].astype(F32).T
        router_ref[j * NR : (j + 1) * NR, :] = blocks[j, :, W + LR : W + LR + NR].astype(F32).T


def join_blocks(kernel, R, r, pieces, outs):
    rows, width = pieces[0][2].shape

    def body(r_ref, *refs):
        block_ref = refs[-1]
        for (k, row, values), ref in zip(pieces, refs):
            block_ref[r_ref[0] ^ k, row : row + values.shape[0], :] = ref[...]
        kernel(block_ref, *refs[len(pieces) : -1])

    return pl.pallas_call(
        body,
        in_specs=[pl.BlockSpec(memory_space=pltpu.SMEM)]
        + [whole_block(values.shape) for _, _, values in pieces],
        out_specs=[whole_block(s) for s in outs],
        out_shape=[jax.ShapeDtypeStruct(s, F32) for s in outs],
        scratch_shapes=[pltpu.VMEM((R, rows, width), BF)],
    )(r.reshape(1), *[values for _, _, values in pieces])


def make_local(R, S):
    DL = D // S
    HR = H // R
    HS = H // S
    KR = KVR // R
    DC = D // R
    FR = FF // R
    SR = SH // R
    LR = (KVR + DR) // R
    NR = NE // R
    T = R * TOK
    QW = HR * DN + 256
    half = DR // 2
    HL = HR * half
    GR = DL // 64
    links = [[(i, i ^ k) for i in range(R)] for k in range(R)]

    def send(values, k):
        return lax.ppermute(values, REP, links[k])

    def gather(values):
        return [values] + [send(values, k) for k in range(1, R)]

    def local(
        hidden_in,
        segment_ids,
        routes,
        norm_gain,
        query_weight,
        kv_down,
        kv_gain,
        kv_up,
        out_weight,
        mixer_gain,
        router_weight,
        shared_gate,
        shared_up,
        shared_down,
        expert_gate,
        expert_up,
        expert_down,
        cotangent,
    ):
        r = lax.axis_index(REP)

        def part(values, width, axis=1):
            return lax.dynamic_slice_in_dim(values, r * width, width, axis)

        def natural(blocks):
            stacked = jnp.stack(blocks)
            return [
                lax.dynamic_index_in_dim(stacked, r ^ j, 0, keepdims=False) for j in range(R)
            ]

        def reduce_parts(parts):
            own = parts[0].astype(F32)
            received = [send(parts[k].astype(BF), k) for k in range(1, R)]
            for part_sum in received:
                own = own + part_sum.astype(F32)
            return own

        def reduce_blocks(total):
            return reduce_parts([total[k * TOK : (k + 1) * TOK] for k in range(R)])

        def gather_pieces(values):
            if R != 4:
                return [(k, 0, block) for k, block in enumerate(gather(values))]
            mid = values.shape[0] // 2
            side, other = send(values, 1), send(values, 2)
            top, low = send(other[:mid], 1), send(side[mid:], 2)
            return [(0, 0, values), (1, 0, side), (2, 0, other), (3, 0, top), (3, mid, low)]

        def shard_gather(values):
            return lax.all_gather(values, SHD, axis=0, tiled=True)

        def shard_reduce(values):
            return lax.psum_scatter(values, SHD, scatter_dimension=0, tiled=True)

        index = jnp.arange(TOK, dtype=jnp.int32)
        same_own = segment_ids[:, None] == segment_ids[None, :]
        start_own = jnp.min(jnp.where(same_own, index[None, :], TOK), axis=1)
        chosen_own = jnp.any(routes == 0, axis=1)
        meta_own = jnp.concatenate(
            [
                start_own.astype(BF)[None],
                chosen_own.astype(BF)[None],
                jnp.zeros((6, TOK), BF),
            ]
        )
        meta = jnp.stack(gather(meta_own))
        x_all = jnp.concatenate(gather(hidden_in))
        cot_all = jnp.concatenate(gather(cotangent))

        CD, CR, CG = QW, QW + KVR + DR, QW + KVR + DR + NE
        CH = -(-CG // 128) * 128
        KW = HS * KR * (DN + DV) // DL
        kv_piece = (
            part(kv_up, KR, 0).reshape(KR, HS, DN + DV).transpose(1, 0, 2).reshape(HS * KR, DN + DV)
        )

        def gain_rows(one, two, kv):
            lead = one.shape[:-1]
            pads = [(0, 0)] * len(lead)
            rows = jnp.concatenate(
                [
                    one.reshape(lead + (GR, 64)),
                    two.reshape(lead + (GR, 64)),
                    jnp.pad(kv, pads + [(0, 64 - KVR // S)]).reshape(lead + (1, 64)),
                ],
                axis=-2,
            )
            return jnp.pad(rows, pads + [(0, DL - 2 * GR - 1), (0, 0)])

        q_own = part(query_weight, HR * (DN + DR)).reshape(DL, HR, DN + DR)
        rope_pad = ((0, 0), (0, 128 - HL))
        attn_own = jnp.concatenate(
            [
                q_own[..., :DN].reshape(DL, HR * DN),
                jnp.pad(q_own[..., DN : DN + half].reshape(DL, HL), rope_pad),
                jnp.pad(q_own[..., DN + half :].reshape(DL, HL), rope_pad),
                kv_down,
                router_weight,
                *([jnp.zeros((DL, CH - CG), BF)] if CH > CG else []),
                part(out_weight, DC),
                fold(kv_piece, DL),
            ],
            axis=1,
        )
        attn_all = shard_gather(attn_own)
        head_blocks = []
        for k in range(R):
            piece = lax.dynamic_slice_in_dim(attn_all, (r ^ k) * HR * DV, HR * DV, 0)[:, CH:]
            head_blocks.append(send(piece, k) if k else piece)
        if R == 4:
            out_ws = kvus = head_blocks
            kvu_spec = pl.BlockSpec((HR * KR, DN + DV), lambda i, r_ref: (0, DC // KW))
        else:
            head_nat = natural(head_blocks)
            out_ws = [b[:, :DC] for b in head_nat]
            kvus = [unfold_all(b[:, DC:], S // R, DL, HS * KR) for b in head_nat]
            kvu_spec = whole_block((HR * KR, DN + DV))
        out_w_spec = pl.BlockSpec((HR * DV, DC), lambda i, r_ref: (0, 0))
        r_one = r.reshape(1)
        w_q = attn_all[:, :QW]
        gain_own = jnp.concatenate([norm_gain, mixer_gain, kv_gain])
        shard = lax.axis_index(SHD)
        gain_got = [gain_own] + [
            lax.ppermute(gain_own, SHD, [(i, i ^ j) for i in range(S)]) for j in range(1, S)
        ]
        gain_got = jnp.stack(gain_got).astype(F32)
        gain_all = jnp.concatenate(
            [lax.dynamic_index_in_dim(gain_got, shard ^ j, 0) for j in range(S)]
        )
        gain_one = gain_all[:, :DL].reshape(D)
        gain_two = gain_all[:, DL : 2 * DL].reshape(D)
        gain_kv = gain_all[:, 2 * DL :].reshape(KVR)

        EX = (SR + FR) % 128
        down_t = jnp.concatenate([part(shared_down, SR, 0).T, part(expert_down[0], FR, 0).T], axis=1)
        in_all = shard_gather(
            jnp.concatenate(
                [
                    part(shared_gate, SR),
                    part(shared_up, SR),
                    part(expert_gate[0], FR),
                    part(expert_up[0], FR),
                    down_t[:, SR + FR - EX :],
                ],
                axis=1,
            ),
        )
        rest_all = shard_gather(down_t[:, : SR + FR - EX])

        xf = x_all.astype(F32)
        scale_one = inv_rms(xf)
        n1 = (xf * scale_one * gain_one).astype(BF)
        qlat = dot(n1, attn_all[:, :CH])
        latent = qlat[:, CD : CD + KVR]
        scale_kv = inv_rms(latent)
        lat_n = (latent * scale_kv * gain_kv).astype(BF)

        start = meta[:, 0].astype(F32)
        position = index.astype(F32)[None] - start
        freq = 10000.0 ** (-jnp.arange(half, dtype=F32) / half)
        angles = position.reshape(T, 1) * jnp.tile(freq, 4)[None]
        cosine, sine = jnp.cos(angles), jnp.sin(angles)
        allowed = (start[:, :, None] == start[:, None, :]) & (index[None, :] <= index[:, None])[None]
        bias = jnp.where(allowed, 0.0, NEGATIVE).astype(F32)

        def rows(width, column=0):
            return pl.BlockSpec((TOK, width), lambda i, r_ref: (i, column))

        HN = HR * DN
        probs_spec = pl.BlockSpec((HR, TOK, TOK), lambda i, r_ref: (i, 0, 0))
        forward = pl.pallas_call(
            lambda *refs: attention_kernel(R, HR, *refs),
            grid_spec=pltpu.PrefetchScalarGridSpec(
                num_scalar_prefetch=1,
                grid=(R,),
                in_specs=[
                    rows(QW),
                    rows(128, (CD + KVR) // 128),
                    rows(KVR),
                    rows(128),
                    rows(128),
                    pl.BlockSpec((1, TOK, TOK), lambda i, r_ref: (i, 0, 0)),
                ]
                + [out_w_spec] * R
                + [kvu_spec] * R,
                out_specs=[rows(HN), probs_spec, rows(QW), rows(256), rows(2 * HN)]
                + [whole_block((TOK, D))] * R,
                scratch_shapes=[pltpu.VMEM((TOK, D), BF)],
            ),
            out_shape=[
                jax.ShapeDtypeStruct((T, HN), BF),
                jax.ShapeDtypeStruct((R * HR, TOK, TOK), F32),
                jax.ShapeDtypeStruct((T, QW), BF),
                jax.ShapeDtypeStruct((T, 256), BF),
                jax.ShapeDtypeStruct((T, 2 * HN), BF),
            ]
            + [jax.ShapeDtypeStruct((TOK, D), BF)] * R,
        )
        att, probs, q_b, kr_b, kv, *out_parts = forward(
            r_one, qlat, qlat, lat_n, cosine, sine, bias, *out_ws, *kvus
        )
        x_own = hidden_in.astype(F32)
        hidden = x_own + reduce_parts(out_parts)

        scale_two = inv_rms(hidden)
        n2_own = (hidden * scale_two * gain_two).astype(BF)
        n2_blocks = gather(n2_own)
        att_all = gather(att)
        RC = R * CAP
        chosen = meta[:, 1].astype(F32)
        place = jnp.cumsum(chosen.astype(jnp.int32), axis=1) - 1
        slot = place + CAP * jnp.arange(R)[:, None]
        slot = jnp.where((chosen > 0.5) & (place < CAP), slot, -1).reshape(T)
        pick = (jnp.arange(RC)[:, None] == slot[None]).astype(BF)
        spread = (slot[:, None] == jnp.arange(2 * RC)[None] % RC).astype(BF)
        chosen_wide = jnp.broadcast_to(chosen.reshape(T, 1), (T, 128))
        rows_g = dot(pick, cot_all)

        def call(kernel, operands, specs, outs, scratch=()):
            return pl.pallas_call(
                kernel,
                grid=(STEPS,),
                in_specs=[specs.get(n, whole_block(v.shape)) for n, v in enumerate(operands)],
                out_specs=[
                    pl.BlockSpec((h, CHUNK), lambda i: (0, i))
                    if w == D
                    else whole_block((h, abs(w)))
                    for h, w, _ in outs
                ],
                out_shape=[jax.ShapeDtypeStruct((h, abs(w)), t) for h, w, t in outs],
                scratch_shapes=[pltpu.VMEM(shape, F32) for shape in scratch],
            )(*operands)

        def columns(values):
            return pl.BlockSpec((values.shape[0], CHUNK), lambda i: (0, i))

        def chunk_rows(width, column=0):
            return pl.BlockSpec((CHUNK, width), lambda i: (i, column))

        w_in_spec, router_spec = chunk_rows(2 * SR + 2 * FR + EX), chunk_rows(128, CR // 128)
        more_spec = chunk_rows(128, (2 * SR + 2 * FR) // 128)
        (
            n2, rows_in, act, slope_up, s_hid, e_act, e_slope_up, e_hid, probs_r, rows_w, rows_geo
        ) = call(
            lambda *refs: ffn_in_kernel(R, SR, FR, *refs),
            (*n2_blocks, in_all, attn_all, pick, chosen_wide, rows_g),
            {**{k: columns(n2_own) for k in range(R)}, R: w_in_spec, R + 1: router_spec},
            [
                (T, D, BF), (RC, D, BF), (T, SR, F32), (T, SR, F32), (T, SR, BF), (RC, FR, F32),
                (RC, FR, F32), (RC, FR, BF), (T, NE, F32), (RC, 128, F32), (RC, -D, BF),
            ],
            [(T, 2 * SR), (RC, 2 * FR), (T, NE)],
        )

        down_part = pl.pallas_call(
            product_kernel,
            grid=(STEPS,),
            in_specs=[columns(cot_all), whole_block((T, SR))],
            out_specs=pl.BlockSpec((CHUNK, SR), lambda i: (i, 0)),
            out_shape=jax.ShapeDtypeStruct((D, SR), BF),
        )(cot_all, s_hid)
        down_red = shard_reduce(down_part)

        s_geg, e_geg, rows_out, gc_wide, lg_part = call(
            lambda *refs: ffn_grad_kernel(SR, FR, EX, *refs),
            (
                cot_all, rest_all, in_all, act, slope_up, e_hid, e_act, e_slope_up, rows_geo, rows_g,
                spread, probs_r, chosen_wide,
            ),
            {
                0: columns(cot_all),
                1: chunk_rows(SR + FR - EX),
                2: more_spec,
                8: columns(rows_geo),
                9: columns(rows_g),
            },
            [(T, 2 * SR, BF), (RC, 2 * FR, BF), (RC, D, F32), (T, 128, F32), (T, NE, BF)],
            [(T, SR), (RC, FR), (RC, 128)],
        )
        gn2_parts = call(
            lambda *refs: ffn_n2_kernel(R, SR, *refs),
            (s_geg, e_geg, lg_part, spread, in_all, attn_all),
            {4: w_in_spec, 5: router_spec},
            [(TOK, D, BF)] * R,
        )
        gc_part = gc_wide[:, 0].reshape(R, TOK)

        def logits_grad(gc):
            p = (gc * chosen).reshape(T, 1)
            first = (jnp.arange(NE) == 0).astype(F32)[None]
            return (probs_r * (p * first - probs_r[:, :1] * p)).astype(BF)

        gn2 = reduce_parts(gn2_parts)

        GW = -(-(2 * SR + 3 * FR) // 128) * 128
        gu_part = pl.pallas_call(
            lambda *refs: ffn_weight_kernel(SR, FR, *refs),
            grid=(STEPS,),
            in_specs=[
                columns(n2),
                whole_block(s_geg.shape),
                columns(rows_in),
                whole_block(e_geg.shape),
                columns(rows_geo),
                whole_block(e_hid.shape),
            ],
            out_specs=pl.BlockSpec((CHUNK, GW), lambda i: (i, 0)),
            out_shape=jax.ShapeDtypeStruct((D, GW), BF),
        )(n2, s_geg, rows_in, e_geg, rows_geo, e_hid)
        gu_red = shard_reduce(gu_part)
        operands = (s_hid, rest_all, spread, rows_w, rows_out)
        specs = {
            1: pl.BlockSpec((CHUNK, SR + FR - EX), lambda i: (i, 0)),
            4: pl.BlockSpec((RC, CHUNK), lambda i: (0, i)),
        }
        out_ffn = pl.pallas_call(
            lambda *refs: ffn_out_kernel(R, SR, *refs),
            grid=(STEPS,),
            in_specs=[specs.get(n, whole_block(v.shape)) for n, v in enumerate(operands)],
            out_specs=[pl.BlockSpec((TOK, CHUNK), lambda i: (0, i))] * R,
            out_shape=[jax.ShapeDtypeStruct((TOK, D), BF)] * R,
        )(*operands)
        out_ffn = [out_ffn[0]] + [send(out_ffn[k], k) for k in range(1, R)]
        result = pl.pallas_call(
            add_kernel, out_shape=jax.ShapeDtypeStruct((TOK, D), BF)
        )(hidden, *out_ffn)
        gc_all = gather(gc_part)
        gc_total = gc_all[0]
        for j in range(1, R):
            gc_total = gc_total + jnp.stack([gc_all[j][k ^ j] for k in range(R)])

        g_mixer = jnp.sum(gn2 * hidden * scale_two, axis=0)
        scaled = gn2 * gain_two
        grad_hidden = (
            cotangent.astype(F32)
            + scale_two * scaled
            - hidden * scale_two**3 * jnp.mean(scaled * hidden, axis=-1, keepdims=True)
        )

        backward = pl.pallas_call(
            lambda *refs: attention_grad_kernel(R, HR, *refs),
            grid_spec=pltpu.PrefetchScalarGridSpec(
                num_scalar_prefetch=1,
                grid=(R,),
                in_specs=[whole_block((TOK, D))] * R
                + [out_w_spec] * R
                + [kvu_spec] * R
                + [
                    rows(HN),
                    probs_spec,
                    rows(2 * HN),
                    rows(QW),
                    rows(256),
                    rows(128),
                    rows(128),
                ],
                out_specs=[rows(QW), rows(2 * HN)] + [whole_block((TOK, KVR + 128))] * R,
                scratch_shapes=[pltpu.VMEM((TOK, D), BF), pltpu.VMEM((TOK, KVR + 128), BF)],
            ),
            out_shape=[
                jax.ShapeDtypeStruct((T, QW), BF),
                jax.ShapeDtypeStruct((T, 2 * HN), BF),
            ]
            + [jax.ShapeDtypeStruct((TOK, KVR + 128), BF)] * R,
        )
        ghb = gather(grad_hidden.astype(BF))
        gq, g_kv, *glat_parts = backward(
            r_one, *ghb, *out_ws, *kvus, att, probs, kv, q_b, kr_b, cosine, sine
        )
        attn_part = pl.pallas_call(
            lambda *refs: attention_weight_kernel(R, QW, *refs),
            grid_spec=pltpu.PrefetchScalarGridSpec(
                num_scalar_prefetch=1,
                grid=(R,),
                in_specs=[
                    pl.BlockSpec((T, DC), lambda i, r_ref: (0, i)),
                    whole_block((T, QW)),
                ]
                + [pl.BlockSpec((TOK, DC), lambda i, r_ref: (0, r_ref[0]))] * R
                + [whole_block((T, HN))] * R,
                out_specs=pl.BlockSpec((DC, QW + DC), lambda i, r_ref: (i, 0)),
                scratch_shapes=[pltpu.VMEM((T, DC), BF), pltpu.VMEM((T, HN), BF)],
            ),
            out_shape=jax.ShapeDtypeStruct((D, QW + DC), BF),
        )(r.reshape(1), n1, gq, *ghb, *att_all)
        glat = reduce_parts(glat_parts)
        latent_own, scale_kv_own = latent[:TOK], scale_kv[:TOK]
        gl_n = glat[:, :KVR]
        g_kvgain = jnp.sum(gl_n * latent_own * scale_kv_own, axis=0)
        lat_scaled = gl_n * gain_kv
        g_latent = scale_kv_own * lat_scaled - latent_own * scale_kv_own**3 * jnp.mean(
            lat_scaled * latent_own, axis=-1, keepdims=True
        )
        gd_own = jnp.concatenate([g_latent, glat[:, KVR : KVR + DR]], axis=1).astype(BF)
        gd = part(jnp.concatenate(gather(gd_own)), LR)
        gn1_part = dot_t(gq, w_q) + dot_t(gd, lax.dynamic_slice(attn_all, (0, CD + r * LR), (D, LR)))
        gn1 = reduce_blocks(gn1_part)
        scale_own = scale_one[:TOK]
        scaled_one = gn1 * gain_one
        grad_input = (
            grad_hidden
            + scale_own * scaled_one
            - x_own * scale_own**3 * jnp.mean(scaled_one * x_own, axis=-1, keepdims=True)
        )
        g_norm = jnp.sum(gn1_part * xf * scale_one, axis=0)

        g_kvu = t_dot(lat_n, g_kv).astype(BF).reshape(KVR, HR, DN + DV).transpose(1, 0, 2)
        kvu_blocks = []
        for k in range(R):
            b = lax.dynamic_slice_in_dim(g_kvu, (r ^ k) * KR, KR, 1)
            kvu_blocks.append(send(b, k) if k else b)
        lg = part(logits_grad(gc_total), NR)
        vectors = jnp.concatenate([g_norm, g_mixer, g_kvgain])
        gathered = gather(vectors)
        summed = sum(gathered)
        g_gains = gain_rows(
            summed[:D].reshape(S, DL),
            summed[D : 2 * D].reshape(S, DL),
            summed[2 * D :].reshape(S, KVR // S),
        )
        attn_red = shard_reduce(attn_part)
        TW = -(-(KW + LR + NR + 64) // 128) * 128
        if KW == DN + DV:
            tail_part = pl.pallas_call(
                lambda *refs: tail_kernel(R, HS, HR, KR, LR, NR, *refs),
                grid_spec=pltpu.PrefetchScalarGridSpec(
                    num_scalar_prefetch=1,
                    grid=(S,),
                    in_specs=[
                        pl.BlockSpec((T, DL), lambda i, r_ref: (0, i)),
                        pl.BlockSpec((T, DL), lambda i, r_ref: (0, i)),
                        whole_block(gd.shape),
                        whole_block(lg.shape),
                        pl.BlockSpec((1, 16, 64), lambda i, r_ref: (i, 0, 0)),
                    ]
                    + [whole_block((HR, KR, DN + DV))] * R,
                    out_specs=pl.BlockSpec((DL, TW), lambda i, r_ref: (i, 0)),
                ),
                out_shape=jax.ShapeDtypeStruct((D, TW), BF),
            )(r_one, n1, n2, gd, lg, g_gains[:, :16], *kvu_blocks)
        else:
            g_kvu_all = jnp.concatenate(natural(kvu_blocks))
            tail_part = jnp.concatenate(
                [
                    fold_all(g_kvu_all.reshape(H * KR, DN + DV), S, DL),
                    t_dot(n1, gd).astype(BF),
                    t_dot(n2, lg).astype(BF),
                    g_gains.reshape(D, 64).astype(BF),
                    jnp.zeros((D, TW - KW - LR - NR - 64), BF),
                ],
                axis=1,
            )
        tail_red = shard_reduce(tail_part)

        (own_sd,) = join_blocks(
            lambda *refs: join_down_kernel(R, SR, *refs), R, r, gather_pieces(down_red), [(SH, DL)]
        )
        own_sg, own_su, own_eg, own_eu, own_ed = join_blocks(
            lambda *refs: join_ffn_kernel(R, SR, FR, *refs),
            R,
            r,
            gather_pieces(gu_red),
            [(DL, SH), (DL, SH), (DL, FF), (DL, FF), (FF, DL)],
        )
        own_qw, own_ow = join_blocks(
            lambda *refs: join_attention_kernel(R, HR, *refs),
            R,
            r,
            gather_pieces(attn_red),
            [(DL, H * (DN + DR)), (DL, D)],
        )
        tail_pieces = gather(tail_red)
        gains_red = tail_red[:, KW + LR + NR : KW + LR + NR + 64].astype(F32)
        if KW == DN + DV:
            own_ku, own_kd, own_rw = join_blocks(
                lambda *refs: join_tail_kernel(R, HS, KR, LR, *refs),
                R,
                r,
                [(k, 0, block) for k, block in enumerate(tail_pieces)],
                [(KVR, HS * (DN + DV)), (KVR + DR, DL), (NE, DL)],
            )
            own_kd, own_rw = own_kd.T, own_rw.T
        else:
            tail_nat = natural(tail_pieces)
            own_ku = jnp.concatenate(
                [
                    unfold(b[:, :KW], HS * KR)
                    .reshape(HS, KR, DN + DV)
                    .transpose(1, 0, 2)
                    .reshape(KR, HS * (DN + DV))
                    for b in tail_nat
                ]
            ).astype(F32)
            own_kd = jnp.concatenate([b[:, KW : KW + LR] for b in tail_nat], axis=1).astype(F32)
            own_rw = jnp.concatenate([b[:, KW + LR : KW + LR + NR] for b in tail_nat], axis=1).astype(F32)
        return (
            result,
            grad_input,
            gains_red[:GR].reshape(DL),
            own_qw,
            own_kd,
            gains_red[2 * GR, : KVR // S],
            own_ku,
            own_ow,
            gains_red[GR : 2 * GR].reshape(DL),
            own_rw,
            own_sg,
            own_su,
            own_sd,
            own_eg[None],
            own_eu[None],
            own_ed[None],
        )

    return local


def unfold_all(values, S, DL, rows):
    _, c = values.shape
    f = DL // rows
    if f <= 1:
        return values
    return values.reshape(S, f, rows, c).transpose(0, 2, 1, 3).reshape(S * rows, f * c)


def fold_all(values, S, DL):
    n, c = values.shape
    f = S * DL // n
    if f <= 1:
        return values
    return values.reshape(S, n // S, f, c // f).transpose(0, 2, 1, 3).reshape(S * DL, c // f)


def solution(mesh):
    tokens = P((REP, SHD), None)
    rows, cols = P(SHD, None), P(None, SHD)
    placed = (
        tokens,
        P((REP, SHD)),
        tokens,
        P(SHD),
        rows,
        rows,
        P(SHD),
        cols,
        rows,
        P(SHD),
        rows,
        rows,
        rows,
        cols,
        P(None, SHD, None),
        P(None, SHD, None),
        P(None, None, SHD),
        tokens,
    )
    outs = (tokens, tokens) + placed[3:17]
    body = make_local(mesh.shape[REP], mesh.shape[SHD])

    return jax.shard_map(
        body,
        mesh=mesh,
        in_specs=placed,
        out_specs=outs,
        check_vma=False,
    )
```

```python
import jax
import jax.numpy as jnp
from jax import lax
from jax.experimental import pallas as pl
from jax.experimental.pallas import tpu as pltpu
from jax.sharding import PartitionSpec as P

D = 2048
H = 16
DN = 128
DR = 64
DV = 128
KVR = 512
NE = 64
CAP = 16
FF = 1408
SH = 2816
TOK = 128

EPSILON = 1e-06
NEGATIVE = -1e30
BF = jnp.bfloat16
F32 = jnp.float32
SCALE = (DN + DR) ** (-0.5)


def dot(left, right):
    return jnp.dot(left, right, preferred_element_type=F32)


def dot_t(left, right):
    return lax.dot_general(left, right, (((1,), (1,)), ((), ())), preferred_element_type=F32)


def t_dot(left, right):
    return lax.dot_general(left, right, (((0,), (0,)), ((), ())), preferred_element_type=F32)


def inv_rms(values):
    return lax.rsqrt(jnp.mean(values * values, axis=-1, keepdims=True) + EPSILON)


def silu_parts(pre_act):
    sigmoid_val = jax.nn.sigmoid(pre_act)
    return (pre_act * sigmoid_val, sigmoid_val * (1.0 + pre_act * (1.0 - sigmoid_val)))


def unfold(values, rows):
    n, c = values.shape
    f = n // rows
    if f <= 1:
        return values
    return values.reshape(f, rows, c).transpose(1, 0, 2).reshape(rows, f * c)


def roll_sum(values):
    values = values + pltpu.roll(values, 64, 1)
    return values + pltpu.roll(values, 32, 1)


def lane_index():
    return lax.broadcasted_iota(jnp.int32, (TOK, 128), 1)


def block_at(R, r_ref, k, width):
    if R != 4:
        return slice(k * width, (k + 1) * width)
    return pl.ds(pl.multiple_of((r_ref[0] ^ k) * width, width), width)


def attention_kernel(R, HR, r_ref, q_ref, rope_ref, lat_ref, cos_ref, sin_ref, bias_ref, *refs):
    out_w_refs, kvu_refs = refs[:R], refs[R : 2 * R]
    att_ref, probs_ref, qb_ref, krb_ref, kv_ref = refs[2 * R : 2 * R + 5]
    part_refs, sum_ref = refs[2 * R + 5 : 3 * R + 5], refs[-1]
    HN, KR, W = HR * DN, KVR // R, DN + DV
    lats = [lat_ref[:, block_at(R, r_ref, k, KR)] for k in range(R)]
    for h in range(HR):
        total = dot(lats[0], kvu_refs[0][h * KR : (h + 1) * KR, :])
        for k in range(1, R):
            total = total + dot(lats[k], kvu_refs[k][h * KR : (h + 1) * KR, :])
        kv_ref[:, h * W : (h + 1) * W] = total.astype(BF)
    lane = lane_index()
    cos, sin = cos_ref[...], sin_ref[...]
    rope = rope_ref[...]
    k_1 = roll_sum(jnp.where(lane < 32, rope, 0.0))
    k_2 = roll_sum(jnp.where((lane >= 32) & (lane < 64), rope, 0.0))
    kr_1 = (k_1 * cos - k_2 * sin).astype(BF)
    kr_2 = (k_2 * cos + k_1 * sin).astype(BF)
    krb_ref[:, :128] = kr_1
    krb_ref[:, 128:] = kr_2
    q_1, q_2 = q_ref[:, HN : HN + 128], q_ref[:, HN + 128 :]
    qr_1 = (q_1 * cos - q_2 * sin) * SCALE
    qr_2 = (q_2 * cos + q_1 * sin) * SCALE
    q_n = (q_ref[:, :HN] * SCALE).astype(BF)
    qb_ref[:, :HN] = q_n
    qb_ref[:, HN : HN + 128] = qr_1.astype(BF)
    qb_ref[:, HN + 128 :] = qr_2.astype(BF)
    bias = bias_ref[0]
    for h in range(HR):
        head = (lane >= 32 * h) & (lane < 32 * h + 32)
        scores = (
            dot_t(q_n[:, h * DN : (h + 1) * DN], kv_ref[:, h * W : h * W + DN])
            + dot_t(jnp.where(head, qr_1, 0.0).astype(BF), kr_1)
            + dot_t(jnp.where(head, qr_2, 0.0).astype(BF), kr_2)
            + bias
        )
        expd = jnp.exp(scores - jnp.max(scores, axis=-1, keepdims=True))
        probs = expd / jnp.sum(expd, axis=-1, keepdims=True)
        probs_ref[h] = probs
        value = kv_ref[:, h * W + DN : (h + 1) * W]
        att_ref[:, h * DV : (h + 1) * DV] = dot(probs.astype(BF), value).astype(BF)
    att = att_ref[...]
    for k in range(R):
        sum_ref[:, block_at(R, r_ref, k, D // R)] = dot(att, out_w_refs[k][...]).astype(BF)
    for k in range(R):

        @pl.when(pl.program_id(0) == k)
        def _():
            part_refs[k][...] = sum_ref[...]


def attention_grad_kernel(R, HR, r_ref, *refs):
    grad_refs, out_w_refs, kvu_refs = refs[:R], refs[R : 2 * R], refs[2 * R : 3 * R]
    (att_ref, probs_ref, kv_ref, qb_ref, krb_ref, cos_ref, sin_ref,
     gq_ref, gkv_ref) = refs[3 * R : 3 * R + 9]
    glat_refs = refs[3 * R + 9 : 4 * R + 9]
    ghb_ref, lat_ref = refs[4 * R + 9 :]
    HN, KR, W = HR * DN, KVR // R, DN + DV
    step = pl.program_id(0)
    for k in range(R):

        @pl.when(step == k)
        def _():
            ghb_ref[...] = grad_refs[k][...]

    g_att = dot_t(ghb_ref[:, block_at(R, r_ref, 0, D // R)], out_w_refs[0][...])
    for k in range(1, R):
        g_att = g_att + dot_t(ghb_ref[:, block_at(R, r_ref, k, D // R)], out_w_refs[k][...])
    g_att = g_att.astype(BF)
    lane = lane_index()
    cos, sin = cos_ref[...], sin_ref[...]
    kr_1, kr_2 = krb_ref[:, :128], krb_ref[:, 128:]
    qr_1 = qb_ref[:, HN : HN + 128].astype(F32)
    qr_2 = qb_ref[:, HN + 128 :].astype(F32)
    zero = jnp.zeros((TOK, 128), F32)
    gq_1, gq_2, gk_1, gk_2 = zero, zero, zero, zero
    for h in range(HR):
        cut = slice(h * DN, (h + 1) * DN)
        key, value = slice(h * W, h * W + DN), slice(h * W + DN, (h + 1) * W)
        head = (lane >= 32 * h) & (lane < 32 * h + 32)
        ga = g_att[:, cut]
        probs = probs_ref[h]
        gkv_ref[:, value] = t_dot(probs.astype(BF), ga).astype(BF)
        delta = jnp.sum(ga.astype(F32) * att_ref[:, cut].astype(F32), axis=-1, keepdims=True)
        gs = (probs * (dot_t(ga, kv_ref[:, value]) - delta)).astype(BF)
        gq_ref[:, cut] = (dot(gs, kv_ref[:, key]) * SCALE).astype(BF)
        gq_1 = gq_1 + jnp.where(head, dot(gs, kr_1), 0.0)
        gq_2 = gq_2 + jnp.where(head, dot(gs, kr_2), 0.0)
        gkv_ref[:, key] = t_dot(gs, qb_ref[:, cut]).astype(BF)
        gk_1 = gk_1 + t_dot(gs, jnp.where(head, qr_1, 0.0).astype(BF))
        gk_2 = gk_2 + t_dot(gs, jnp.where(head, qr_2, 0.0).astype(BF))
    gq_ref[:, HN : HN + 128] = ((gq_1 * cos + gq_2 * sin) * SCALE).astype(BF)
    gq_ref[:, HN + 128 :] = ((gq_2 * cos - gq_1 * sin) * SCALE).astype(BF)
    u_1, u_2 = roll_sum(gk_1), roll_sum(gk_2)
    r_1, r_2 = u_1 * cos + u_2 * sin, u_2 * cos - u_1 * sin
    g_rope = jnp.where(lane < 32, r_1, jnp.where(lane < 64, r_2, 0.0)).astype(BF)
    lat_ref[:, KVR:] = g_rope
    for k in range(R):
        total = dot_t(gkv_ref[:, :W], kvu_refs[k][:KR, :])
        for h in range(1, HR):
            total = total + dot_t(
                gkv_ref[:, h * W : (h + 1) * W], kvu_refs[k][h * KR : (h + 1) * KR, :]
            )
        lat_ref[:, block_at(R, r_ref, k, KR)] = total.astype(BF)
    for k in range(R):

        @pl.when(step == k)
        def _():
            glat_refs[k][...] = lat_ref[...]


def scatter_rows(spread, rows):
    high = rows.astype(BF)
    low = (rows - high.astype(F32)).astype(BF)
    return dot(spread, jnp.concatenate([high, low], axis=0))


REP, SHD = "replica", "shard"


STEPS = 4
CHUNK = D // STEPS


def add_step(step, ref, value):
    @pl.when(step == 0)
    def _():
        ref[...] = value

    @pl.when(step > 0)
    def _():
        ref[...] += value


def ffn_in_kernel(R, SR, FR, *refs):
    (in_ref, router_ref, pick_ref, chosen_ref, rows_g_ref, n2_ref, rows_in_ref, act_ref, slope_ref,
     s_hid_ref, e_act_ref, e_slope_ref, e_hid_ref, probs_ref, rows_w_ref, rows_geo_ref, acc_ref,
     e_acc_ref, logits_ref) = refs[R:]
    step = pl.program_id(0)
    for k in range(R):
        n2_ref[k * TOK : (k + 1) * TOK, :] = refs[k][...]
    n2 = n2_ref[...]
    rows_in = dot(pick_ref[...], n2).astype(BF)
    rows_in_ref[...] = rows_in
    add_step(step, acc_ref, dot(n2, in_ref[:, : 2 * SR]))
    add_step(step, e_acc_ref, dot(rows_in, in_ref[:, 2 * SR : 2 * SR + 2 * FR]))
    add_step(step, logits_ref, dot(n2, router_ref[:, 128 - NE :]))

    @pl.when(step == STEPS - 1)
    def _():
        up = acc_ref[:, SR:]
        act, slope = silu_parts(acc_ref[:, :SR])
        act_ref[...] = act
        slope_ref[...] = slope * up
        s_hid_ref[...] = (act * up).astype(BF)
        e_up = e_acc_ref[:, FR:]
        e_act, e_slope = silu_parts(e_acc_ref[:, :FR])
        e_act_ref[...] = e_act
        e_slope_ref[...] = e_slope * e_up
        e_hid_ref[...] = (e_act * e_up).astype(BF)
        logits = logits_ref[...]
        expd = jnp.exp(logits - jnp.max(logits, axis=-1, keepdims=True))
        probs = expd / jnp.sum(expd, axis=-1, keepdims=True)
        probs_ref[...] = probs
        combine = probs[:, :1] * chosen_ref[...]
        high = combine.astype(BF)
        low = (combine - high.astype(F32)).astype(BF)
        rows_w = dot(pick_ref[...], high) + dot(pick_ref[...], low)
        rows_w_ref[...] = rows_w
        rows_geo_ref[...] = (rows_w[:, :1] * rows_g_ref[...]).astype(BF)


def ffn_grad_kernel(SR, FR, EX, cot_ref, rest_ref, more_ref, act_ref, slope_ref, e_hid_ref, e_act_ref,
                    e_slope_ref, rows_geo_ref, rows_g_ref, spread_ref, probs_ref, chosen_ref,
                    geg_ref, e_geg_ref, rows_out_ref, gc_ref, lg_ref, acc_ref, e_acc_ref,
                    gc_acc_ref):
    step = pl.program_id(0)
    FM, at = FR - EX, (2 * SR + 2 * FR) % 128
    w_edt, w_more = rest_ref[:, SR:], more_ref[:, at : at + EX]
    geo = rows_geo_ref[...]
    add_step(step, acc_ref, dot(cot_ref[...], rest_ref[:, :SR]))
    add_step(step, e_acc_ref.at[:, :FM], dot(geo, w_edt))
    add_step(step, e_acc_ref.at[:, FM:], dot(geo, w_more))
    rows_out = dot_t(e_hid_ref[:, :FM], w_edt) + dot_t(e_hid_ref[:, FM:], w_more)
    rows_out_ref[...] = rows_out
    gc_rows = jnp.sum(rows_g_ref[...] * rows_out, axis=-1, keepdims=True)
    add_step(step, gc_acc_ref, jnp.broadcast_to(gc_rows, gc_acc_ref.shape))

    @pl.when(step == STEPS - 1)
    def _():
        s_gh = acc_ref[...]
        geg_ref[:, :SR] = (s_gh * slope_ref[...]).astype(BF)
        geg_ref[:, SR:] = (s_gh * act_ref[...]).astype(BF)
        e_gh = e_acc_ref[...]
        e_geg_ref[:, :FR] = (e_gh * e_slope_ref[...]).astype(BF)
        e_geg_ref[:, FR:] = (e_gh * e_act_ref[...]).astype(BF)
        gc = scatter_rows(spread_ref[...], gc_acc_ref[...])
        gc_ref[...] = gc
        p = (gc * chosen_ref[...])[:, :NE]
        probs = probs_ref[...]
        first = lax.broadcasted_iota(jnp.int32, probs.shape, 1) == 0
        lg = probs * (jnp.where(first, p, 0.0) - probs[:, :1] * p)
        lg_ref[...] = lg.astype(BF)


def ffn_n2_kernel(R, SR, geg_ref, e_geg_ref, lg_ref, spread_ref, in_ref, router_ref, *part_refs):
    total = dot_t(geg_ref[...], in_ref[:, : 2 * SR]) + dot_t(lg_ref[...], router_ref[:, 128 - NE :])
    rows_back = dot_t(e_geg_ref[...], in_ref[:, 2 * SR : 2 * SR + e_geg_ref.shape[1]])
    total = total + scatter_rows(spread_ref[...], rows_back)
    for k in range(R):
        part_refs[k][...] = total[k * TOK : (k + 1) * TOK].astype(BF)


def ffn_out_kernel(R, SR, s_hid_ref, rest_ref, spread_ref, rows_w_ref, rows_out_ref, *part_refs):
    total = dot_t(s_hid_ref[...], rest_ref[:, :SR]) + scatter_rows(
        spread_ref[...], rows_w_ref[:, :1] * rows_out_ref[...]
    )
    for k in range(R):
        part_refs[k][...] = total[k * TOK : (k + 1) * TOK].astype(BF)


def add_kernel(hidden_ref, *refs):
    total = hidden_ref[...]
    for ref in refs[:-1]:
        total = total + ref[...].astype(F32)
    refs[-1][...] = total.astype(BF)


def ffn_weight_kernel(
    SR, FR, n2_ref, geg_ref, rows_in_ref, e_geg_ref, rows_geo_ref, e_hid_ref, *refs
):
    out_ref, cut = refs[-1], 2 * SR + 2 * FR
    out_ref[:, : 2 * SR] = t_dot(n2_ref[...], geg_ref[...]).astype(BF)
    out_ref[:, 2 * SR : cut] = t_dot(rows_in_ref[...], e_geg_ref[...]).astype(BF)
    out_ref[:, cut : cut + FR] = t_dot(rows_geo_ref[...], e_hid_ref[...]).astype(BF)
    cut = cut + FR
    for more_ref in refs[:-1]:
        out_ref[:, cut : cut + more_ref.shape[1]] = more_ref[...]
        cut = cut + more_ref.shape[1]
    if out_ref.shape[1] > cut:
        out_ref[:, cut:] = jnp.zeros((CHUNK, out_ref.shape[1] - cut), BF)


def product_kernel(left_ref, right_ref, *out_refs):
    part = t_dot(left_ref[...], right_ref[...]).astype(BF)
    cut = 0
    for ref in out_refs:
        ref[...] = part[:, cut : cut + ref.shape[1]]
        cut = cut + ref.shape[1]


def attention_weight_kernel(R, QW, r_ref, n1_ref, gq_ref, *refs):
    grad_refs, att_refs = refs[:R], refs[R : 2 * R]
    out_ref, ghb_ref, att_ref = refs[2 * R :]
    step = pl.program_id(0)

    @pl.when(step == 0)
    def _():
        for k in range(R):
            ghb_ref[k * TOK : (k + 1) * TOK, :] = grad_refs[k][...]

    for k in range(R):

        @pl.when((r_ref[0] ^ step) == k)
        def _():
            for i in range(R):
                att_ref[i * TOK : (i + 1) * TOK, :] = att_refs[k][
                    (i ^ k) * TOK : ((i ^ k) + 1) * TOK, :
                ]

    out_ref[:, :QW] = t_dot(n1_ref[...], gq_ref[...]).astype(BF)
    out_ref[:, QW:] = t_dot(att_ref[...], ghb_ref[...]).astype(BF)


def tail_kernel(R, HS, HR, KR, LR, NR, r_ref, n1_ref, n2_ref, gd_ref, lg_ref, gains_ref, *refs):
    out_ref = refs[R]
    W, n = DN + DV, HR // HS
    step = pl.program_id(0)
    out_ref[...] = jnp.zeros(out_ref.shape, BF)
    for k in range(R):

        @pl.when((r_ref[0] ^ (step // n)) == k)
        def _():
            for h in range(HS):
                out_ref[h * KR : (h + 1) * KR, :W] = refs[k][(step % n) * HS + h]

    out_ref[:, W : W + LR] = t_dot(n1_ref[...], gd_ref[...]).astype(BF)
    out_ref[:, W + LR : W + LR + NR] = t_dot(n2_ref[...], lg_ref[...]).astype(BF)
    cut = W + LR + NR
    out_ref[: gains_ref.shape[1], cut : cut + 64] = gains_ref[0].astype(BF)


def whole_block(shape):
    return pl.BlockSpec(shape, lambda *_: (0,) * len(shape))


def attention_columns_kernel(
    HR, HS, CH, r_ref, query_ref, down_ref, router_ref, up_ref, out_w_ref, out_ref
):
    HN, W, half = HR * DN, DN + DR, DR // 2
    for h in range(HR):
        one, two = HN + h * half, HN + 128 + h * half
        out_ref[:, h * DN : (h + 1) * DN] = query_ref[:, h * W : h * W + DN]
        out_ref[:, one : one + half] = query_ref[:, h * W + DN : h * W + DN + half]
        out_ref[:, two : two + half] = query_ref[:, h * W + DN + half : (h + 1) * W]
    rows, cut = out_ref.shape[0], HN + 256
    if HR * half < 128:
        pad = jnp.zeros((rows, 128 - HR * half), BF)
        out_ref[:, HN + HR * half : HN + 128] = pad
        out_ref[:, HN + 128 + HR * half : cut] = pad
    for ref in (down_ref, router_ref):
        out_ref[:, cut : cut + ref.shape[0]] = ref[...].T
        cut = cut + ref.shape[0]
    if CH > cut:
        out_ref[:, cut:CH] = jnp.zeros((rows, CH - cut), BF)
    cut = CH + out_w_ref.shape[1]
    out_ref[:, CH:cut] = out_w_ref[...]
    width, n = out_ref.shape[1] - cut, up_ref.shape[0]
    for f in range((DN + DV) // width):
        for h in range(HS):
            at, first = (f * HS + h) * n, h * (DN + DV) + f * width
            out_ref[at : at + n, cut:] = up_ref[:, first : first + width]


def join_ffn_kernel(
    R, SR, FR, blocks, downs, gate_ref, up_ref, e_gate_ref, e_up_ref, e_down_ref, down_ref
):
    cut, width = 2 * SR, downs.shape[2]
    for j in range(R):
        gate_ref[:, j * SR : (j + 1) * SR] = blocks[j, :, :SR].astype(F32)
        up_ref[:, j * SR : (j + 1) * SR] = blocks[j, :, SR:cut].astype(F32)
        e_gate_ref[:, j * FR : (j + 1) * FR] = blocks[j, :, cut : cut + FR].astype(F32)
        e_up_ref[:, j * FR : (j + 1) * FR] = blocks[j, :, cut + FR : cut + 2 * FR].astype(F32)
        e_down = blocks[j, :, cut + 2 * FR : cut + 3 * FR].astype(F32)
        e_down_ref[j * FR : (j + 1) * FR, :] = e_down.T
        down_ref[j * SR : j * SR + width, :] = downs[j].astype(F32).T
        if width < SR:
            more = blocks[j, :, cut + 3 * FR : cut + 3 * FR + SR - width].astype(F32)
            down_ref[j * SR + width : (j + 1) * SR, :] = more.T


def join_attention_kernel(R, HR, blocks, query_ref, out_ref):
    HN, W, half = HR * DN, DN + DR, DR // 2
    DC = D // R
    for j in range(R):
        for h in range(HR):
            at = (j * HR + h) * W
            one, two = HN + h * half, HN + 128 + h * half
            query_ref[:, at : at + DN] = blocks[j, :, h * DN : (h + 1) * DN].astype(F32)
            query_ref[:, at + DN : at + DN + half] = blocks[j, :, one : one + half].astype(F32)
            query_ref[:, at + DN + half : at + W] = blocks[j, :, two : two + half].astype(F32)
        out_ref[:, j * DC : (j + 1) * DC] = blocks[j, :, HN + 256 :].astype(F32)


def join_tail_kernel(R, HS, KR, LR, blocks, up_ref, down_ref, router_ref):
    W, NR = DN + DV, NE // R
    for j in range(R):
        for h in range(HS):
            up_ref[j * KR : (j + 1) * KR, h * W : (h + 1) * W] = blocks[
                j, h * KR : (h + 1) * KR, :W
            ].astype(F32)
        down_ref[j * LR : (j + 1) * LR, :] = blocks[j, :, W : W + LR].astype(F32).T
        router_ref[j * NR : (j + 1) * NR, :] = blocks[j, :, W + LR : W + LR + NR].astype(F32).T


def join_blocks(kernel, R, r, groups, outs):
    pieces = [(n, *piece) for n, group in enumerate(groups) for piece in group]

    def body(r_ref, *refs):
        block_refs = refs[-len(groups) :]
        for (n, k, row, values), ref in zip(pieces, refs):
            block_refs[n][r_ref[0] ^ k, row : row + values.shape[0], :] = ref[...]
        kernel(*block_refs, *refs[len(pieces) : -len(groups)])

    return pl.pallas_call(
        body,
        in_specs=[pl.BlockSpec(memory_space=pltpu.SMEM)]
        + [whole_block(piece[3].shape) for piece in pieces],
        out_specs=[whole_block(s) for s in outs],
        out_shape=[jax.ShapeDtypeStruct(s, F32) for s in outs],
        scratch_shapes=[pltpu.VMEM((R,) + group[0][2].shape, BF) for group in groups],
    )(r.reshape(1), *[piece[3] for piece in pieces])


def make_local(R, S):
    DL = D // S
    HR = H // R
    HS = H // S
    KR = KVR // R
    DC = D // R
    FR = FF // R
    SR = SH // R
    LR = (KVR + DR) // R
    NR = NE // R
    T = R * TOK
    QW = HR * DN + 256
    half = DR // 2
    GR = DL // 64
    links = [[(i, i ^ k) for i in range(R)] for k in range(R)]

    def send(values, k):
        return lax.ppermute(values, REP, links[k])

    def gather(values):
        return [values] + [send(values, k) for k in range(1, R)]

    def local(
        hidden_in,
        segment_ids,
        routes,
        norm_gain,
        query_weight,
        kv_down,
        kv_gain,
        kv_up,
        out_weight,
        mixer_gain,
        router_weight,
        shared_gate,
        shared_up,
        shared_down,
        expert_gate,
        expert_up,
        expert_down,
        cotangent,
    ):
        r = lax.axis_index(REP)

        def part(values, width, axis=1):
            return lax.dynamic_slice_in_dim(values, r * width, width, axis)

        def natural(blocks):
            stacked = jnp.stack(blocks)
            return [
                lax.dynamic_index_in_dim(stacked, r ^ j, 0, keepdims=False) for j in range(R)
            ]

        def reduce_parts(parts):
            own = parts[0].astype(F32)
            received = [send(parts[k].astype(BF), k) for k in range(1, R)]
            for part_sum in received:
                own = own + part_sum.astype(F32)
            return own

        def reduce_blocks(total):
            return reduce_parts([total[k * TOK : (k + 1) * TOK] for k in range(R)])

        def gather_pieces(values):
            if R != 4:
                return [(k, 0, block) for k, block in enumerate(gather(values))]
            mid = values.shape[0] // 2
            side, other = send(values, 1), send(values, 2)
            top, low = send(other[:mid], 1), send(side[mid:], 2)
            return [(0, 0, values), (1, 0, side), (2, 0, other), (3, 0, top), (3, mid, low)]

        def shard_gather(values):
            return lax.all_gather(values, SHD, axis=0, tiled=True)

        def shard_reduce(values):
            return lax.psum_scatter(values, SHD, scatter_dimension=0, tiled=True)

        index = jnp.arange(TOK, dtype=jnp.int32)
        same_own = segment_ids[:, None] == segment_ids[None, :]
        start_own = jnp.min(jnp.where(same_own, index[None, :], TOK), axis=1)
        chosen_own = jnp.any(routes == 0, axis=1)
        meta_own = jnp.concatenate(
            [
                start_own.astype(BF)[None],
                chosen_own.astype(BF)[None],
                jnp.zeros((6, TOK), BF),
            ]
        )
        meta = jnp.stack(gather(meta_own))
        x_all = jnp.concatenate(gather(hidden_in))
        cot_all = jnp.concatenate(gather(cotangent))

        CD, CR, CG = QW, QW + KVR + DR, QW + KVR + DR + NE
        CH = -(-CG // 128) * 128
        KW = HS * KR * (DN + DV) // DL

        def gain_rows(one, two, kv):
            lead = one.shape[:-1]
            pads = [(0, 0)] * len(lead)
            rows = jnp.concatenate(
                [
                    one.reshape(lead + (GR, 64)),
                    two.reshape(lead + (GR, 64)),
                    jnp.pad(kv, pads + [(0, 64 - KVR // S)]).reshape(lead + (1, 64)),
                ],
                axis=-2,
            )
            return jnp.pad(rows, pads + [(0, DL - 2 * GR - 1), (0, 0)])

        r_one = r.reshape(1)
        attn_own = pl.pallas_call(
            lambda *refs: attention_columns_kernel(HR, HS, CH, *refs),
            grid_spec=pltpu.PrefetchScalarGridSpec(
                num_scalar_prefetch=1,
                grid=(1,),
                in_specs=[
                    pl.BlockSpec((DL, HR * (DN + DR)), lambda i, r_ref: (0, r_ref[0])),
                    whole_block((KVR + DR, DL)),
                    whole_block((NE, DL)),
                    pl.BlockSpec((KR, HS * (DN + DV)), lambda i, r_ref: (r_ref[0], 0)),
                    pl.BlockSpec((DL, DC), lambda i, r_ref: (0, r_ref[0])),
                ],
                out_specs=whole_block((DL, CH + DC + KW)),
            ),
            out_shape=jax.ShapeDtypeStruct((DL, CH + DC + KW), BF),
        )(r_one, query_weight, kv_down.T, router_weight.T, kv_up, out_weight)
        attn_all = shard_gather(attn_own)
        head_blocks = []
        for k in range(R):
            piece = lax.dynamic_slice_in_dim(attn_all, (r ^ k) * HR * DV, HR * DV, 0)[:, CH:]
            head_blocks.append(send(piece, k) if k else piece)
        if R == 4:
            out_ws = kvus = head_blocks
            kvu_spec = pl.BlockSpec((HR * KR, DN + DV), lambda i, r_ref: (0, DC // KW))
        else:
            head_nat = natural(head_blocks)
            out_ws = [b[:, :DC] for b in head_nat]
            kvus = [unfold_all(b[:, DC:], S // R, DL, HS * KR) for b in head_nat]
            kvu_spec = whole_block((HR * KR, DN + DV))
        out_w_spec = pl.BlockSpec((HR * DV, DC), lambda i, r_ref: (0, 0))
        w_q = attn_all[:, :QW]
        gain_own = jnp.concatenate([norm_gain, mixer_gain, kv_gain])
        shard = lax.axis_index(SHD)
        gain_got = [gain_own] + [
            lax.ppermute(gain_own, SHD, [(i, i ^ j) for i in range(S)]) for j in range(1, S)
        ]
        gain_got = jnp.stack(gain_got).astype(F32)
        gain_all = jnp.concatenate(
            [lax.dynamic_index_in_dim(gain_got, shard ^ j, 0) for j in range(S)]
        )
        gain_one = gain_all[:, :DL].reshape(D)
        gain_two = gain_all[:, DL : 2 * DL].reshape(D)
        gain_kv = gain_all[:, 2 * DL :].reshape(KVR)

        EX = (SR + FR) % 128
        IN = -(-(2 * SR + 2 * FR + EX) // 128) * 128
        down_t = jnp.concatenate([part(shared_down, SR, 0).T, part(expert_down[0], FR, 0).T], axis=1)
        in_all = shard_gather(
            jnp.concatenate(
                [
                    part(shared_gate, SR),
                    part(shared_up, SR),
                    part(expert_gate[0], FR),
                    part(expert_up[0], FR),
                    down_t[:, SR + FR - EX :],
                    jnp.zeros((DL, IN - 2 * SR - 2 * FR - EX), BF),
                ],
                axis=1,
            ),
        )
        rest_all = shard_gather(down_t[:, : SR + FR - EX])

        xf = x_all.astype(F32)
        scale_one = inv_rms(xf)
        n1 = (xf * scale_one * gain_one).astype(BF)
        qlat = dot(n1, attn_all[:, :CH])
        latent = qlat[:, CD : CD + KVR]
        scale_kv = inv_rms(latent)
        lat_n = (latent * scale_kv * gain_kv).astype(BF)

        start = meta[:, 0].astype(F32)
        position = index.astype(F32)[None] - start
        freq = 10000.0 ** (-jnp.arange(half, dtype=F32) / half)
        angles = position.reshape(T, 1) * jnp.tile(freq, 4)[None]
        cosine, sine = jnp.cos(angles), jnp.sin(angles)
        allowed = (start[:, :, None] == start[:, None, :]) & (index[None, :] <= index[:, None])[None]
        bias = jnp.where(allowed, 0.0, NEGATIVE).astype(F32)

        def rows(width, column=0):
            return pl.BlockSpec((TOK, width), lambda i, r_ref: (i, column))

        HN = HR * DN
        probs_spec = pl.BlockSpec((HR, TOK, TOK), lambda i, r_ref: (i, 0, 0))
        forward = pl.pallas_call(
            lambda *refs: attention_kernel(R, HR, *refs),
            grid_spec=pltpu.PrefetchScalarGridSpec(
                num_scalar_prefetch=1,
                grid=(R,),
                in_specs=[
                    rows(QW),
                    rows(128, (CD + KVR) // 128),
                    rows(KVR),
                    rows(128),
                    rows(128),
                    pl.BlockSpec((1, TOK, TOK), lambda i, r_ref: (i, 0, 0)),
                ]
                + [out_w_spec] * R
                + [kvu_spec] * R,
                out_specs=[rows(HN), probs_spec, rows(QW), rows(256), rows(2 * HN)]
                + [whole_block((TOK, D))] * R,
                scratch_shapes=[pltpu.VMEM((TOK, D), BF)],
            ),
            out_shape=[
                jax.ShapeDtypeStruct((T, HN), BF),
                jax.ShapeDtypeStruct((R * HR, TOK, TOK), F32),
                jax.ShapeDtypeStruct((T, QW), BF),
                jax.ShapeDtypeStruct((T, 256), BF),
                jax.ShapeDtypeStruct((T, 2 * HN), BF),
            ]
            + [jax.ShapeDtypeStruct((TOK, D), BF)] * R,
        )
        att, probs, q_b, kr_b, kv, *out_parts = forward(
            r_one, qlat, qlat, lat_n, cosine, sine, bias, *out_ws, *kvus
        )
        x_own = hidden_in.astype(F32)
        hidden = x_own + reduce_parts(out_parts)

        scale_two = inv_rms(hidden)
        n2_own = (hidden * scale_two * gain_two).astype(BF)
        n2_blocks = gather(n2_own)
        att_all = gather(att)
        RC = R * CAP
        chosen = meta[:, 1].astype(F32)
        place = jnp.cumsum(chosen.astype(jnp.int32), axis=1) - 1
        slot = place + CAP * jnp.arange(R)[:, None]
        slot = jnp.where((chosen > 0.5) & (place < CAP), slot, -1).reshape(T)
        pick = (jnp.arange(RC)[:, None] == slot[None]).astype(BF)
        spread = (slot[:, None] == jnp.arange(2 * RC)[None] % RC).astype(BF)
        chosen_wide = jnp.broadcast_to(chosen.reshape(T, 1), (T, 128))
        rows_g = dot(pick, cot_all)

        def call(kernel, operands, specs, outs, scratch=()):
            return pl.pallas_call(
                kernel,
                grid=(STEPS,),
                in_specs=[specs.get(n, whole_block(v.shape)) for n, v in enumerate(operands)],
                out_specs=[
                    pl.BlockSpec((h, CHUNK), lambda i: (0, i))
                    if w == D
                    else whole_block((h, abs(w)))
                    for h, w, _ in outs
                ],
                out_shape=[jax.ShapeDtypeStruct((h, abs(w)), t) for h, w, t in outs],
                scratch_shapes=[pltpu.VMEM(shape, F32) for shape in scratch],
            )(*operands)

        def columns(values):
            return pl.BlockSpec((values.shape[0], CHUNK), lambda i: (0, i))

        def chunk_rows(width, column=0):
            return pl.BlockSpec((CHUNK, width), lambda i: (i, column))

        w_in_spec, router_spec = chunk_rows(IN), chunk_rows(128, CR // 128)
        more_spec = chunk_rows(128, (2 * SR + 2 * FR) // 128)
        (
            n2, rows_in, act, slope_up, s_hid, e_act, e_slope_up, e_hid, probs_r, rows_w, rows_geo
        ) = call(
            lambda *refs: ffn_in_kernel(R, SR, FR, *refs),
            (*n2_blocks, in_all, attn_all, pick, chosen_wide, rows_g),
            {**{k: columns(n2_own) for k in range(R)}, R: w_in_spec, R + 1: router_spec},
            [
                (T, D, BF), (RC, D, BF), (T, SR, F32), (T, SR, F32), (T, SR, BF), (RC, FR, F32),
                (RC, FR, F32), (RC, FR, BF), (T, NE, F32), (RC, 128, F32), (RC, -D, BF),
            ],
            [(T, 2 * SR), (RC, 2 * FR), (T, NE)],
        )

        GW = -(-(2 * SR + 3 * FR) // 128) * 128
        DX = SR % 128 if 2 * SR + 3 * FR + SR % 128 <= GW else 0
        down_widths = [SR - DX] + [DX] * bool(DX)
        down_part, *down_more = pl.pallas_call(
            product_kernel,
            grid=(STEPS,),
            in_specs=[columns(cot_all), whole_block((T, SR))],
            out_specs=[pl.BlockSpec((CHUNK, w), lambda i: (i, 0)) for w in down_widths],
            out_shape=[jax.ShapeDtypeStruct((D, w), BF) for w in down_widths],
        )(cot_all, s_hid)
        down_red = shard_reduce(down_part)

        s_geg, e_geg, rows_out, gc_wide, lg_part = call(
            lambda *refs: ffn_grad_kernel(SR, FR, EX, *refs),
            (
                cot_all, rest_all, in_all, act, slope_up, e_hid, e_act, e_slope_up, rows_geo, rows_g,
                spread, probs_r, chosen_wide,
            ),
            {
                0: columns(cot_all),
                1: chunk_rows(SR + FR - EX),
                2: more_spec,
                8: columns(rows_geo),
                9: columns(rows_g),
            },
            [(T, 2 * SR, BF), (RC, 2 * FR, BF), (RC, D, F32), (T, 128, F32), (T, NE, BF)],
            [(T, SR), (RC, FR), (RC, 128)],
        )
        gn2_parts = call(
            lambda *refs: ffn_n2_kernel(R, SR, *refs),
            (s_geg, e_geg, lg_part, spread, in_all, attn_all),
            {4: w_in_spec, 5: router_spec},
            [(TOK, D, BF)] * R,
        )
        gc_part = gc_wide[:, 0].reshape(R, TOK)

        def logits_grad(gc):
            p = (gc * chosen).reshape(T, 1)
            first = (jnp.arange(NE) == 0).astype(F32)[None]
            return (probs_r * (p * first - probs_r[:, :1] * p)).astype(BF)

        gn2 = reduce_parts(gn2_parts)

        gu_part = pl.pallas_call(
            lambda *refs: ffn_weight_kernel(SR, FR, *refs),
            grid=(STEPS,),
            in_specs=[
                columns(n2),
                whole_block(s_geg.shape),
                columns(rows_in),
                whole_block(e_geg.shape),
                columns(rows_geo),
                whole_block(e_hid.shape),
            ]
            + [chunk_rows(DX)] * len(down_more),
            out_specs=pl.BlockSpec((CHUNK, GW), lambda i: (i, 0)),
            out_shape=jax.ShapeDtypeStruct((D, GW), BF),
        )(n2, s_geg, rows_in, e_geg, rows_geo, e_hid, *down_more)
        gu_red = shard_reduce(gu_part)
        operands = (s_hid, rest_all, spread, rows_w, rows_out)
        specs = {
            1: pl.BlockSpec((CHUNK, SR + FR - EX), lambda i: (i, 0)),
            4: pl.BlockSpec((RC, CHUNK), lambda i: (0, i)),
        }
        out_ffn = pl.pallas_call(
            lambda *refs: ffn_out_kernel(R, SR, *refs),
            grid=(STEPS,),
            in_specs=[specs.get(n, whole_block(v.shape)) for n, v in enumerate(operands)],
            out_specs=[pl.BlockSpec((TOK, CHUNK), lambda i: (0, i))] * R,
            out_shape=[jax.ShapeDtypeStruct((TOK, D), BF)] * R,
        )(*operands)
        out_ffn = [out_ffn[0]] + [send(out_ffn[k], k) for k in range(1, R)]
        result = pl.pallas_call(
            add_kernel, out_shape=jax.ShapeDtypeStruct((TOK, D), BF)
        )(hidden, *out_ffn)
        gc_all = gather(gc_part)
        gc_total = gc_all[0]
        for j in range(1, R):
            gc_total = gc_total + jnp.stack([gc_all[j][k ^ j] for k in range(R)])

        g_mixer = jnp.sum(gn2 * hidden * scale_two, axis=0)
        scaled = gn2 * gain_two
        grad_hidden = (
            cotangent.astype(F32)
            + scale_two * scaled
            - hidden * scale_two**3 * jnp.mean(scaled * hidden, axis=-1, keepdims=True)
        )

        backward = pl.pallas_call(
            lambda *refs: attention_grad_kernel(R, HR, *refs),
            grid_spec=pltpu.PrefetchScalarGridSpec(
                num_scalar_prefetch=1,
                grid=(R,),
                in_specs=[whole_block((TOK, D))] * R
                + [out_w_spec] * R
                + [kvu_spec] * R
                + [
                    rows(HN),
                    probs_spec,
                    rows(2 * HN),
                    rows(QW),
                    rows(256),
                    rows(128),
                    rows(128),
                ],
                out_specs=[rows(QW), rows(2 * HN)] + [whole_block((TOK, KVR + 128))] * R,
                scratch_shapes=[pltpu.VMEM((TOK, D), BF), pltpu.VMEM((TOK, KVR + 128), BF)],
            ),
            out_shape=[
                jax.ShapeDtypeStruct((T, QW), BF),
                jax.ShapeDtypeStruct((T, 2 * HN), BF),
            ]
            + [jax.ShapeDtypeStruct((TOK, KVR + 128), BF)] * R,
        )
        ghb = gather(grad_hidden.astype(BF))
        gq, g_kv, *glat_parts = backward(
            r_one, *ghb, *out_ws, *kvus, att, probs, kv, q_b, kr_b, cosine, sine
        )
        attn_part = pl.pallas_call(
            lambda *refs: attention_weight_kernel(R, QW, *refs),
            grid_spec=pltpu.PrefetchScalarGridSpec(
                num_scalar_prefetch=1,
                grid=(R,),
                in_specs=[
                    pl.BlockSpec((T, DC), lambda i, r_ref: (0, i)),
                    whole_block((T, QW)),
                ]
                + [pl.BlockSpec((TOK, DC), lambda i, r_ref: (0, r_ref[0]))] * R
                + [whole_block((T, HN))] * R,
                out_specs=pl.BlockSpec((DC, QW + DC), lambda i, r_ref: (i, 0)),
                scratch_shapes=[pltpu.VMEM((T, DC), BF), pltpu.VMEM((T, HN), BF)],
            ),
            out_shape=jax.ShapeDtypeStruct((D, QW + DC), BF),
        )(r.reshape(1), n1, gq, *ghb, *att_all)
        glat = reduce_parts(glat_parts)
        latent_own, scale_kv_own = latent[:TOK], scale_kv[:TOK]
        gl_n = glat[:, :KVR]
        g_kvgain = jnp.sum(gl_n * latent_own * scale_kv_own, axis=0)
        lat_scaled = gl_n * gain_kv
        g_latent = scale_kv_own * lat_scaled - latent_own * scale_kv_own**3 * jnp.mean(
            lat_scaled * latent_own, axis=-1, keepdims=True
        )
        gd_own = jnp.concatenate([g_latent, glat[:, KVR : KVR + DR]], axis=1).astype(BF)
        gd = part(jnp.concatenate(gather(gd_own)), LR)
        gn1_part = dot_t(gq, w_q) + dot_t(gd, lax.dynamic_slice(attn_all, (0, CD + r * LR), (D, LR)))
        gn1 = reduce_blocks(gn1_part)
        scale_own = scale_one[:TOK]
        scaled_one = gn1 * gain_one
        grad_input = (
            grad_hidden
            + scale_own * scaled_one
            - x_own * scale_own**3 * jnp.mean(scaled_one * x_own, axis=-1, keepdims=True)
        )
        g_norm = jnp.sum(gn1_part * xf * scale_one, axis=0)

        g_kvu = t_dot(lat_n, g_kv).astype(BF).reshape(KVR, HR, DN + DV).transpose(1, 0, 2)
        kvu_blocks = []
        for k in range(R):
            b = lax.dynamic_slice_in_dim(g_kvu, (r ^ k) * KR, KR, 1)
            kvu_blocks.append(send(b, k) if k else b)
        lg = part(logits_grad(gc_total), NR)
        vectors = jnp.concatenate([g_norm, g_mixer, g_kvgain])
        gathered = gather(vectors)
        summed = sum(gathered)
        g_gains = gain_rows(
            summed[:D].reshape(S, DL),
            summed[D : 2 * D].reshape(S, DL),
            summed[2 * D :].reshape(S, KVR // S),
        )
        attn_red = shard_reduce(attn_part)
        TW = -(-(KW + LR + NR + 64) // 128) * 128
        if KW == DN + DV:
            tail_part = pl.pallas_call(
                lambda *refs: tail_kernel(R, HS, HR, KR, LR, NR, *refs),
                grid_spec=pltpu.PrefetchScalarGridSpec(
                    num_scalar_prefetch=1,
                    grid=(S,),
                    in_specs=[
                        pl.BlockSpec((T, DL), lambda i, r_ref: (0, i)),
                        pl.BlockSpec((T, DL), lambda i, r_ref: (0, i)),
                        whole_block(gd.shape),
                        whole_block(lg.shape),
                        pl.BlockSpec((1, 16, 64), lambda i, r_ref: (i, 0, 0)),
                    ]
                    + [whole_block((HR, KR, DN + DV))] * R,
                    out_specs=pl.BlockSpec((DL, TW), lambda i, r_ref: (i, 0)),
                ),
                out_shape=jax.ShapeDtypeStruct((D, TW), BF),
            )(r_one, n1, n2, gd, lg, g_gains[:, :16], *kvu_blocks)
        else:
            g_kvu_all = jnp.concatenate(natural(kvu_blocks))
            tail_part = jnp.concatenate(
                [
                    fold_all(g_kvu_all.reshape(H * KR, DN + DV), S, DL),
                    t_dot(n1, gd).astype(BF),
                    t_dot(n2, lg).astype(BF),
                    g_gains.reshape(D, 64).astype(BF),
                    jnp.zeros((D, TW - KW - LR - NR - 64), BF),
                ],
                axis=1,
            )
        tail_red = shard_reduce(tail_part)

        own_sg, own_su, own_eg, own_eu, own_ed, own_sd = join_blocks(
            lambda *refs: join_ffn_kernel(R, SR, FR, *refs),
            R,
            r,
            [gather_pieces(gu_red), gather_pieces(down_red)],
            [(DL, SH), (DL, SH), (DL, FF), (DL, FF), (FF, DL), (SH, DL)],
        )
        own_qw, own_ow = join_blocks(
            lambda *refs: join_attention_kernel(R, HR, *refs),
            R,
            r,
            [gather_pieces(attn_red)],
            [(DL, H * (DN + DR)), (DL, D)],
        )
        tail_pieces = gather(tail_red)
        gains_red = tail_red[:, KW + LR + NR : KW + LR + NR + 64].astype(F32)
        if KW == DN + DV:
            own_ku, own_kd, own_rw = join_blocks(
                lambda *refs: join_tail_kernel(R, HS, KR, LR, *refs),
                R,
                r,
                [[(k, 0, block) for k, block in enumerate(tail_pieces)]],
                [(KVR, HS * (DN + DV)), (KVR + DR, DL), (NE, DL)],
            )
            own_kd, own_rw = own_kd.T, own_rw.T
        else:
            tail_nat = natural(tail_pieces)
            own_ku = jnp.concatenate(
                [
                    unfold(b[:, :KW], HS * KR)
                    .reshape(HS, KR, DN + DV)
                    .transpose(1, 0, 2)
                    .reshape(KR, HS * (DN + DV))
                    for b in tail_nat
                ]
            ).astype(F32)
            own_kd = jnp.concatenate([b[:, KW : KW + LR] for b in tail_nat], axis=1).astype(F32)
            own_rw = jnp.concatenate([b[:, KW + LR : KW + LR + NR] for b in tail_nat], axis=1).astype(F32)
        return (
            result,
            grad_input,
            gains_red[:GR].reshape(DL),
            own_qw,
            own_kd,
            gains_red[2 * GR, : KVR // S],
            own_ku,
            own_ow,
            gains_red[GR : 2 * GR].reshape(DL),
            own_rw,
            own_sg,
            own_su,
            own_sd,
            own_eg[None],
            own_eu[None],
            own_ed[None],
        )

    return local


def unfold_all(values, S, DL, rows):
    _, c = values.shape
    f = DL // rows
    if f <= 1:
        return values
    return values.reshape(S, f, rows, c).transpose(0, 2, 1, 3).reshape(S * rows, f * c)


def fold_all(values, S, DL):
    n, c = values.shape
    f = S * DL // n
    if f <= 1:
        return values
    return values.reshape(S, n // S, f, c // f).transpose(0, 2, 1, 3).reshape(S * DL, c // f)


def solution(mesh):
    tokens = P((REP, SHD), None)
    rows, cols = P(SHD, None), P(None, SHD)
    placed = (
        tokens,
        P((REP, SHD)),
        tokens,
        P(SHD),
        rows,
        rows,
        P(SHD),
        cols,
        rows,
        P(SHD),
        rows,
        rows,
        rows,
        cols,
        P(None, SHD, None),
        P(None, SHD, None),
        P(None, None, SHD),
        tokens,
    )
    outs = (tokens, tokens) + placed[3:17]
    body = make_local(mesh.shape[REP], mesh.shape[SHD])

    return jax.shard_map(
        body,
        mesh=mesh,
        in_specs=placed,
        out_specs=outs,
        check_vma=False,
    )
```
